32 devices in a mesh: dp: 16 (over z, y, core), tensor: 2 (over x).
Axes of the slice: x: 2, y: 2, z: 4, core: 2. Of those that a mesh axis runs over, the one named last changes fastest.
Arguments:
- tokens: bfloat16 [4096, 2048], P(('dp', 'tensor')), may hold values from -6 to 6
- frag_lengths: int32 [128], P('dp'), may hold values from 0 to 256, as said below
- attn_gain: float32 [2048], replicated, may hold values from 0.1 to 1.9
- w_query: bfloat16 [2048, 2048], P(None, 'tensor'), may hold values from -0.125 to 0.125
- w_key: bfloat16 [2048, 256], P(None, 'tensor'), may hold values from -0.125 to 0.125
- w_value: bfloat16 [2048, 256], P(None, 'tensor'), may hold values from -0.125 to 0.125
- w_out: bfloat16 [2048, 2048], P('tensor'), may hold values from -0.375 to 0.375
- mlp_gain: float32 [2048], replicated, may hold values from 0.1 to 1.9
- w_gate: bfloat16 [2048, 5632], P(None, 'tensor'), may hold values from -0.125 to 0.125
- w_up: bfloat16 [2048, 5632], P(None, 'tensor'), may hold values from -0.125 to 0.125
- w_down: bfloat16 [5632, 2048], P('tensor'), may hold values from -0.109375 to 0.109375
- out_cotangent: bfloat16 [4096, 2048], P(('dp', 'tensor')), may hold values from -6 to 6
Outputs:
- layer_out: bfloat16 [4096, 2048], P(('dp', 'tensor'))
- token_grad: bfloat16 [4096, 2048], P(('dp', 'tensor'))
- g_attn_gain: float32 [2048], P(('dp', 'tensor'))
- g_query: float32 [2048, 2048], P('dp', 'tensor')
- g_key: float32 [2048, 256], P('dp', 'tensor')
- g_value: float32 [2048, 256], P('dp', 'tensor')
- g_out: float32 [2048, 2048], P('tensor', 'dp')
- g_mlp_gain: float32 [2048], P(('dp', 'tensor'))
- g_gate: float32 [2048, 5632], P('dp', 'tensor')
- g_up: float32 [2048, 5632], P('dp', 'tensor')
- g_down: float32 [5632, 2048], P('tensor', 'dp')
The draws below stay inside these ranges and needn't reach their ends.
Inputs may be any that keep to these rules, and one draw needn't show every extreme that they name: `frag_lengths`: each index of dp holds the 8 lengths of its own packed batch; their sum is at most 256. In every draw some batch holds a single fragment of exactly 256 slots.
All inputs are finite; a program needn't handle non-finite values.
Results may differ from the reference program's by a relative error of at most 0.014.
Values may be sent and summed in bfloat16 or wider, within the bound.
A program may use at most 320 MiB of HBM per device.

```python
import math
import jax
import jax.numpy as jnp
from jax import lax

D = 2048
HEADS = 32
KV = 4
HD = 64
FF = 5632
NFRAG = 8
PACK = 256
TOKENS = 4096
N_DP = 16


def draw_frag_lengths(key, part):
    chat_key = jax.random.fold_in(key, 11)
    whole_key = jax.random.fold_in(key, 12)
    pick_key = jax.random.fold_in(key, 13)
    chat = jax.random.randint(chat_key, (N_DP, NFRAG), 1, PACK // NFRAG + 1, dtype=jnp.int32)
    whole_doc = jax.random.randint(whole_key, (N_DP,), 0, 4, dtype=jnp.int32) == 0
    forced = jax.random.randint(pick_key, (), 0, N_DP, dtype=jnp.int32)
    whole_doc = whole_doc | (jnp.arange(N_DP, dtype=jnp.int32) == forced)
    slot_ids = jnp.arange(NFRAG, dtype=jnp.int32)
    single = jnp.where(slot_ids == 0, PACK, 0).astype(jnp.int32)
    result = jnp.where(whole_doc[:, None], single[None, :], chat)
    return result.reshape(N_DP * NFRAG).astype(jnp.int32)


def spiked(array, own_key, source, target, parts, factor):
    owner, partner = [(jnp.arange(array.shape[axis_at]) // (array.shape[axis_at] // parts)).reshape([-1 if axis == axis_at else 1 for axis in range(array.ndim)]) for axis_at in (source, target)]
    chosen = jax.random.permutation(own_key, parts)[partner]
    strong = (owner == chosen) | (owner == (partner + parts // 2) % parts)
    return jnp.where(strong, factor * array, array)


def shard_levels(stream_key, extent, split, low, largest):
    def one(axis_at, blocks):
        heights = jax.random.uniform(jax.random.fold_in(jax.random.fold_in(stream_key, 6), axis_at), (blocks,), jnp.float32, low / len(split), largest / len(split))
        return jnp.repeat(jnp.exp(heights), extent[axis_at] // blocks).reshape((-1,) + (1,) * (len(extent) - axis_at - 1))

    level = one(*split[0])
    for cut in split[1:]:
        level = level * one(*cut)
    return level


def scatter_about(key, shape, scale, bound, cuts=(), kind=jnp.bfloat16):
    factor_of = shard_levels(key, shape, cuts, -0.22, 0.18) if cuts else 1.0
    drawn = jax.random.normal(key, shape, jnp.float32) * scale * factor_of
    return jnp.minimum(jnp.maximum(drawn, -bound), bound).astype(kind)


def bell_draw_with(stream_key, dims, spread, most, shards, heavy, held_as=jnp.bfloat16):
    values = spread * jax.random.normal(stream_key, dims, jnp.float32)
    if shards:
        values = values * shard_levels(stream_key, dims, shards, -0.22, 0.18)
    return jnp.clip(spiked(values, jax.random.fold_in(stream_key, 3), *heavy), -most, most).astype(held_as)


def setup_inputs(seed: int = 0) -> dict:
    key_list = jax.random.split(jax.random.key(seed), 13)
    tokens = bell_draw_with(key_list[0], (TOKENS, D), 1.0, 6.0, ((0, 32),), (0, 1, 32, 2.75))
    frag_lengths = draw_frag_lengths(jax.random.fold_in(key_list[12], 71), 0)
    attn_gain = jnp.clip(1.0 + 0.18 * jax.random.normal(key_list[2], (D,), jnp.float32), 0.1, 1.9)
    w_query = scatter_about(key_list[3], (D, HEADS * HD), D ** -0.5, 0.125, ((1, 2),))
    w_key = scatter_about(key_list[4], (D, KV * HD), D ** -0.5, 0.125, ((1, 2),))
    w_value = scatter_about(key_list[5], (D, KV * HD), D ** -0.5, 0.125, ((1, 2),))
    w_out = scatter_about(key_list[6], (HEADS * HD, D), (HEADS * HD // 8) ** -0.5, 0.375, ((0, 2),))
    mlp_gain = jnp.clip(1.0 + 0.18 * jax.random.normal(key_list[7], (D,), jnp.float32), 0.1, 1.9)
    w_gate = scatter_about(key_list[8], (D, FF), D ** -0.5, 0.125, ((1, 2),))
    w_up = scatter_about(key_list[9], (D, FF), D ** -0.5, 0.125, ((1, 2),))
    w_down = scatter_about(key_list[10], (FF, D), (FF // 2) ** -0.5, 0.109375, ((0, 2),))
    out_cotangent = bell_draw_with(key_list[11], (TOKENS, D), 1.0, 6.0, ((0, 32),), (0, 1, 32, 2.75))
    return dict(tokens=tokens, frag_lengths=frag_lengths, attn_gain=attn_gain, w_query=w_query, w_key=w_key, w_value=w_value, w_out=w_out, mlp_gain=mlp_gain, w_gate=w_gate, w_up=w_up, w_down=w_down, out_cotangent=out_cotangent)


highest = lax.Precision.HIGHEST
norm_eps = 1e-05
masked_score = -1e+30

@jax.custom_vjp
def low(v):
    return lax.optimization_barrier(v.astype(jnp.bfloat16)).astype(jnp.float32)

@jax.custom_vjp
def low_back(v):
    return v

def low_keep(v):
    return (low(v), None)

def low_pass(kept, grad):
    return (grad,)

def back_keep(v):
    return (v, None)

def back_low(kept, grad):
    return (low(grad),)
low.defvjp(low_keep, low_pass)
low_back.defvjp(back_keep, back_low)

def packing(lengths, places):
    frag_count = lengths.shape[0]
    ends_at = jnp.cumsum(lengths, dtype=jnp.int32)
    filled = ends_at[frag_count - 1]
    segment = lax.optimization_barrier(jnp.sum((places[:, None] >= ends_at[None, :]).astype(jnp.int32), axis=1)).astype(jnp.int32)
    starts = jnp.concatenate([ends_at - lengths, filled[None]]).astype(jnp.int32)
    labels = jnp.arange(frag_count + 1, dtype=jnp.int32)
    offset = lax.optimization_barrier(jnp.sum(jnp.where(segment[:, None] == labels[None, :], starts[None, :], 0), axis=1)).astype(jnp.int32)
    return (segment, places - offset, (places < filled).astype(jnp.float32))

def rotary_tables(position, head_dim):
    halves = jnp.arange(head_dim // 2, dtype=jnp.float32)
    inverse = jnp.exp(halves * (-2.0 * math.log(10000.0) / head_dim))
    angles = position.astype(jnp.float32)[:, None] * inverse[None, :]
    return (jnp.cos(angles), jnp.sin(angles))

def rotate(values, cosine, sine):
    half_dim = values.shape[-1] // 2
    first_half = values[..., :half_dim]
    second_half = values[..., half_dim:]
    cos_rows = cosine[:, None, :]
    sin_rows = sine[:, None, :]
    return jnp.concatenate([first_half * cos_rows - second_half * sin_rows, second_half * cos_rows + first_half * sin_rows], axis=-1)

def rms_norm(values):
    return values * lax.rsqrt(lax.optimization_barrier(jnp.mean(values * values, axis=-1, keepdims=True)) + norm_eps)

def layer_forward(params, tokens_in, segment, position, valid):
    attn_gain, w_query, w_key, w_value, w_out, mlp_gain, w_gate, w_up, w_down = params
    row_count = tokens_in.shape[0]
    masked = tokens_in * valid[:, None]
    normed_one = low(rms_norm(masked) * attn_gain)
    query_lin = low_back(jnp.dot(normed_one, w_query, precision=highest))
    key_lin = low_back(jnp.dot(normed_one, w_key, precision=highest))
    value_low = low(low_back(jnp.dot(normed_one, w_value, precision=highest))).reshape(row_count, KV, HD)
    cosine, sine = rotary_tables(position, HD)
    query_rot = low(rotate(query_lin.reshape(row_count, HEADS, HD), cosine, sine))
    key_rot = low(rotate(key_lin.reshape(row_count, KV, HD), cosine, sine))
    grouped = query_rot.reshape(row_count, KV, HEADS // KV, HD)
    scores = low_back(jnp.einsum('ikgd,jkd->kgij', grouped, key_rot, precision=highest) * HD ** (-0.5))
    places = jnp.arange(row_count, dtype=jnp.int32)
    allowed = (segment[:, None] == segment[None, :]) & (places[None, :] <= places[:, None])
    scores = jnp.where(allowed[None, None], scores, masked_score)
    probs = low(jax.nn.softmax(scores, axis=-1))
    attended = jnp.einsum('kgij,jkd->ikgd', probs, value_low, precision=highest).reshape(row_count, HEADS * HD)
    attended = low(low_back(attended))
    branch = low_back(jnp.dot(attended, w_out, precision=highest))
    middle = masked + branch
    normed_two = low(rms_norm(middle) * mlp_gain)
    gate = low_back(jnp.dot(normed_two, w_gate, precision=highest))
    up_proj = low_back(jnp.dot(normed_two, w_up, precision=highest))
    act = low(jax.nn.silu(gate) * up_proj)
    mlp = low_back(jnp.dot(act, w_down, precision=highest))
    return middle + mlp

def add_pair(first, second):
    return first + second

def reference(tokens, frag_lengths, attn_gain, w_query, w_key, w_value, w_out, mlp_gain, w_gate, w_up, w_down, out_cotangent):
    params = tuple((weight.astype(jnp.float32) for weight in (attn_gain, w_query, w_key, w_value, w_out, mlp_gain, w_gate, w_up, w_down)))
    grouped_tokens = tokens.astype(jnp.float32).reshape(N_DP, PACK, D)
    grouped_cot = out_cotangent.astype(jnp.float32).reshape(N_DP, PACK, D)
    grouped_len = frag_lengths.reshape(N_DP, NFRAG)
    places = jnp.arange(PACK, dtype=jnp.int32)

    def one_group(totals, inputs):
        group_tokens, group_cot, group_len = inputs
        segment, position, valid = packing(group_len, places)

        def forward(params_in, tokens_in):
            return layer_forward(params_in, tokens_in, segment, position, valid)
        output, pullback = jax.vjp(forward, params, group_tokens)
        param_grads, input_grads = pullback(group_cot * valid[:, None])
        totals = jax.tree.map(add_pair, totals, param_grads)
        return (totals, (output.astype(jnp.bfloat16), input_grads.astype(jnp.bfloat16)))
    zero_grads = tuple((jnp.zeros(weight.shape, jnp.float32) for weight in params))
    totals, (outputs, input_grads) = lax.scan(one_group, zero_grads, (grouped_tokens, grouped_cot, grouped_len))
    return (outputs.reshape(N_DP * PACK, D), input_grads.reshape(N_DP * PACK, D), totals[0], totals[1], totals[2], totals[3], totals[4], totals[5], totals[6], totals[7], totals[8])
```

```python
import math

import jax
import jax.numpy as jnp
from jax import lax
from jax.sharding import PartitionSpec as P

HD = 64


norm_eps = 1e-05
masked_score = -1e30


def packing(lengths, places):
    frag_count = lengths.shape[0]
    ends_at = jnp.cumsum(lengths, dtype=jnp.int32)
    filled = ends_at[frag_count - 1]
    segment = jnp.sum((places[:, None] >= ends_at[None, :]).astype(jnp.int32), axis=1)
    starts = jnp.concatenate([ends_at - lengths, filled[None]])
    labels = jnp.arange(frag_count + 1, dtype=jnp.int32)
    offset = jnp.sum(jnp.where(segment[:, None] == labels[None, :], starts[None, :], 0), axis=1)
    return (segment, places - offset, (places < filled).astype(jnp.float32))


def rotary_tables(position, head_dim):
    halves = jnp.arange(head_dim // 2, dtype=jnp.float32)
    inverse = jnp.exp(halves * (-2.0 * math.log(10000.0) / head_dim))
    angles = position.astype(jnp.float32)[:, None] * inverse[None, :]
    return (jnp.cos(angles), jnp.sin(angles))


def rotate(values, cosine, sine):
    half_dim = values.shape[-1] // 2
    first_half = values[..., :half_dim]
    second_half = values[..., half_dim:]
    cos_rows = cosine[:, None, :]
    sin_rows = sine[:, None, :]
    return jnp.concatenate(
        [
            first_half * cos_rows - second_half * sin_rows,
            second_half * cos_rows + first_half * sin_rows,
        ],
        axis=-1,
    )


def unrotate(grads, cosine, sine):
    half_dim = grads.shape[-1] // 2
    first_half = grads[..., :half_dim]
    second_half = grads[..., half_dim:]
    cos_rows = cosine[:, None, :]
    sin_rows = sine[:, None, :]
    return jnp.concatenate(
        [
            first_half * cos_rows + second_half * sin_rows,
            second_half * cos_rows - first_half * sin_rows,
        ],
        axis=-1,
    )


def inner_rows(left, right):
    return lax.dot_general(
        left, right, (((0,), (0,)), ((), ())), preferred_element_type=jnp.float32
    )


def against(left, right):
    return lax.dot_general(
        left, right, (((1,), (1,)), ((), ())), preferred_element_type=jnp.float32
    )


def block_mask(segment, start, block_rows):
    row_places = start + jnp.arange(block_rows, dtype=jnp.int32)
    col_places = jnp.arange(segment.shape[0], dtype=jnp.int32)
    return (segment[:, None] == segment[None, :]) & (col_places[None, :] <= row_places[:, None])


def norm_back(grad_normed, normed, scale, gain):
    gain_part = jnp.sum(grad_normed * normed, axis=0)
    scaled = grad_normed * gain
    return (scale * (scaled - normed * jnp.mean(scaled * normed, axis=1, keepdims=True)), gain_part)


def swap(value, axis, bit):
    size = lax.axis_size(axis)
    return lax.ppermute(value, axis, [(i, i ^ bit) for i in range(size)])


def join_rows(own, other, rank):
    first = jnp.where(rank == 0, own, other)
    second = jnp.where(rank == 0, other, own)
    return jnp.concatenate([first, second], axis=0)


def full_rows(own, rank):
    return join_rows(own, swap(own, "tensor", 1), rank)


def own_rows(partial, rank, rows):
    away = lax.dynamic_slice_in_dim(partial, (1 - rank) * rows, rows).astype(jnp.bfloat16)
    kept = lax.dynamic_slice_in_dim(partial, rank * rows, rows)
    return kept + swap(away, "tensor", 1).astype(jnp.float32)


def gather_four(rows):
    beside = swap(rows, "dp", 1)
    across = swap(rows, "dp", 2)
    return jnp.concatenate([rows, beside, across, swap(across, "dp", 1)], axis=0)


def gather_features(rows):
    tokens, width = rows.shape
    count = lax.axis_size("dp")
    me = lax.axis_index("dp")
    high, low = me // 4, me % 4
    block = width // count
    turned = rows.T.reshape(count // 4, 4, block, tokens)
    order = [jnp.bitwise_xor(high, k) for k in range(count // 4)]
    mine = lambda k: lax.dynamic_index_in_dim(turned, jnp.bitwise_xor(low, k), 1, keepdims=False)
    ours, beside, across, corner = mine(0), mine(1), mine(2), mine(3)
    from_across = swap(jnp.stack([across, corner]), "dp", 2)
    from_beside = swap(jnp.stack([beside, from_across[1]]), "dp", 1)
    every = jnp.concatenate([ours, from_beside[0], from_across[0], from_beside[1]], axis=-1)
    return jnp.stack([lax.dynamic_index_in_dim(every, at, 0, keepdims=False) for at in order])


def reduce_high(features, rows):
    count, block, depth = features.shape
    width = rows.shape[1]

    def product(which):
        left = features[which].reshape(-1, depth)
        out = jnp.dot(left, rows, preferred_element_type=jnp.float32)
        return out.reshape(-1, block, width)

    received = {}
    bit = 1
    while bit < count:
        sent = [k for k in range(count) if k & bit and not k & (bit - 1)]
        out = product(jnp.array(sent))
        for earlier in received.values():
            out = out + jnp.stack([earlier[k] for k in sent]).astype(jnp.float32)
        came = swap(out.astype(jnp.bfloat16), "dp", 4 * bit)
        received[bit] = {k ^ bit: came[i] for i, k in enumerate(sent)}
        bit *= 2
    out = product(jnp.array([0]))[0]
    for earlier in received.values():
        out = out + earlier[0].astype(jnp.float32)
    return out


def sum_all(value):
    bit = 1
    while bit < lax.axis_size("dp"):
        value = value + swap(value, "dp", bit)
        bit *= 2
    return value + swap(value, "tensor", 1)


def on_device(
    tokens,
    frag_lengths,
    attn_gain,
    w_query,
    w_key,
    w_value,
    w_out,
    mlp_gain,
    w_gate,
    w_up,
    w_down,
    out_cotangent,
):
    tok_rows, model_width = tokens.shape
    tensor_size = lax.axis_size("tensor")
    pack_rows = tok_rows * tensor_size
    head_dim = HD
    query_width = w_query.shape[1]
    local_heads = query_width // head_dim
    local_kv = w_key.shape[1] // head_dim
    kv_width = w_key.shape[1]
    groups = local_heads // local_kv
    score_scale = head_dim ** (-0.5)
    block_rows = min(512, pack_rows)
    block_count = pack_rows // block_rows
    places = jnp.arange(pack_rows, dtype=jnp.int32)
    segment, position, valid = packing(frag_lengths, places)
    rank = lax.axis_index("tensor")
    gain_rows = model_width // (tensor_size * lax.axis_size("dp"))
    first_row = rank * tok_rows
    own_valid = lax.dynamic_slice_in_dim(valid, first_row, tok_rows)
    cosine, sine = rotary_tables(position, head_dim)
    masked = tokens.astype(jnp.float32) * own_valid[:, None]
    first_scale = lax.rsqrt(jnp.mean(masked * masked, axis=1, keepdims=True) + norm_eps)
    first_norm = masked * first_scale
    full_one = full_rows((first_norm * attn_gain).astype(jnp.bfloat16), rank)
    query_lin = jnp.dot(full_one, w_query, preferred_element_type=jnp.float32)
    key_lin = jnp.dot(full_one, w_key, preferred_element_type=jnp.float32)
    value_low = (
        jnp.dot(full_one, w_value, preferred_element_type=jnp.float32)
        .astype(jnp.bfloat16)
        .reshape(pack_rows, local_kv, head_dim)
    )
    query_rot = rotate(query_lin.reshape(pack_rows, local_heads, head_dim), cosine, sine).astype(
        jnp.bfloat16
    )
    key_rot = rotate(key_lin.reshape(pack_rows, local_kv, head_dim), cosine, sine).astype(
        jnp.bfloat16
    )

    def block_scores(index):
        start = index * block_rows
        query_blk = query_rot.reshape(block_rows, local_kv, groups, head_dim)
        allowed = block_mask(segment, start, block_rows)
        scores = (
            jnp.einsum("ikgd,jkd->kgij", query_blk, key_rot, preferred_element_type=jnp.float32)
            * score_scale
        )
        return (start, query_blk, jnp.where(allowed[None, None], scores, masked_score))

    def attend_block(index):
        start, query_blk, scores = block_scores(index)
        top_score = jnp.max(scores, axis=-1, keepdims=True)
        expo = jnp.exp(scores - top_score)
        totals = jnp.sum(expo, axis=-1, keepdims=True)
        probs_low = (expo / totals).astype(jnp.bfloat16)
        out_blk = jnp.einsum(
            "kgij,jkd->ikgd", probs_low, value_low, preferred_element_type=jnp.float32
        )
        return (
            out_blk.reshape(block_rows, query_width).astype(jnp.bfloat16),
            (top_score + jnp.log(totals))[..., 0],
        )

    attended_blocks, log_totals = lax.map(attend_block, jnp.arange(block_count, dtype=jnp.int32))
    attended = attended_blocks.reshape(pack_rows, query_width)
    branch = own_rows(jnp.dot(attended, w_out, preferred_element_type=jnp.float32), rank, tok_rows)
    middle = masked + branch
    second_scale = lax.rsqrt(jnp.mean(middle * middle, axis=1, keepdims=True) + norm_eps)
    second_norm = middle * second_scale
    full_two = full_rows((second_norm * mlp_gain).astype(jnp.bfloat16), rank)
    gate = jnp.dot(full_two, w_gate, preferred_element_type=jnp.float32)
    up_proj = jnp.dot(full_two, w_up, preferred_element_type=jnp.float32)
    sigmoid_gate = jax.nn.sigmoid(gate)
    silu_gate = gate * sigmoid_gate
    act = (silu_gate * up_proj).astype(jnp.bfloat16)
    mlp = own_rows(jnp.dot(act, w_down, preferred_element_type=jnp.float32), rank, tok_rows)
    layer_out = (middle + mlp).astype(jnp.bfloat16)
    d_out = out_cotangent.astype(jnp.float32) * own_valid[:, None]
    full_dy = full_rows(d_out.astype(jnp.bfloat16), rank)
    d_act = against(full_dy, w_down)
    d_gate = (d_act * up_proj * sigmoid_gate * (1.0 + gate * (1.0 - sigmoid_gate))).astype(
        jnp.bfloat16
    )
    d_up = (d_act * silu_gate).astype(jnp.bfloat16)
    down_rows = reduce_high(gather_features(full_dy), gather_four(act))
    features_two = gather_features(full_two)
    g_gate = reduce_high(features_two, gather_four(d_gate))
    g_up = reduce_high(features_two, gather_four(d_up))
    d_normed_two = own_rows(against(d_gate, w_gate) + against(d_up, w_up), rank, tok_rows)
    mlp_norm_back, mlp_gain_part = norm_back(d_normed_two, second_norm, second_scale, mlp_gain)
    d_middle = d_out + mlp_norm_back
    full_db = full_rows(d_middle.astype(jnp.bfloat16), rank)
    d_attended = against(full_db, w_out).astype(jnp.bfloat16)

    def back_block(carry, inputs):
        key_acc, value_acc = carry
        index, log_total = inputs
        start, query_blk, scores = block_scores(index)
        probs = jnp.exp(scores - log_total[..., None])
        d_out_blk = d_attended.reshape(block_rows, local_kv, groups, head_dim)
        d_probs = jnp.einsum(
            "ikgd,jkd->kgij", d_out_blk, value_low, preferred_element_type=jnp.float32
        )
        d_scores = (probs * (d_probs - jnp.sum(probs * d_probs, axis=-1, keepdims=True))).astype(
            jnp.bfloat16
        )
        d_query = (
            jnp.einsum("kgij,jkd->ikgd", d_scores, key_rot, preferred_element_type=jnp.float32)
            * score_scale
        )
        key_acc = (
            key_acc
            + jnp.einsum("kgij,ikgd->jkd", d_scores, query_blk, preferred_element_type=jnp.float32)
            * score_scale
        )
        value_acc = value_acc + jnp.einsum(
            "kgij,ikgd->jkd",
            probs.astype(jnp.bfloat16),
            d_out_blk,
            preferred_element_type=jnp.float32,
        )
        return ((key_acc, value_acc), d_query.reshape(block_rows, local_heads, head_dim))

    zero_kv = jnp.zeros((pack_rows, local_kv, head_dim), jnp.float32)
    (d_key_rot, d_value_sum), d_query_blocks = lax.scan(
        back_block, (zero_kv, zero_kv), (jnp.arange(block_count, dtype=jnp.int32), log_totals)
    )
    d_query_rot = d_query_blocks.reshape(pack_rows, local_heads, head_dim)
    d_query = (
        unrotate(d_query_rot, cosine, sine).reshape(pack_rows, query_width).astype(jnp.bfloat16)
    )
    d_key = unrotate(d_key_rot, cosine, sine).reshape(pack_rows, kv_width).astype(jnp.bfloat16)
    d_value = d_value_sum.reshape(pack_rows, kv_width).astype(jnp.bfloat16)
    out_rows = reduce_high(gather_features(full_db), gather_four(attended))
    d_all = gather_four(jnp.concatenate([d_query, d_key, d_value], axis=1))
    g_all = reduce_high(gather_features(full_one), d_all)
    g_query, g_key, g_value = jnp.split(g_all, [query_width, query_width + kv_width], axis=1)
    d_normed_one = own_rows(
        against(d_query, w_query) + against(d_key, w_key) + against(d_value, w_value),
        rank,
        tok_rows,
    )
    attn_norm_back, attn_gain_part = norm_back(d_normed_one, first_norm, first_scale, attn_gain)
    token_grad = ((d_middle + attn_norm_back) * own_valid[:, None]).astype(jnp.bfloat16)
    place = (lax.axis_index("dp") * tensor_size + rank) * gain_rows
    g_mlp_gain = lax.dynamic_slice_in_dim(sum_all(mlp_gain_part), place, gain_rows)
    g_attn_gain = lax.dynamic_slice_in_dim(sum_all(attn_gain_part), place, gain_rows)
    return (
        layer_out,
        token_grad,
        g_attn_gain,
        g_query,
        g_key,
        g_value,
        out_rows.T,
        g_mlp_gain,
        g_gate,
        g_up,
        down_rows.T,
    )


def solution(mesh):
    placed = (
        P(("dp", "tensor"), None),
        P("dp"),
        P(),
        P(None, "tensor"),
        P(None, "tensor"),
        P(None, "tensor"),
        P("tensor", None),
        P(),
        P(None, "tensor"),
        P(None, "tensor"),
        P("tensor", None),
        P(("dp", "tensor"), None),
    )
    return jax.shard_map(
        on_device,
        mesh=mesh,
        in_specs=placed,
        out_specs=(
            P(("dp", "tensor"), None),
            P(("dp", "tensor"), None),
            P(("dp", "tensor")),
            P("dp", "tensor"),
            P("dp", "tensor"),
            P("dp", "tensor"),
            P("tensor", "dp"),
            P(("dp", "tensor")),
            P("dp", "tensor"),
            P("dp", "tensor"),
            P("tensor", "dp"),
        ),
        check_vma=False,
    )
```

```python
import functools
import math

import jax
import jax.numpy as jnp
from jax import lax
from jax.experimental import pallas as pl
from jax.experimental.pallas import tpu as pltpu
from jax.sharding import PartitionSpec as P

MESH = pl.DeviceIdType.MESH
TILE = 256

HD = 64


norm_eps = 1e-05
masked_score = -1e30


def packing(lengths, places):
    frag_count = lengths.shape[0]
    ends_at = jnp.cumsum(lengths, dtype=jnp.int32)
    filled = ends_at[frag_count - 1]
    segment = jnp.sum((places[:, None] >= ends_at[None, :]).astype(jnp.int32), axis=1)
    starts = jnp.concatenate([ends_at - lengths, filled[None]])
    labels = jnp.arange(frag_count + 1, dtype=jnp.int32)
    offset = jnp.sum(jnp.where(segment[:, None] == labels[None, :], starts[None, :], 0), axis=1)
    return (segment, places - offset, (places < filled).astype(jnp.float32))


def rotary_tables(position, head_dim):
    halves = jnp.arange(head_dim // 2, dtype=jnp.float32)
    inverse = jnp.exp(halves * (-2.0 * math.log(10000.0) / head_dim))
    angles = position.astype(jnp.float32)[:, None] * inverse[None, :]
    return (jnp.cos(angles), jnp.sin(angles))


def rotate(values, cosine, sine):
    half_dim = values.shape[-1] // 2
    first_half = values[..., :half_dim]
    second_half = values[..., half_dim:]
    cos_rows = cosine[:, None, :]
    sin_rows = sine[:, None, :]
    return jnp.concatenate(
        [
            first_half * cos_rows - second_half * sin_rows,
            second_half * cos_rows + first_half * sin_rows,
        ],
        axis=-1,
    )


def unrotate(grads, cosine, sine):
    half_dim = grads.shape[-1] // 2
    first_half = grads[..., :half_dim]
    second_half = grads[..., half_dim:]
    cos_rows = cosine[:, None, :]
    sin_rows = sine[:, None, :]
    return jnp.concatenate(
        [
            first_half * cos_rows + second_half * sin_rows,
            second_half * cos_rows - first_half * sin_rows,
        ],
        axis=-1,
    )


def inner_rows(left, right):
    return lax.dot_general(
        left, right, (((0,), (0,)), ((), ())), preferred_element_type=jnp.float32
    )


def against(left, right):
    return lax.dot_general(
        left, right, (((1,), (1,)), ((), ())), preferred_element_type=jnp.float32
    )


def block_mask(segment, start, block_rows):
    row_places = start + jnp.arange(block_rows, dtype=jnp.int32)
    col_places = jnp.arange(segment.shape[0], dtype=jnp.int32)
    return (segment[:, None] == segment[None, :]) & (col_places[None, :] <= row_places[:, None])


def norm_back(grad_normed, normed, scale, gain):
    gain_part = jnp.sum(grad_normed * normed, axis=0)
    scaled = grad_normed * gain
    return (scale * (scaled - normed * jnp.mean(scaled * normed, axis=1, keepdims=True)), gain_part)


def swap(value, axis, bit):
    size = lax.axis_size(axis)
    return lax.ppermute(value, axis, [(i, i ^ bit) for i in range(size)])


def join_rows(own, other, rank):
    first = jnp.where(rank == 0, own, other)
    second = jnp.where(rank == 0, other, own)
    return jnp.concatenate([first, second], axis=0)


def full_rows(own, rank):
    return join_rows(own, swap(own, "tensor", 1), rank)


def own_rows(partial, rank, rows):
    away = lax.dynamic_slice_in_dim(partial, (1 - rank) * rows, rows).astype(jnp.bfloat16)
    kept = lax.dynamic_slice_in_dim(partial, rank * rows, rows)
    return kept + swap(away, "tensor", 1).astype(jnp.float32)


def spread_features(rows):
    tokens, width = rows.shape
    count = lax.axis_size("dp") // 4
    bits = count.bit_length() - 1
    turned = rows.T.reshape((2,) * bits + (4, width // (4 * count), tokens))
    return turned.transpose((bits,) + tuple(range(bits))[::-1] + (bits + 1, bits + 2)).reshape(
        4, width // 4, tokens
    )


def split_width(width, most):
    tiles = width // TILE
    parts = -(-width // most)
    sizes = [tiles // parts + (1 if i < tiles % parts else 0) for i in range(parts)]
    starts = [sum(sizes[:i]) * TILE for i in range(parts)]
    return [(start, size * TILE) for start, size in zip(starts, sizes)]


def grads_kernel(plan, bits, tokens, arrays, features, *refs):
    refs = list(refs)
    take = lambda n: [refs.pop(0) for _ in range(n)]
    own = take(arrays)
    spread = take(features)
    outs = take(max(out for job in plan for out, _, _ in job[4]) + 1)
    every = take(arrays)
    left = take(features)
    sent = take(arrays)
    came = take(arrays)
    sent_late = take(arrays)
    came_late = take(arrays)
    total = take(arrays)
    local_sem, feat_send, feat_recv, near_send, near_recv, far_send, far_recv, out_sem = refs
    late = bits - 1
    me = lax.axis_index("dp")
    low, high = lax.rem(me, 4), lax.div(me, 4)
    bit = [lax.rem(lax.div(high, 2**s), 2) for s in range(bits)]
    rows = left[0].shape[0]
    half, quarter = rows // 2, rows // 4

    def flip(value, by):
        for step in range(8):
            if by >> step & 1:
                value = value + (1 - 2 * lax.rem(lax.div(value, 2**step), 2)) * 2**step
        return value

    partners = [1, 2, 3] + [4 << s for s in range(bits)]
    barrier = pltpu.get_barrier_semaphore()
    for by in partners:
        pl.semaphore_signal(barrier, inc=1, device_id={"dp": flip(me, by)}, device_id_type=MESH)
    pl.semaphore_wait(barrier, len(partners))

    def remote(src, dst, send, recv, by):
        return pltpu.make_async_remote_copy(
            src_ref=src, dst_ref=dst, send_sem=send, recv_sem=recv, device_id={"dp": flip(me, by)}, device_id_type=MESH
        )

    def slot(ref, j, start, width):
        return ref.at[pl.ds(j * tokens, tokens), pl.ds(start, width)]

    def feature_local(f):
        return pltpu.make_async_copy(spread[f].at[low], left[f].at[:, pl.ds(0, tokens)], local_sem.at[len(plan) + f])

    def feature_copy(f, j):
        return remote(
            spread[f].at[flip(low, j)],
            left[f].at[:, pl.ds(j * tokens, tokens)],
            feat_send.at[f, j],
            feat_recv.at[f, j],
            j,
        )

    def job_local(t):
        array, _, start, width, _ = plan[t]
        return pltpu.make_async_copy(own[array].at[:, pl.ds(start, width)], slot(every[array], 0, start, width), local_sem.at[t])

    def near(t, j):
        array, _, start, width, _ = plan[t]
        src = slot(every[array], 2, start, width) if j == 3 else own[array].at[:, pl.ds(start, width)]
        return remote(src, slot(every[array], j, start, width), near_send.at[t, j], near_recv.at[t, j], 2 if j == 2 else 1)

    def far(t, s):
        array, _, start, width, _ = plan[t]
        if s == 0:
            src, dst = sent[array], came[array]
            first, size = 0, half
        else:
            src, dst = sent_late[array], came_late[array]
            first, size = quarter * 2 - (quarter * 2 >> (s - 1)), quarter >> (s - 1)
        at = (pl.ds(first, size), pl.ds(start, width))
        return remote(src.at[at], dst.at[at], far_send.at[t, s], far_recv.at[t, s], 4 << s)

    def outputs(t):
        array, _, start, width, pieces = plan[t]
        size = quarter >> (bits - 2)
        copies = []
        done = 0
        for i, (out, first, columns) in enumerate(pieces):
            copies.append(
                pltpu.make_async_copy(
                    total[array].at[pl.ds(final_row(), size), pl.ds(start + done, columns)],
                    outs[out].at[:, pl.ds(first, columns)],
                    out_sem.at[t, i],
                )
            )
            done += columns
        return copies

    def final_row():
        row = 0
        for s in range(2, bits):
            row = row + bit[s] * (quarter >> (s - 1))
        return pl.multiple_of(row, quarter >> (bits - 2)) if bits > 2 else 0

    def tiles(t, body):
        _, _, start, width, _ = plan[t]

        @pl.loop(0, width // TILE)
        def _(i):
            body(pl.ds(pl.multiple_of(start + i * TILE, TILE), TILE))

    def dot(f, first, size, array, at):
        return jnp.dot(
            left[f][pl.ds(pl.multiple_of(first, size), size), :], every[array][:, at], preferred_element_type=jnp.float32
        )

    def first_pass(t):
        array, f = plan[t][:2]

        def body(at):
            sent[array][:, at] = dot(f, (1 - bit[0]) * half, half, array, at).astype(jnp.bfloat16)

        tiles(t, body)
        far(t, 0).start()

    def second_pass(t):
        array, f = plan[t][:2]
        far(t, 0).wait_recv()
        base = bit[0] * half

        def body(at):
            away, kept = (1 - bit[1]) * quarter, bit[1] * quarter
            out = dot(f, base + away, quarter, array, at)
            out = out + came[array][pl.ds(pl.multiple_of(away, quarter), quarter), at].astype(jnp.float32)
            sent_late[array][pl.ds(0, quarter), at] = out.astype(jnp.bfloat16)
            out = dot(f, base + kept, quarter, array, at)
            out = out + came[array][pl.ds(pl.multiple_of(kept, quarter), quarter), at].astype(jnp.float32)
            total[array][:, at] = out

        tiles(t, body)
        far(t, 1).start()

    def later_pass(t, s):
        array = plan[t][0]
        far(t, s - 1).wait_recv()
        size = quarter >> (s - 2)
        first = quarter * 2 - (quarter * 2 >> (s - 2))
        mine = 0
        for q in range(2, s):
            mine = mine + bit[q] * (quarter >> (q - 1))

        def body(at):
            piece = size // 2
            away, kept = (1 - bit[s]) * piece, bit[s] * piece
            out = total[array][pl.ds(pl.multiple_of(mine + away, piece), piece), at]
            out = out + came_late[array][pl.ds(pl.multiple_of(first + away, piece), piece), at].astype(jnp.float32)
            sent_late[array][pl.ds(first + size, piece), at] = out.astype(jnp.bfloat16)
            out = total[array][pl.ds(pl.multiple_of(mine + kept, piece), piece), at]
            out = out + came_late[array][pl.ds(pl.multiple_of(first + kept, piece), piece), at].astype(jnp.float32)
            total[array][pl.ds(pl.multiple_of(mine + kept, piece), piece), at] = out

        tiles(t, body)
        far(t, s).start()

    def last_pass(t):
        array = plan[t][0]
        far(t, late).wait_recv()
        size = quarter >> (bits - 2)
        first = quarter * 2 - (quarter * 2 >> (late - 1))

        def body(at):
            row = pl.ds(final_row(), size)
            total[array][row, at] = total[array][row, at] + came_late[array][pl.ds(first, size), at].astype(jnp.float32)

        tiles(t, body)
        for copy in outputs(t):
            copy.start()

    jobs = len(plan)
    feature_first = {}
    for t, job in enumerate(plan):
        feature_first.setdefault(job[1], t)

    def start_features(f):
        feature_local(f).start()
        for j in (2, 3, 1):
            feature_copy(f, j).start()

    def begin(t):
        if feature_first[plan[t][1]] == t:
            start_features(plan[t][1])
        job_local(t).start()
        near(t, 1).start()
        near(t, 2).start()

    begin(0)
    begin(1)
    depth = bits
    for t in range(jobs + depth):
        if t < jobs:
            near(t, 2).wait_recv()
            near(t, 3).start()
            if t + 2 < jobs:
                begin(t + 2)
            f = plan[t][1]
            if feature_first[f] == t:
                feature_local(f).wait()
                for j in (1, 2, 3):
                    feature_copy(f, j).wait_recv()
            job_local(t).wait()
            near(t, 1).wait_recv()
            near(t, 3).wait_recv()
            first_pass(t)
        if 0 <= t - 1 < jobs:
            second_pass(t - 1)
        for s in range(2, bits):
            if 0 <= t - s < jobs:
                later_pass(t - s, s)
        if 0 <= t - bits < jobs:
            last_pass(t - bits)

    for f in feature_first:
        for j in (1, 2, 3):
            feature_copy(f, j).wait_send()
    for t in range(jobs):
        for j in (1, 2, 3):
            near(t, j).wait_send()
        for s in range(bits):
            far(t, s).wait_send()
        for copy in outputs(t):
            copy.wait()


def weight_grads(arrays, spread, plan, out_widths):
    count = lax.axis_size("dp")
    bits = (count // 4).bit_length() - 1
    tokens = arrays[0].shape[0]
    rows = spread[0].shape[1]
    block = rows * 4 // count
    jobs = len(plan)
    most = max(len(job[4]) for job in plan)
    wide = [array.shape[1] for array in arrays]
    any_space = pl.BlockSpec(memory_space=pl.ANY)
    late_rows = rows // 2 - (rows // 2 >> (bits - 1))
    scratch = (
        [pltpu.VMEM((4 * tokens, w), jnp.bfloat16) for w in wide]
        + [pltpu.VMEM((rows, 4 * tokens), jnp.bfloat16) for _ in spread]
        + [pltpu.VMEM((rows // 2, w), jnp.bfloat16) for w in wide] * 2
        + [pltpu.VMEM((late_rows, w), jnp.bfloat16) for w in wide] * 2
        + [pltpu.VMEM((rows // 4, w), jnp.float32) for w in wide]
        + [
            pltpu.SemaphoreType.DMA((jobs + len(spread),)),
            pltpu.SemaphoreType.DMA((len(spread), 4)),
            pltpu.SemaphoreType.DMA((len(spread), 4)),
            pltpu.SemaphoreType.DMA((jobs, 4)),
            pltpu.SemaphoreType.DMA((jobs, 4)),
            pltpu.SemaphoreType.DMA((jobs, bits)),
            pltpu.SemaphoreType.DMA((jobs, bits)),
            pltpu.SemaphoreType.DMA((jobs, most)),
        ]
    )
    return pl.pallas_call(
        functools.partial(grads_kernel, plan, bits, tokens, len(arrays), len(spread)),
        out_shape=[jax.ShapeDtypeStruct((block, w), jnp.float32) for w in out_widths],
        in_specs=[any_space] * (len(arrays) + len(spread)),
        out_specs=[any_space] * len(out_widths),
        scratch_shapes=scratch,
        compiler_params=pltpu.CompilerParams(
            collective_id=0, has_side_effects=True, vmem_limit_bytes=62 * 1024 * 1024
        ),
    )(*arrays, *spread)


def sum_all(value):
    bit = 1
    while bit < lax.axis_size("dp"):
        value = value + swap(value, "dp", bit)
        bit *= 2
    return value + swap(value, "tensor", 1)


def on_device(
    tokens,
    frag_lengths,
    attn_gain,
    w_query,
    w_key,
    w_value,
    w_out,
    mlp_gain,
    w_gate,
    w_up,
    w_down,
    out_cotangent,
):
    tok_rows, model_width = tokens.shape
    tensor_size = lax.axis_size("tensor")
    pack_rows = tok_rows * tensor_size
    head_dim = HD
    query_width = w_query.shape[1]
    local_heads = query_width // head_dim
    local_kv = w_key.shape[1] // head_dim
    kv_width = w_key.shape[1]
    groups = local_heads // local_kv
    score_scale = head_dim ** (-0.5)
    block_rows = min(512, pack_rows)
    block_count = pack_rows // block_rows
    places = jnp.arange(pack_rows, dtype=jnp.int32)
    segment, position, valid = packing(frag_lengths, places)
    rank = lax.axis_index("tensor")
    gain_rows = model_width // (tensor_size * lax.axis_size("dp"))
    first_row = rank * tok_rows
    own_valid = lax.dynamic_slice_in_dim(valid, first_row, tok_rows)
    cosine, sine = rotary_tables(position, head_dim)
    masked = tokens.astype(jnp.float32) * own_valid[:, None]
    first_scale = lax.rsqrt(jnp.mean(masked * masked, axis=1, keepdims=True) + norm_eps)
    first_norm = masked * first_scale
    full_one = full_rows((first_norm * attn_gain).astype(jnp.bfloat16), rank)
    query_lin = jnp.dot(full_one, w_query, preferred_element_type=jnp.float32)
    key_lin = jnp.dot(full_one, w_key, preferred_element_type=jnp.float32)
    value_low = (
        jnp.dot(full_one, w_value, preferred_element_type=jnp.float32)
        .astype(jnp.bfloat16)
        .reshape(pack_rows, local_kv, head_dim)
    )
    query_rot = rotate(query_lin.reshape(pack_rows, local_heads, head_dim), cosine, sine).astype(
        jnp.bfloat16
    )
    key_rot = rotate(key_lin.reshape(pack_rows, local_kv, head_dim), cosine, sine).astype(
        jnp.bfloat16
    )

    def block_scores(index):
        start = index * block_rows
        query_blk = query_rot.reshape(block_rows, local_kv, groups, head_dim)
        allowed = block_mask(segment, start, block_rows)
        scores = (
            jnp.einsum("ikgd,jkd->kgij", query_blk, key_rot, preferred_element_type=jnp.float32)
            * score_scale
        )
        return (start, query_blk, jnp.where(allowed[None, None], scores, masked_score))

    def attend_block(index):
        start, query_blk, scores = block_scores(index)
        top_score = jnp.max(scores, axis=-1, keepdims=True)
        expo = jnp.exp(scores - top_score)
        totals = jnp.sum(expo, axis=-1, keepdims=True)
        probs_low = (expo / totals).astype(jnp.bfloat16)
        out_blk = jnp.einsum(
            "kgij,jkd->ikgd", probs_low, value_low, preferred_element_type=jnp.float32
        )
        return (
            out_blk.reshape(block_rows, query_width).astype(jnp.bfloat16),
            (top_score + jnp.log(totals))[..., 0],
        )

    attended_blocks, log_totals = lax.map(attend_block, jnp.arange(block_count, dtype=jnp.int32))
    attended = attended_blocks.reshape(pack_rows, query_width)
    branch = own_rows(jnp.dot(attended, w_out, preferred_element_type=jnp.float32), rank, tok_rows)
    middle = masked + branch
    second_scale = lax.rsqrt(jnp.mean(middle * middle, axis=1, keepdims=True) + norm_eps)
    second_norm = middle * second_scale
    full_two = full_rows((second_norm * mlp_gain).astype(jnp.bfloat16), rank)
    gate = jnp.dot(full_two, w_gate, preferred_element_type=jnp.float32)
    up_proj = jnp.dot(full_two, w_up, preferred_element_type=jnp.float32)
    sigmoid_gate = jax.nn.sigmoid(gate)
    silu_gate = gate * sigmoid_gate
    act = (silu_gate * up_proj).astype(jnp.bfloat16)
    mlp = own_rows(jnp.dot(act, w_down, preferred_element_type=jnp.float32), rank, tok_rows)
    layer_out = (middle + mlp).astype(jnp.bfloat16)
    d_out = out_cotangent.astype(jnp.float32) * own_valid[:, None]
    full_dy = full_rows(d_out.astype(jnp.bfloat16), rank)
    d_act = against(full_dy, w_down)
    d_gate = (d_act * up_proj * sigmoid_gate * (1.0 + gate * (1.0 - sigmoid_gate))).astype(
        jnp.bfloat16
    )
    d_up = (d_act * silu_gate).astype(jnp.bfloat16)
    d_normed_two = own_rows(against(d_gate, w_gate) + against(d_up, w_up), rank, tok_rows)
    mlp_norm_back, mlp_gain_part = norm_back(d_normed_two, second_norm, second_scale, mlp_gain)
    d_middle = d_out + mlp_norm_back
    full_db = full_rows(d_middle.astype(jnp.bfloat16), rank)
    d_attended = against(full_db, w_out).astype(jnp.bfloat16)

    def back_block(carry, inputs):
        key_acc, value_acc = carry
        index, log_total = inputs
        start, query_blk, scores = block_scores(index)
        probs = jnp.exp(scores - log_total[..., None])
        d_out_blk = d_attended.reshape(block_rows, local_kv, groups, head_dim)
        d_probs = jnp.einsum(
            "ikgd,jkd->kgij", d_out_blk, value_low, preferred_element_type=jnp.float32
        )
        d_scores = (probs * (d_probs - jnp.sum(probs * d_probs, axis=-1, keepdims=True))).astype(
            jnp.bfloat16
        )
        d_query = (
            jnp.einsum("kgij,jkd->ikgd", d_scores, key_rot, preferred_element_type=jnp.float32)
            * score_scale
        )
        key_acc = (
            key_acc
            + jnp.einsum("kgij,ikgd->jkd", d_scores, query_blk, preferred_element_type=jnp.float32)
            * score_scale
        )
        value_acc = value_acc + jnp.einsum(
            "kgij,ikgd->jkd",
            probs.astype(jnp.bfloat16),
            d_out_blk,
            preferred_element_type=jnp.float32,
        )
        return ((key_acc, value_acc), d_query.reshape(block_rows, local_heads, head_dim))

    zero_kv = jnp.zeros((pack_rows, local_kv, head_dim), jnp.float32)
    (d_key_rot, d_value_sum), d_query_blocks = lax.scan(
        back_block, (zero_kv, zero_kv), (jnp.arange(block_count, dtype=jnp.int32), log_totals)
    )
    d_query_rot = d_query_blocks.reshape(pack_rows, local_heads, head_dim)
    d_query = (
        unrotate(d_query_rot, cosine, sine).reshape(pack_rows, query_width).astype(jnp.bfloat16)
    )
    d_key = unrotate(d_key_rot, cosine, sine).reshape(pack_rows, kv_width).astype(jnp.bfloat16)
    d_value = d_value_sum.reshape(pack_rows, kv_width).astype(jnp.bfloat16)
    d_all = jnp.concatenate([d_query, d_key, d_value], axis=1)
    hidden = act.shape[1]
    plan = []
    for array, feature, out in ((0, 0, 0), (1, 1, 1), (2, 1, 2)):
        for start, width in split_width(hidden, 1536):
            plan.append((array, feature, start, width, ((out, start, width),)))
    plan.append((3, 2, 0, query_width, ((3, 0, query_width),)))
    plan.append(
        (4, 3, 0, d_all.shape[1], ((4, 0, query_width), (5, 0, kv_width), (6, 0, kv_width)))
    )
    down_rows, g_gate, g_up, out_rows, g_query, g_key, g_value = weight_grads(
        [act, d_gate, d_up, attended, d_all],
        [spread_features(x) for x in (full_dy, full_two, full_db, full_one)],
        plan,
        [hidden, hidden, hidden, query_width, query_width, kv_width, kv_width],
    )
    d_normed_one = own_rows(
        against(d_query, w_query) + against(d_key, w_key) + against(d_value, w_value),
        rank,
        tok_rows,
    )
    attn_norm_back, attn_gain_part = norm_back(d_normed_one, first_norm, first_scale, attn_gain)
    token_grad = ((d_middle + attn_norm_back) * own_valid[:, None]).astype(jnp.bfloat16)
    place = (lax.axis_index("dp") * tensor_size + rank) * gain_rows
    g_mlp_gain = lax.dynamic_slice_in_dim(sum_all(mlp_gain_part), place, gain_rows)
    g_attn_gain = lax.dynamic_slice_in_dim(sum_all(attn_gain_part), place, gain_rows)
    return (
        layer_out,
        token_grad,
        g_attn_gain,
        g_query,
        g_key,
        g_value,
        out_rows.T,
        g_mlp_gain,
        g_gate,
        g_up,
        down_rows.T,
    )


def solution(mesh):
    placed = (
        P(("dp", "tensor"), None),
        P("dp"),
        P(),
        P(None, "tensor"),
        P(None, "tensor"),
        P(None, "tensor"),
        P("tensor", None),
        P(),
        P(None, "tensor"),
        P(None, "tensor"),
        P("tensor", None),
        P(("dp", "tensor"), None),
    )
    return jax.shard_map(
        on_device,
        mesh=mesh,
        in_specs=placed,
        out_specs=(
            P(("dp", "tensor"), None),
            P(("dp", "tensor"), None),
            P(("dp", "tensor")),
            P("dp", "tensor"),
            P("dp", "tensor"),
            P("dp", "tensor"),
            P("tensor", "dp"),
            P(("dp", "tensor")),
            P("dp", "tensor"),
            P("dp", "tensor"),
            P("tensor", "dp"),
        ),
        check_vma=False,
    )
```

```python
import functools
import math

import jax
import jax.numpy as jnp
from jax import lax
from jax.experimental import pallas as pl
from jax.experimental.pallas import tpu as pltpu
from jax.sharding import PartitionSpec as P

HD = 64
MESH = pl.DeviceIdType.MESH
TILE = 256
MOST = 1024
LANES = 128
RING = 4
ROWS = 16


norm_eps = 1e-05
masked_score = -1e30


def packing(lengths, places):
    frag_count = lengths.shape[0]
    ends_at = jnp.cumsum(lengths, dtype=jnp.int32)
    filled = ends_at[frag_count - 1]
    segment = jnp.sum((places[:, None] >= ends_at[None, :]).astype(jnp.int32), axis=1)
    starts = jnp.concatenate([ends_at - lengths, filled[None]])
    labels = jnp.arange(frag_count + 1, dtype=jnp.int32)
    offset = jnp.sum(jnp.where(segment[:, None] == labels[None, :], starts[None, :], 0), axis=1)
    return (segment, places - offset, (places < filled).astype(jnp.float32))


def rotary_tables(position, head_dim):
    halves = jnp.arange(head_dim // 2, dtype=jnp.float32)
    inverse = jnp.exp(halves * (-2.0 * math.log(10000.0) / head_dim))
    angles = position.astype(jnp.float32)[:, None] * inverse[None, :]
    return (jnp.cos(angles), jnp.sin(angles))


def rotate(values, cosine, sine):
    half_dim = values.shape[-1] // 2
    first_half = values[..., :half_dim]
    second_half = values[..., half_dim:]
    cos_rows = cosine[:, None, :]
    sin_rows = sine[:, None, :]
    return jnp.concatenate(
        [
            first_half * cos_rows - second_half * sin_rows,
            second_half * cos_rows + first_half * sin_rows,
        ],
        axis=-1,
    )


def against(left, right):
    return lax.dot_general(
        left, right, (((1,), (1,)), ((), ())), preferred_element_type=jnp.float32
    )


def inner_rows(left, right):
    return lax.dot_general(
        left, right, (((0,), (0,)), ((), ())), preferred_element_type=jnp.float32
    )


def swap(value):
    return lax.ppermute(value, "tensor", [(0, 1), (1, 0)])


def join_rows(own, other, rank):
    first = jnp.where(rank == 0, own, other)
    second = jnp.where(rank == 0, other, own)
    return jnp.concatenate([first, second], axis=0)


def own_rows(partial, rank, rows):
    away = lax.dynamic_slice_in_dim(partial, (1 - rank) * rows, rows).astype(jnp.bfloat16)
    kept = lax.dynamic_slice_in_dim(partial, rank * rows, rows)
    return kept + swap(away).astype(jnp.float32)


def flip(value, by):
    for step in range(by.bit_length()):
        if by >> step & 1:
            value = value + (1 - 2 * lax.rem(lax.div(value, 2**step), 2)) * 2**step
    return value


def aligned(start, size):
    return pl.ds(pl.multiple_of(start, size), size)


class Jobs:
    def __init__(self, hidden, query_width, kv_width):
        self.groups = []
        tiles = hidden // TILE
        parts = -(-hidden // MOST)
        sizes = [tiles // parts + (1 if i >= parts - tiles % parts else 0) for i in range(parts)]
        self.plan = []
        for part in range(parts):
            start, width = sum(sizes[:part]) * TILE, sizes[part] * TILE
            self.groups.append((sum(sizes[:part]), sizes[part]))
            for array, feature in ((0, 0), (1, 1), (2, 1)):
                self.plan.append((array, feature, start, width, ((array, start, width),)))
        self.first_attention = len(self.plan)
        self.plan.append((3, 2, 0, query_width, ((3, 0, query_width),)))
        cut = 3 * TILE
        self.plan.append((4, 3, 0, cut, ((4, 0, cut),)))
        rest = query_width - cut
        self.plan.append(
            (4, 3, cut, rest + 2 * kv_width, ((4, cut, rest), (5, 0, kv_width), (6, 0, kv_width)))
        )
        self.widths = [hidden, hidden, hidden, query_width, query_width + 2 * kv_width]
        self.outs = [hidden, hidden, hidden, query_width, query_width, kv_width, kv_width]
        self.most = max(job[3] for job in self.plan)
        self.pieces = max(len(job[4]) for job in self.plan)


INPUTS = (
    "two_own", "dy", "one", "middle", "tokens", "valid",
    "attended", "query", "keys", "values", "mask", "cosine",
    "sine", "attn_gain", "mlp_gain", "w_query", "w_key", "w_value",
    "w_out", "w_gate", "w_up", "w_down",
)
SCRATCH = (
    "x0", "x1", "x2", "x3", "x4", "f0",
    "f1", "f2", "f3", "source", "sent", "came",
    "sent_late", "came_late", "total", "gate_w", "up_w", "down_w",
    "mlp_acc", "norm_acc", "two_full", "db_full", "x_came", "x_sent",
    "d_att", "d_middle", "stage", "gain_part", "gain_all", "gain_came",
    "keys_acc", "values_acc", "local_sem", "feat_send", "feat_recv", "near_send",
    "near_recv", "far_send", "far_recv", "out_sem", "weight_sem", "x_send",
    "x_recv", "gain_send", "gain_recv", "last_sem",
)


def layer_kernel(jobs, bits, *refs):
    plan = jobs.plan
    inp = dict(zip(INPUTS, refs))
    refs = refs[len(INPUTS) :]
    outs = refs[: len(jobs.outs)]
    layer_out, token_grad, gains_out = refs[len(jobs.outs) : len(jobs.outs) + 3]
    scr = dict(zip(SCRATCH, refs[len(jobs.outs) + 3 :]))
    every = [scr["x%d" % i] for i in range(5)]
    left = [scr["f%d" % i] for i in range(4)]
    sent, came, sent_late, came_late, total = (
        scr[name] for name in ("sent", "came", "sent_late", "came_late", "total")
    )
    local_sem, near_send, near_recv = scr["local_sem"], scr["near_send"], scr["near_recv"]
    tokens, width = inp["dy"].shape
    own = tokens // 2
    rows = left[0].shape[0]
    half, quarter = rows // 2, rows // 4
    ring_total = total.shape[0]
    ring_sent = sent.shape[0]

    me = lax.axis_index("dp")
    rank = lax.axis_index("tensor")
    low, high = lax.rem(me, 4), lax.div(me, 4)
    bit = [lax.rem(lax.div(high, 2**s), 2) for s in range(bits)]
    mine = aligned(rank * own, own)

    partners = [1, 2, 3] + [4 << s for s in range(bits)]
    barrier = pltpu.get_barrier_semaphore()
    for by in partners:
        pl.semaphore_signal(barrier, inc=1, device_id={"dp": flip(me, by)}, device_id_type=MESH)
    pl.semaphore_signal(barrier, inc=1, device_id={"tensor": 1 - rank}, device_id_type=MESH)
    pl.semaphore_wait(barrier, len(partners) + 1)

    def remote(src, dst, send, recv, by):
        return pltpu.make_async_remote_copy(
            src_ref=src,
            dst_ref=dst,
            send_sem=send,
            recv_sem=recv,
            device_id={"dp": flip(me, by)},
            device_id_type=MESH,
        )

    def x_copy(src, dst, i):
        return pltpu.make_async_remote_copy(
            src_ref=src,
            dst_ref=dst,
            send_sem=scr["x_send"].at[i],
            recv_sem=scr["x_recv"].at[i],
            device_id={"tensor": 1 - rank},
            device_id_type=MESH,
        )


    def slot(array, j, start, columns):
        return every[array].at[pl.ds(j * tokens, tokens), pl.ds(start, columns)]

    def near(t, j):
        array, _, start, columns, _ = plan[t]
        src = slot(array, 2 if j == 3 else 0, start, columns)
        dst = slot(array, j, start, columns)
        return remote(src, dst, near_send.at[t, j], near_recv.at[t, j], 2 if j == 2 else 1)

    def stage_rows(s):
        return half - (half >> (s - 1)), quarter >> (s - 1)

    def far(t, s):
        columns = plan[t][3]
        if s == 0:
            src, dst = sent.at[t % ring_sent], came.at[t % RING]
            at = (slice(None), pl.ds(0, columns))
        else:
            src, dst = sent_late.at[t % ring_sent], came_late.at[t % RING]
            at = (pl.ds(*stage_rows(s)), pl.ds(0, columns))
        return remote(
            src.at[at], dst.at[at], scr["far_send"].at[t, s], scr["far_recv"].at[t, s], 4 << s
        )

    def final_row():
        row = 0
        for s in range(2, bits):
            row = row + bit[s] * (quarter >> (s - 1))
        return row

    last_size = quarter >> (bits - 2)

    def outputs(t):
        copies = []
        done = 0
        for i, (out, first, columns) in enumerate(plan[t][4]):
            copies.append(
                pltpu.make_async_copy(
                    total.at[t % ring_total].at[
                        aligned(final_row(), last_size), pl.ds(done, columns)
                    ],
                    outs[out].at[:, pl.ds(first, columns)],
                    scr["out_sem"].at[t, i],
                )
            )
            done += columns
        return copies

    def tiles(t, body):
        _, _, start, columns, _ = plan[t]

        @pl.loop(0, columns // TILE)
        def _(i):
            body(aligned(start + i * TILE, TILE), aligned(i * TILE, TILE))

    def dot(t, first, size, at):
        array, f = plan[t][:2]
        return jnp.dot(
            left[f][aligned(first, size), :], every[array][:, at], preferred_element_type=jnp.float32
        )

    def begin(t):
        near(t, 1).start()
        near(t, 2).start()

    def first_pass(t):
        if t >= ring_sent:
            far(t - ring_sent, 0).wait_send()

        def body(at, to):
            out = dot(t, (1 - bit[0]) * half, half, at)
            sent[t % ring_sent, :, to] = out.astype(jnp.bfloat16)

        tiles(t, body)
        far(t, 0).start()

    def second_pass(t):
        far(t, 0).wait_recv()
        if t >= ring_sent:
            far(t - ring_sent, 1).wait_send()
        if t >= ring_total:
            for copy in outputs(t - ring_total):
                copy.wait()
        base = bit[0] * half

        def body(at, to):
            away, kept = (1 - bit[1]) * quarter, bit[1] * quarter
            out = dot(t, base + away, quarter, at)
            out = out + came[t % RING, aligned(away, quarter), to].astype(jnp.float32)
            sent_late[t % ring_sent, pl.ds(0, quarter), to] = out.astype(jnp.bfloat16)
            out = dot(t, base + kept, quarter, at)
            out = out + came[t % RING, aligned(kept, quarter), to].astype(jnp.float32)
            total[t % ring_total, :, to] = out

        tiles(t, body)
        far(t, 1).start()

    def later_pass(t, s):
        far(t, s - 1).wait_recv()
        if t >= ring_sent:
            far(t - ring_sent, s).wait_send()
        first, size = stage_rows(s - 1)
        piece = size // 2
        at_row = 0
        for q in range(2, s):
            at_row = at_row + bit[q] * (quarter >> (q - 1))
        away, kept = (1 - bit[s]) * piece, bit[s] * piece

        def body(at, to):
            out = total[t % ring_total, aligned(at_row + away, piece), to]
            out = out + came_late[t % RING, aligned(first + away, piece), to].astype(jnp.float32)
            sent_late[t % ring_sent, pl.ds(first + size, piece), to] = out.astype(jnp.bfloat16)
            row = aligned(at_row + kept, piece)
            out = total[t % ring_total, row, to]
            out = out + came_late[t % RING, aligned(first + kept, piece), to].astype(jnp.float32)
            total[t % ring_total, row, to] = out

        tiles(t, body)
        far(t, s).start()

    def last_pass(t):
        far(t, bits - 1).wait_recv()
        first, size = stage_rows(bits - 1)

        def body(at, to):
            row = aligned(final_row(), last_size)
            out = total[t % ring_total, row, to]
            out = out + came_late[t % RING, pl.ds(first, size), to].astype(jnp.float32)
            total[t % ring_total, row, to] = out

        tiles(t, body)
        for copy in outputs(t):
            copy.start()

    feature_waited = set()

    def step(t):
        if t < len(plan):
            near(t, 2).wait_recv()
            near(t, 3).start()
            ahead = t + 2
            if ahead < len(plan) and ahead != jobs.first_attention:
                begin(ahead)
            f = plan[t][1]
            if f not in feature_waited:
                feature_waited.add(f)
                for j in (1, 2, 3):
                    feature_copy(f, j).wait_recv()
            near(t, 1).wait_recv()
            near(t, 3).wait_recv()
            first_pass(t)
        if 0 <= t - 1 < len(plan):
            second_pass(t - 1)
        for s in range(2, bits):
            if 0 <= t - s < len(plan):
                later_pass(t - s, s)
        if 0 <= t - bits < len(plan):
            last_pass(t - bits)


    source_of = {0: 0, 3: 1, 1: 0, 2: 1}

    def feature_copy(f, j):
        return remote(
            scr["source"].at[source_of[f], flip(low, j)],
            left[f].at[:, pl.ds(j * tokens, tokens)],
            scr["feat_send"].at[f, j],
            scr["feat_recv"].at[f, j],
            j,
        )

    def spread(ref, f):
        count = 4 << bits
        block = width // count
        source = scr["source"].at[source_of[f]]

        @pl.loop(0, width // LANES)
        def _(c):
            turned = ref[:, aligned(c * LANES, LANES)].T
            for piece in range(LANES // block):
                d = c * (LANES // block) + piece
                group = lax.div(d, 4)
                place = 0
                for s in range(bits):
                    place = place + lax.rem(lax.div(group, 2**s), 2) * 2 ** (bits - 1 - s)
                source[lax.rem(d, 4), aligned(place * block, block), :] = turned[
                    piece * block : (piece + 1) * block
                ]

        for j in (2, 3, 1):
            feature_copy(f, j).start()
        left[f][:, pl.ds(0, tokens)] = source[low]


    weight_sem = scr["weight_sem"]

    def hidden_weights(i):
        at = lax.rem(i, 2)
        columns = aligned(i * TILE, TILE)
        return (
            pltpu.make_async_copy(
                inp["w_gate"].at[:, columns], scr["gate_w"].at[at], weight_sem.at[0, at]
            ),
            pltpu.make_async_copy(
                inp["w_up"].at[:, columns], scr["up_w"].at[at], weight_sem.at[1, at]
            ),
            pltpu.make_async_copy(
                inp["w_down"].at[columns, :], scr["down_w"].at[at], weight_sem.at[2, at]
            ),
        )

    hidden_tiles = jobs.outs[0] // TILE
    wide = 512

    def hidden_part(first, count):
        @pl.loop(first, first + count)
        def _(i):
            at = lax.rem(i, 2)

            @pl.when(i + 1 < hidden_tiles)
            def _():
                for copy in hidden_weights(i + 1):
                    copy.start()

            for copy in hidden_weights(i):
                copy.wait()
            gate_w, up_w, down_w = scr["gate_w"].at[at], scr["up_w"].at[at], scr["down_w"].at[at]
            two = scr["two_full"][...]
            gate = jnp.dot(two, gate_w[...], preferred_element_type=jnp.float32)
            up = jnp.dot(two, up_w[...], preferred_element_type=jnp.float32)
            d_act = against(inp["dy"][...], down_w[...])
            sig = jax.nn.sigmoid(gate)
            silu = gate * sig
            act = (silu * up).astype(jnp.bfloat16)
            d_gate = (d_act * up * sig * (1.0 + gate * (1.0 - sig))).astype(jnp.bfloat16)
            d_up = (d_act * silu).astype(jnp.bfloat16)
            columns = aligned(i * TILE, TILE)
            every[0][pl.ds(0, tokens), columns] = act
            every[1][pl.ds(0, tokens), columns] = d_gate
            every[2][pl.ds(0, tokens), columns] = d_up

            @pl.loop(0, width // wide)
            def _(n):
                part = aligned(n * wide, wide)
                scr["mlp_acc"][:, part] += jnp.dot(
                    act, down_w[:, part], preferred_element_type=jnp.float32
                )
                scr["norm_acc"][:, part] += against(d_gate, gate_w[part, :]) + against(
                    d_up, up_w[part, :]
                )

    def row_loop(body):
        @pl.loop(0, own // ROWS)
        def _(i):
            body(aligned(i * ROWS, ROWS), aligned(rank * own + i * ROWS, ROWS))

    def eight(value):
        return jnp.sum(value.reshape(ROWS // 8, 8, width), axis=0)

    def send_partial(acc, buffer):
        @pl.loop(0, own // ROWS)
        def _(i):
            row = aligned((1 - rank) * own + i * ROWS, ROWS)
            scr["x_sent"][buffer, aligned(i * ROWS, ROWS), :] = scr[acc][row, :].astype(
                jnp.bfloat16
            )


    def out_weights(i):
        return pltpu.make_async_copy(
            inp["w_out"].at[aligned(i * TILE, TILE), :],
            scr["down_w"].at[lax.rem(i, 2)],
            weight_sem.at[2, lax.rem(i, 2)],
        )

    def query_weights(j):
        name, index, at = (("gate_w", 0, 0), ("gate_w", 0, 1), ("up_w", 1, 0), ("up_w", 1, 1))[j % 4]
        dst, sem = scr[name].at[at], weight_sem.at[index, at]
        if j < query_tiles:
            return [
                pltpu.make_async_copy(inp["w_query"].at[:, pl.ds(j * TILE, TILE)], dst, sem)
            ]
        kv = inp["w_key"].shape[1]
        return [
            pltpu.make_async_copy(inp["w_key"], dst.at[:, pl.ds(0, kv)], sem),
            pltpu.make_async_copy(inp["w_value"], dst.at[:, pl.ds(kv, kv)], scr["last_sem"].at[2]),
        ]

    query_width = jobs.outs[3]
    kv_width = jobs.outs[5]
    query_tiles = query_width // TILE
    kv_heads = kv_width // HD
    pairs = query_width // LANES // kv_heads
    score_scale = HD ** (-0.5)

    def lane_masks():
        lane = lax.broadcasted_iota(jnp.int32, (1, LANES), 1)
        first = (lane < HD).astype(jnp.float32)
        return first, 1.0 - first

    def unrotate(value):
        lane = lax.broadcasted_iota(jnp.int32, value.shape, 1)
        other = jnp.where(
            lax.rem(lane, HD) < HD // 2,
            pltpu.roll(value, LANES - HD // 2, 1),
            pltpu.roll(value, HD // 2, 1),
        )
        return value * inp["cosine"][...] + other * inp["sine"][...]

    def d_attended():
        @pl.loop(0, query_tiles)
        def _(i):
            out_weights(i).wait()
            scr["d_att"][:, aligned(i * TILE, TILE)] = against(
                scr["db_full"][...], scr["down_w"][lax.rem(i, 2)]
            ).astype(jnp.bfloat16)

            @pl.when(i + 2 < query_tiles)
            def _():
                out_weights(i + 2).start()

    def attend_back(kv):
        keys, values = inp["keys"].at[kv], inp["values"].at[kv]
        keys_acc, values_acc = scr["keys_acc"].at[kv], scr["values_acc"].at[kv]
        keys_acc[...] = jnp.zeros_like(keys_acc)
        values_acc[...] = jnp.zeros_like(values_acc)

        @pl.loop(0, pairs)
        def _(p):
            columns = aligned((kv * pairs + p) * LANES, LANES)
            d_query = jnp.zeros((tokens, LANES), jnp.float32)
            for lanes in lane_masks():
                lanes_low = lanes.astype(jnp.bfloat16)
                query = inp["query"][:, columns] * lanes_low
                d_att = scr["d_att"][:, columns] * lanes_low
                scores = against(query, keys[...]) * score_scale
                scores = jnp.where(inp["mask"][...] > 0, scores, masked_score)
                expo = jnp.exp(scores - jnp.max(scores, axis=1, keepdims=True))
                probs = expo * (1.0 / jnp.sum(expo, axis=1, keepdims=True))
                d_probs = against(d_att, values[...])
                inner = jnp.sum(probs * d_probs, axis=1, keepdims=True)
                d_scores = (probs * (d_probs - inner)).astype(jnp.bfloat16)
                d_query = d_query + lanes * jnp.dot(
                    d_scores, keys[...], preferred_element_type=jnp.float32
                )
                keys_acc[...] += inner_rows(d_scores, query)
                values_acc[...] += inner_rows(probs.astype(jnp.bfloat16), d_att)
            every[4][pl.ds(0, tokens), columns] = unrotate(d_query * score_scale).astype(
                jnp.bfloat16
            )

    def finish_keys():
        lanes = lane_masks()
        d_key = jnp.zeros((tokens, LANES), jnp.float32)
        d_value = jnp.zeros((tokens, LANES), jnp.float32)
        for kv in range(kv_heads):
            for out in (0, 1):
                acc = scr["keys_acc" if out == 0 else "values_acc"][kv]
                acc = (acc + pltpu.roll(acc, HD, 1)) * lanes[kv]
                if out == 0:
                    d_key = d_key + acc
                else:
                    d_value = d_value + acc
        d_key = unrotate(d_key * score_scale)
        every[4][pl.ds(0, tokens), pl.ds(query_width, kv_width)] = d_key.astype(jnp.bfloat16)
        every[4][pl.ds(0, tokens), pl.ds(query_width + kv_width, kv_width)] = d_value.astype(
            jnp.bfloat16
        )

    def d_normed_one():
        for j in range(query_tiles + 1):
            for copy in query_weights(j):
                copy.wait()
            name, at = (("gate_w", 0), ("gate_w", 1), ("up_w", 0), ("up_w", 1))[j % 4]
            weights = scr[name].at[at]
            grads = every[4][pl.ds(0, tokens), pl.ds(j * TILE, TILE)]

            @pl.loop(0, width // wide)
            def _(n):
                part = aligned(n * wide, wide)
                add = against(grads, weights[part, :])
                if j == 0:
                    scr["norm_acc"][:, part] = add
                else:
                    scr["norm_acc"][:, part] += add

            if j + 4 < query_tiles + 1:
                for copy in query_weights(j + 4):
                    copy.start()


    def mean_rows(value):
        return jnp.mean(value, axis=1, keepdims=True)

    def middle_back(row, full):
        grad = scr["norm_acc"][full, :] + scr["x_came"][0, row, :].astype(jnp.float32)
        middle = inp["middle"][row, :]
        scale = lax.rsqrt(mean_rows(middle * middle) + norm_eps)
        normed = middle * scale
        scr["gain_part"][0] += eight(grad * normed)
        scaled = grad * inp["mlp_gain"][...]
        d_middle = inp["dy"][full, :].astype(jnp.float32) + scale * (
            scaled - normed * mean_rows(scaled * normed)
        )
        scr["d_middle"][row, :] = d_middle
        scr["db_full"][full, :] = d_middle.astype(jnp.bfloat16)

    def finish_layer(row, full):
        mlp = scr["mlp_acc"][full, :] + scr["x_came"][1, row, :].astype(jnp.float32)
        scr["stage"][row, :] = (inp["middle"][row, :] + mlp).astype(jnp.bfloat16)

    def token_back(row, full):
        grad = scr["norm_acc"][full, :] + scr["x_came"][2, row, :].astype(jnp.float32)
        valid = inp["valid"][row, :][:, :1]
        masked = inp["tokens"][row, :].astype(jnp.float32) * valid
        scale = lax.rsqrt(mean_rows(masked * masked) + norm_eps)
        normed = masked * scale
        scr["gain_part"][1] += eight(grad * normed)
        scaled = grad * inp["attn_gain"][...]
        out = scr["d_middle"][row, :] + scale * (scaled - normed * mean_rows(scaled * normed))
        scr["stage"][row, :] = (out * valid).astype(jnp.bfloat16)

    def gain_copy(i):
        src, dst = scr["gain_all"].at[i], scr["gain_came"].at[i]
        if i < bits + 2:
            return remote(src, dst, scr["gain_send"].at[i], scr["gain_recv"].at[i], 1 << i)
        return pltpu.make_async_remote_copy(
            src_ref=src,
            dst_ref=dst,
            send_sem=scr["gain_send"].at[i],
            recv_sem=scr["gain_recv"].at[i],
            device_id={"tensor": 1 - rank},
            device_id_type=MESH,
        )

    gain_steps = bits + 3

    def gain_next(i):
        gain_copy(i).wait_recv()
        scr["gain_all"][i + 1] = scr["gain_all"][i] + scr["gain_came"][i]
        if i + 1 < gain_steps:
            gain_copy(i + 1).start()


    two_copy = x_copy(inp["two_own"], scr["two_full"].at[mine, :], 0)
    two_copy.start()
    two_here = pltpu.make_async_copy(inp["two_own"], scr["two_full"].at[mine, :], local_sem.at[0])
    two_here.start()
    for copy in hidden_weights(0):
        copy.start()
    out_job = jobs.first_attention
    every[3][pl.ds(0, tokens), :] = inp["attended"][...]
    begin(out_job)
    spread(inp["dy"], 0)
    spread(inp["one"], 3)
    scr["mlp_acc"][...] = jnp.zeros_like(scr["mlp_acc"])
    scr["norm_acc"][...] = jnp.zeros_like(scr["norm_acc"])
    scr["gain_part"][...] = jnp.zeros_like(scr["gain_part"])
    two_here.wait()
    two_copy.wait_recv()
    hidden_part(*jobs.groups[0])
    begin(0)
    begin(1)
    for j in (1, 2, 3):
        feature_copy(0, j).wait_send()
    spread(scr["two_full"], 1)
    hidden_part(*jobs.groups[1])
    step(0)
    hidden_part(*jobs.groups[2])
    send_partial("norm_acc", 0)
    norm_copy = x_copy(scr["x_sent"].at[0], scr["x_came"].at[0], 1)
    norm_copy.start()
    for i in range(2):
        out_weights(i).start()
    for j in range(4):
        for copy in query_weights(j):
            copy.start()
    send_partial("mlp_acc", 1)
    step(1)
    norm_copy.wait_recv()
    row_loop(middle_back)
    db_copy = x_copy(scr["db_full"].at[mine, :], scr["db_full"].at[mine, :], 2)
    db_copy.start()
    mlp_copy = x_copy(scr["x_sent"].at[1], scr["x_came"].at[1], 3)
    step(2)
    for j in (1, 2, 3):
        feature_copy(3, j).wait_send()
    db_copy.wait_recv()
    mlp_copy.start()
    spread(scr["db_full"], 2)
    d_attended()
    step(3)
    attend_back(0)
    step(4)
    attend_back(1)
    finish_keys()
    step(5)
    d_normed_one()
    norm_copy.wait_send()
    send_partial("norm_acc", 0)
    one_copy = x_copy(scr["x_sent"].at[0], scr["x_came"].at[2], 4)
    one_copy.start()
    mlp_copy.wait_recv()
    row_loop(finish_layer)
    layer_copy = pltpu.make_async_copy(scr["stage"], layer_out, scr["last_sem"].at[0])
    layer_copy.start()
    step(6)
    layer_copy.wait()
    one_copy.wait_recv()
    row_loop(token_back)
    token_copy = pltpu.make_async_copy(scr["stage"], token_grad, scr["last_sem"].at[1])
    token_copy.start()
    gains = scr["gain_all"].at[0]
    gains[...] = jnp.zeros_like(gains)
    for i in range(2):
        gains[pl.ds(i, 1), :] = jnp.sum(scr["gain_part"][i], axis=0, keepdims=True)
    gain_copy(0).start()
    at = 7
    for i in range(gain_steps):
        if at < len(plan) - 1:
            step(at)
            at += 1
        gain_next(i)
    gains_copy = pltpu.make_async_copy(
        scr["gain_all"].at[gain_steps], gains_out, local_sem.at[1]
    )
    gains_copy.start()
    for t in range(at, len(plan) + bits):
        step(t)


    two_copy.wait_send()
    db_copy.wait_send()
    mlp_copy.wait_send()
    one_copy.wait_send()
    token_copy.wait()
    gains_copy.wait()
    for i in range(gain_steps):
        gain_copy(i).wait_send()
    for f in (1, 2):
        for j in (1, 2, 3):
            feature_copy(f, j).wait_send()
    for t in range(len(plan)):
        for j in (1, 2, 3):
            near(t, j).wait_send()
        if t + ring_sent >= len(plan):
            for s in range(bits):
                far(t, s).wait_send()
        if t + ring_total >= len(plan):
            for copy in outputs(t):
                copy.wait()


def layer_call(jobs, args, tokens, width):
    count = lax.axis_size("dp")
    bits = (count // 4).bit_length() - 1
    rows = width // 4
    block = width // count
    own = tokens // 2
    plan = jobs.plan
    vmem, any_space = pl.BlockSpec(memory_space=pltpu.VMEM), pl.BlockSpec(memory_space=pl.ANY)
    bf16, f32 = jnp.bfloat16, jnp.float32
    late_rows = rows // 2 - (rows // 2 >> (bits - 1))
    ring_total = bits + 2
    kv_heads = jobs.outs[5] // HD
    dma = pltpu.SemaphoreType.DMA
    scratch = dict(
        source=((2, 4, rows, tokens), bf16),
        sent=((3, rows // 2, jobs.most), bf16),
        came=((RING, rows // 2, jobs.most), bf16),
        sent_late=((3, late_rows, jobs.most), bf16),
        came_late=((RING, late_rows, jobs.most), bf16),
        total=((ring_total, rows // 4, jobs.most), f32),
        gate_w=((2, width, TILE), bf16),
        up_w=((2, width, TILE), bf16),
        down_w=((2, TILE, width), bf16),
        mlp_acc=((tokens, width), f32),
        norm_acc=((tokens, width), f32),
        two_full=((tokens, width), bf16),
        db_full=((tokens, width), bf16),
        x_came=((3, own, width), bf16),
        x_sent=((2, own, width), bf16),
        d_att=((tokens, jobs.outs[3]), bf16),
        d_middle=((own, width), f32),
        stage=((own, width), bf16),
        gain_part=((2, 8, width), f32),
        gain_all=((bits + 4, 8, width), f32),
        gain_came=((bits + 3, 8, width), f32),
        keys_acc=((kv_heads, tokens, LANES), f32),
        values_acc=((kv_heads, tokens, LANES), f32),
        local_sem=(2,),
        feat_send=(4, 4),
        feat_recv=(4, 4),
        near_send=(len(plan), 4),
        near_recv=(len(plan), 4),
        far_send=(len(plan), bits),
        far_recv=(len(plan), bits),
        out_sem=(len(plan), jobs.pieces),
        weight_sem=(3, 2),
        x_send=(5,),
        x_recv=(5,),
        gain_send=(bits + 3,),
        gain_recv=(bits + 3,),
        last_sem=(3,),
    )
    for i, w in enumerate(jobs.widths):
        scratch["x%d" % i] = ((4 * tokens, w), bf16)
    for i in range(4):
        scratch["f%d" % i] = ((rows, 4 * tokens), bf16)
    shapes = [
        dma(scratch[name]) if name.endswith(("_sem", "_send", "_recv")) else pltpu.VMEM(*scratch[name])
        for name in SCRATCH
    ]
    return pl.pallas_call(
        functools.partial(layer_kernel, jobs, bits),
        out_shape=[jax.ShapeDtypeStruct((block, w), f32) for w in jobs.outs]
        + [
            jax.ShapeDtypeStruct((own, width), bf16),
            jax.ShapeDtypeStruct((own, width), bf16),
            jax.ShapeDtypeStruct((8, width), f32),
        ],
        in_specs=[any_space if name.startswith("w_") else vmem for name in INPUTS],
        out_specs=[any_space] * (len(jobs.outs) + 3),
        scratch_shapes=shapes,
        compiler_params=pltpu.CompilerParams(
            collective_id=0, has_side_effects=True, vmem_limit_bytes=63 * 1024 * 1024
        ),
    )(*[args[name] for name in INPUTS])


def on_device(
    tokens,
    frag_lengths,
    attn_gain,
    w_query,
    w_key,
    w_value,
    w_out,
    mlp_gain,
    w_gate,
    w_up,
    w_down,
    out_cotangent,
):
    tok_rows, model_width = tokens.shape
    pack_rows = tok_rows * lax.axis_size("tensor")
    head_dim = HD
    query_width = w_query.shape[1]
    kv_width = w_key.shape[1]
    local_heads = query_width // head_dim
    local_kv = kv_width // head_dim
    groups = local_heads // local_kv
    score_scale = head_dim ** (-0.5)
    rank = lax.axis_index("tensor")
    places = jnp.arange(pack_rows, dtype=jnp.int32)
    segment, position, valid = packing(frag_lengths, places)
    own_valid = lax.dynamic_slice_in_dim(valid, rank * tok_rows, tok_rows)
    cosine, sine = rotary_tables(position, head_dim)
    masked = tokens.astype(jnp.float32) * own_valid[:, None]
    first_scale = lax.rsqrt(jnp.mean(masked * masked, axis=1, keepdims=True) + norm_eps)
    own_one = (masked * first_scale * attn_gain).astype(jnp.bfloat16)
    full_one = join_rows(own_one, swap(own_one), rank)
    d_out = (out_cotangent.astype(jnp.float32) * own_valid[:, None]).astype(jnp.bfloat16)
    full_one, d_out = lax.optimization_barrier((full_one, d_out))
    other_d_out = swap(d_out)
    query_lin = jnp.dot(full_one, w_query, preferred_element_type=jnp.float32)
    key_lin = jnp.dot(full_one, w_key, preferred_element_type=jnp.float32)
    value_low = jnp.dot(full_one, w_value, preferred_element_type=jnp.float32).astype(jnp.bfloat16)
    value_low = value_low.reshape(pack_rows, local_kv, head_dim)
    query_rot = rotate(query_lin.reshape(pack_rows, local_heads, head_dim), cosine, sine)
    query_rot = query_rot.astype(jnp.bfloat16)
    key_rot = rotate(key_lin.reshape(pack_rows, local_kv, head_dim), cosine, sine)
    key_rot = key_rot.astype(jnp.bfloat16)
    allowed = (segment[:, None] == segment[None, :]) & (places[None, :] <= places[:, None])
    query_blk = query_rot.reshape(pack_rows, local_kv, groups, head_dim)
    scores = jnp.einsum("ikgd,jkd->kgij", query_blk, key_rot, preferred_element_type=jnp.float32)
    scores = jnp.where(allowed[None, None], scores * score_scale, masked_score)
    expo = jnp.exp(scores - jnp.max(scores, axis=-1, keepdims=True))
    probs_low = (expo / jnp.sum(expo, axis=-1, keepdims=True)).astype(jnp.bfloat16)
    attended = jnp.einsum("kgij,jkd->ikgd", probs_low, value_low, preferred_element_type=jnp.float32)
    attended = attended.reshape(pack_rows, query_width).astype(jnp.bfloat16)
    attended, other_d_out = lax.optimization_barrier((attended, other_d_out))
    full_dy = join_rows(d_out, other_d_out, rank)
    branch = own_rows(jnp.dot(attended, w_out, preferred_element_type=jnp.float32), rank, tok_rows)
    middle = masked + branch
    second_scale = lax.rsqrt(jnp.mean(middle * middle, axis=1, keepdims=True) + norm_eps)
    own_two = (middle * second_scale * mlp_gain).astype(jnp.bfloat16)

    def doubled(heads):
        turned = heads.transpose(1, 0, 2)
        return jnp.concatenate([turned, turned], axis=-1)

    jobs = Jobs(w_gate.shape[1], query_width, kv_width)
    args = dict(
        two_own=own_two,
        dy=full_dy,
        one=full_one,
        middle=middle,
        tokens=tokens,
        valid=jnp.broadcast_to(own_valid[:, None], (tok_rows, LANES)),
        attended=attended,
        query=query_rot.reshape(pack_rows, query_width),
        keys=doubled(key_rot),
        values=doubled(value_low),
        mask=allowed.astype(jnp.float32),
        cosine=jnp.concatenate([cosine] * 4, axis=1),
        sine=jnp.concatenate([sine, -sine] * 2, axis=1),
        attn_gain=attn_gain[None, :],
        mlp_gain=mlp_gain[None, :],
        w_query=w_query,
        w_key=w_key,
        w_value=w_value,
        w_out=w_out,
        w_gate=w_gate,
        w_up=w_up,
        w_down=w_down,
    )
    out = layer_call(jobs, args, pack_rows, model_width)
    down_rows, g_gate, g_up, out_rows, g_query, g_key, g_value, layer_out, token_grad, gains = out
    gain_rows = model_width // (lax.axis_size("tensor") * lax.axis_size("dp"))
    place = (lax.axis_index("dp") * lax.axis_size("tensor") + rank) * gain_rows
    gains = lax.dynamic_slice_in_dim(gains[:2], place, gain_rows, axis=1)
    return (
        layer_out,
        token_grad,
        gains[1],
        g_query,
        g_key,
        g_value,
        out_rows.T,
        gains[0],
        g_gate,
        g_up,
        down_rows.T,
    )


def solution(mesh):
    placed = (
        P(("dp", "tensor"), None),
        P("dp"),
        P(),
        P(None, "tensor"),
        P(None, "tensor"),
        P(None, "tensor"),
        P("tensor", None),
        P(),
        P(None, "tensor"),
        P(None, "tensor"),
        P("tensor", None),
        P(("dp", "tensor"), None),
    )
    return jax.shard_map(
        on_device,
        mesh=mesh,
        in_specs=placed,
        out_specs=(
            P(("dp", "tensor"), None),
            P(("dp", "tensor"), None),
            P(("dp", "tensor")),
            P("dp", "tensor"),
            P("dp", "tensor"),
            P("dp", "tensor"),
            P("tensor", "dp"),
            P(("dp", "tensor")),
            P("dp", "tensor"),
            P("dp", "tensor"),
            P("tensor", "dp"),
        ),
        check_vma=False,
    )
```

```python
import functools
import math
from typing import Any, NamedTuple

import jax
import jax.numpy as jnp
from jax import lax
from jax.experimental import pallas as pl
from jax.experimental.pallas import tpu as pltpu
from jax.sharding import PartitionSpec as P

HD = 64
MESH = pl.DeviceIdType.MESH
TILE = 256
MOST = 1024
LANES = 128
RING = 4
ROWS = 16


norm_eps = 1e-05
masked_score = -1e30


def against(left, right):
    return lax.dot_general(
        left, right, (((1,), (1,)), ((), ())), preferred_element_type=jnp.float32
    )


def inner_rows(left, right):
    return lax.dot_general(
        left, right, (((0,), (0,)), ((), ())), preferred_element_type=jnp.float32
    )


def flip(value, by):
    for step in range(by.bit_length()):
        if by >> step & 1:
            value = value + (1 - 2 * lax.rem(lax.div(value, 2**step), 2)) * 2**step
    return value


def aligned(start, size):
    return pl.ds(pl.multiple_of(start, size), size)


class Jobs:
    def __init__(self, hidden, query_width, kv_width):
        self.groups = []
        tiles = hidden // TILE
        parts = -(-hidden // MOST)
        sizes = [tiles // parts + (1 if i >= parts - tiles % parts else 0) for i in range(parts)]
        self.plan = []
        for part in range(parts):
            start, width = sum(sizes[:part]) * TILE, sizes[part] * TILE
            self.groups.append((sum(sizes[:part]), sizes[part]))
            for array, feature in ((0, 0), (1, 1), (2, 1)):
                self.plan.append((array, feature, start, width, ((array, start, width),)))
        self.first_attention = len(self.plan)
        self.plan.append((3, 2, 0, query_width, ((3, 0, query_width),)))
        cut = 3 * TILE
        self.plan.append((4, 3, 0, cut, ((4, 0, cut),)))
        rest = query_width - cut
        self.plan.append(
            (4, 3, cut, rest + 2 * kv_width, ((4, cut, rest), (5, 0, kv_width), (6, 0, kv_width)))
        )
        self.widths = [hidden, hidden, hidden, query_width, query_width + 2 * kv_width]
        self.outs = [hidden, hidden, hidden, query_width, query_width, kv_width, kv_width]
        self.most = max(job[3] for job in self.plan)
        self.pieces = max(len(job[4]) for job in self.plan)


class Inputs(NamedTuple):
    lengths: Any
    attn_gain: Any
    mlp_gain: Any
    tokens: Any
    cotangent: Any
    w_query: Any
    w_key: Any
    w_value: Any
    w_out: Any
    w_gate: Any
    w_up: Any
    w_down: Any


class Scratch(NamedTuple):
    tok_full: Any
    dy: Any
    one_full: Any
    middle: Any
    query: Any
    keys: Any
    values: Any
    mask: Any
    cosine: Any
    sine: Any
    valid: Any
    source: Any
    sent: Any
    came: Any
    sent_late: Any
    came_late: Any
    total: Any
    gate_w: Any
    up_w: Any
    down_w: Any
    mlp_acc: Any
    norm_acc: Any
    two_full: Any
    db_full: Any
    x_came: Any
    x_sent: Any
    d_att: Any
    d_middle: Any
    stage: Any
    gain_part: Any
    gain_all: Any
    gain_came: Any
    keys_acc: Any
    values_acc: Any
    local_sem: Any
    feat_send: Any
    feat_recv: Any
    near_send: Any
    near_recv: Any
    far_send: Any
    far_recv: Any
    out_sem: Any
    weight_sem: Any
    x_send: Any
    x_recv: Any
    gain_send: Any
    gain_recv: Any
    last_sem: Any
    first_sem: Any


def layer_kernel(jobs, bits, *refs):
    plan = jobs.plan
    inp = Inputs(*refs[: len(Inputs._fields)])
    refs = refs[len(Inputs._fields) :]
    outs = refs[: len(jobs.outs)]
    layer_out, token_grad, gains_out = refs[len(jobs.outs) : len(jobs.outs) + 3]
    refs = refs[len(jobs.outs) + 3 :]
    every, left, scr = refs[:5], refs[5:9], Scratch(*refs[9:])
    sent, came, total = scr.sent, scr.came, scr.total
    sent_late, came_late = scr.sent_late, scr.came_late
    local_sem, near_send, near_recv = scr.local_sem, scr.near_send, scr.near_recv
    tokens, width = scr.dy.shape
    own = tokens // 2
    rows = left[0].shape[0]
    half, quarter = rows // 2, rows // 4
    ring_total = total.shape[0]
    ring_sent = sent.shape[0]

    me = lax.axis_index("dp")
    rank = lax.axis_index("tensor")
    low, high = lax.rem(me, 4), lax.div(me, 4)
    bit = [lax.rem(lax.div(high, 2**s), 2) for s in range(bits)]
    mine = aligned(rank * own, own)

    partners = [1, 2, 3] + [4 << s for s in range(bits)]
    barrier = pltpu.get_barrier_semaphore()
    for by in partners:
        pl.semaphore_signal(barrier, inc=1, device_id={"dp": flip(me, by)}, device_id_type=MESH)
    pl.semaphore_signal(barrier, inc=1, device_id={"tensor": 1 - rank}, device_id_type=MESH)
    pl.semaphore_wait(barrier, len(partners) + 1)

    def remote(src, dst, send, recv, by):
        return pltpu.make_async_remote_copy(
            src_ref=src,
            dst_ref=dst,
            send_sem=send,
            recv_sem=recv,
            device_id={"dp": flip(me, by)},
            device_id_type=MESH,
        )

    def x_copy(src, dst, i):
        return pltpu.make_async_remote_copy(
            src_ref=src,
            dst_ref=dst,
            send_sem=scr.x_send.at[i],
            recv_sem=scr.x_recv.at[i],
            device_id={"tensor": 1 - rank},
            device_id_type=MESH,
        )


    def slot(array, j, start, columns):
        return every[array].at[pl.ds(j * tokens, tokens), pl.ds(start, columns)]

    def near(t, j):
        array, _, start, columns, _ = plan[t]
        src = slot(array, 2 if j == 3 else 0, start, columns)
        dst = slot(array, j, start, columns)
        return remote(src, dst, near_send.at[t, j], near_recv.at[t, j], 2 if j == 2 else 1)

    def stage_rows(s):
        return half - (half >> (s - 1)), quarter >> (s - 1)

    def far(t, s):
        columns = plan[t][3]
        if s == 0:
            src, dst = sent.at[t % ring_sent], came.at[t % RING]
            at = (slice(None), pl.ds(0, columns))
        else:
            src, dst = sent_late.at[t % ring_sent], came_late.at[t % RING]
            at = (pl.ds(*stage_rows(s)), pl.ds(0, columns))
        return remote(
            src.at[at], dst.at[at], scr.far_send.at[t, s], scr.far_recv.at[t, s], 4 << s
        )

    def final_row():
        row = 0
        for s in range(2, bits):
            row = row + bit[s] * (quarter >> (s - 1))
        return row

    last_size = quarter >> (bits - 2)

    def outputs(t):
        copies = []
        done = 0
        for i, (out, first, columns) in enumerate(plan[t][4]):
            copies.append(
                pltpu.make_async_copy(
                    total.at[t % ring_total].at[
                        aligned(final_row(), last_size), pl.ds(done, columns)
                    ],
                    outs[out].at[:, pl.ds(first, columns)],
                    scr.out_sem.at[t, i],
                )
            )
            done += columns
        return copies

    def tiles(t, body):
        _, _, start, columns, _ = plan[t]

        @pl.loop(0, columns // TILE)
        def _(i):
            body(aligned(start + i * TILE, TILE), aligned(i * TILE, TILE))

    def dot(t, first, size, at):
        array, f = plan[t][:2]
        return jnp.dot(
            left[f][aligned(first, size), :], every[array][:, at], preferred_element_type=jnp.float32
        )

    def begin(t):
        near(t, 1).start()
        near(t, 2).start()

    def first_pass(t):
        if t >= ring_sent:
            far(t - ring_sent, 0).wait_send()

        def body(at, to):
            out = dot(t, (1 - bit[0]) * half, half, at)
            sent[t % ring_sent, :, to] = out.astype(jnp.bfloat16)

        tiles(t, body)
        far(t, 0).start()

    def second_pass(t):
        far(t, 0).wait_recv()
        if t >= ring_sent:
            far(t - ring_sent, 1).wait_send()
        if t >= ring_total:
            for copy in outputs(t - ring_total):
                copy.wait()
        base = bit[0] * half

        def body(at, to):
            away, kept = (1 - bit[1]) * quarter, bit[1] * quarter
            out = dot(t, base + away, quarter, at)
            out = out + came[t % RING, aligned(away, quarter), to].astype(jnp.float32)
            sent_late[t % ring_sent, pl.ds(0, quarter), to] = out.astype(jnp.bfloat16)
            out = dot(t, base + kept, quarter, at)
            out = out + came[t % RING, aligned(kept, quarter), to].astype(jnp.float32)
            total[t % ring_total, :, to] = out

        tiles(t, body)
        far(t, 1).start()

    def later_pass(t, s):
        far(t, s - 1).wait_recv()
        if t >= ring_sent:
            far(t - ring_sent, s).wait_send()
        first, size = stage_rows(s - 1)
        piece = size // 2
        at_row = 0
        for q in range(2, s):
            at_row = at_row + bit[q] * (quarter >> (q - 1))
        away, kept = (1 - bit[s]) * piece, bit[s] * piece

        def body(at, to):
            out = total[t % ring_total, aligned(at_row + away, piece), to]
            out = out + came_late[t % RING, aligned(first + away, piece), to].astype(jnp.float32)
            sent_late[t % ring_sent, pl.ds(first + size, piece), to] = out.astype(jnp.bfloat16)
            row = aligned(at_row + kept, piece)
            out = total[t % ring_total, row, to]
            out = out + came_late[t % RING, aligned(first + kept, piece), to].astype(jnp.float32)
            total[t % ring_total, row, to] = out

        tiles(t, body)
        far(t, s).start()

    def last_pass(t):
        far(t, bits - 1).wait_recv()
        first, size = stage_rows(bits - 1)

        def body(at, to):
            row = aligned(final_row(), last_size)
            out = total[t % ring_total, row, to]
            out = out + came_late[t % RING, pl.ds(first, size), to].astype(jnp.float32)
            total[t % ring_total, row, to] = out

        tiles(t, body)
        for copy in outputs(t):
            copy.start()

    feature_waited = set()

    def step(t):
        if t < len(plan):
            near(t, 2).wait_recv()
            near(t, 3).start()
            ahead = t + 2
            if ahead < len(plan) and ahead != jobs.first_attention:
                begin(ahead)
            f = plan[t][1]
            if f not in feature_waited:
                feature_waited.add(f)
                for j in (1, 2, 3):
                    feature_copy(f, j).wait_recv()
            near(t, 1).wait_recv()
            near(t, 3).wait_recv()
            first_pass(t)
        if 0 <= t - 1 < len(plan):
            second_pass(t - 1)
        for s in range(2, bits):
            if 0 <= t - s < len(plan):
                later_pass(t - s, s)
        if 0 <= t - bits < len(plan):
            last_pass(t - bits)


    source_of = {0: 0, 3: 1, 1: 0, 2: 1}

    def feature_copy(f, j):
        return remote(
            scr.source.at[source_of[f], flip(low, j)],
            left[f].at[:, pl.ds(j * tokens, tokens)],
            scr.feat_send.at[f, j],
            scr.feat_recv.at[f, j],
            j,
        )

    def spread(ref, f):
        count = 4 << bits
        block = width // count
        source = scr.source.at[source_of[f]]

        @pl.loop(0, width // LANES)
        def _(c):
            turned = ref[:, aligned(c * LANES, LANES)].T
            for piece in range(LANES // block):
                d = c * (LANES // block) + piece
                group = lax.div(d, 4)
                place = 0
                for s in range(bits):
                    place = place + lax.rem(lax.div(group, 2**s), 2) * 2 ** (bits - 1 - s)
                source[lax.rem(d, 4), aligned(place * block, block), :] = turned[
                    piece * block : (piece + 1) * block
                ]

        for j in (2, 3, 1):
            feature_copy(f, j).start()
        left[f][:, pl.ds(0, tokens)] = source[low]


    weight_sem = scr.weight_sem

    def hidden_weights(i):
        at = lax.rem(i, 2)
        columns = aligned(i * TILE, TILE)
        return (
            pltpu.make_async_copy(
                inp.w_gate.at[:, columns], scr.gate_w.at[at], weight_sem.at[0, at]
            ),
            pltpu.make_async_copy(
                inp.w_up.at[:, columns], scr.up_w.at[at], weight_sem.at[1, at]
            ),
            pltpu.make_async_copy(
                inp.w_down.at[columns, :], scr.down_w.at[at], weight_sem.at[2, at]
            ),
        )

    hidden_tiles = jobs.outs[0] // TILE
    wide = 512

    def hidden_part(first, count):
        @pl.loop(first, first + count)
        def _(i):
            at = lax.rem(i, 2)

            @pl.when(i + 1 < hidden_tiles)
            def _():
                for copy in hidden_weights(i + 1):
                    copy.start()

            for copy in hidden_weights(i):
                copy.wait()
            gate_w, up_w, down_w = scr.gate_w.at[at], scr.up_w.at[at], scr.down_w.at[at]
            two = scr.two_full[...]
            gate = jnp.dot(two, gate_w[...], preferred_element_type=jnp.float32)
            up = jnp.dot(two, up_w[...], preferred_element_type=jnp.float32)
            d_act = against(scr.dy[...], down_w[...])
            sig = jax.nn.sigmoid(gate)
            silu = gate * sig
            act = (silu * up).astype(jnp.bfloat16)
            d_gate = (d_act * up * sig * (1.0 + gate * (1.0 - sig))).astype(jnp.bfloat16)
            d_up = (d_act * silu).astype(jnp.bfloat16)
            columns = aligned(i * TILE, TILE)
            every[0][pl.ds(0, tokens), columns] = act
            every[1][pl.ds(0, tokens), columns] = d_gate
            every[2][pl.ds(0, tokens), columns] = d_up

            @pl.loop(0, width // wide)
            def _(n):
                part = aligned(n * wide, wide)
                scr.mlp_acc[:, part] += jnp.dot(
                    act, down_w[:, part], preferred_element_type=jnp.float32
                )
                scr.norm_acc[:, part] += against(d_gate, gate_w[part, :]) + against(
                    d_up, up_w[part, :]
                )

    def row_loop(body):
        @pl.loop(0, own // ROWS)
        def _(i):
            body(aligned(i * ROWS, ROWS), aligned(rank * own + i * ROWS, ROWS))

    def eight(value):
        return jnp.sum(value.reshape(ROWS // 8, 8, width), axis=0)

    def send_partial(acc, buffer):
        @pl.loop(0, own // ROWS)
        def _(i):
            row = aligned((1 - rank) * own + i * ROWS, ROWS)
            scr.x_sent[buffer, aligned(i * ROWS, ROWS), :] = acc[row, :].astype(
                jnp.bfloat16
            )


    def out_weights(i):
        return pltpu.make_async_copy(
            inp.w_out.at[aligned(i * TILE, TILE), :],
            scr.down_w.at[lax.rem(i, 2)],
            weight_sem.at[2, lax.rem(i, 2)],
        )

    def query_buffer(j):
        return (scr.gate_w, scr.up_w)[j % 4 // 2].at[j % 2]

    def query_weights(j):
        dst, sem = query_buffer(j), weight_sem.at[j % 4 // 2, j % 2]
        if j < query_tiles:
            return [
                pltpu.make_async_copy(inp.w_query.at[:, pl.ds(j * TILE, TILE)], dst, sem)
            ]
        kv = inp.w_key.shape[1]
        return [
            pltpu.make_async_copy(inp.w_key, dst.at[:, pl.ds(0, kv)], sem),
            pltpu.make_async_copy(inp.w_value, dst.at[:, pl.ds(kv, kv)], scr.last_sem.at[2]),
        ]

    query_width = jobs.outs[3]
    kv_width = jobs.outs[5]
    query_tiles = query_width // TILE
    kv_heads = kv_width // HD
    pairs = query_width // LANES // kv_heads
    score_scale = HD ** (-0.5)

    def lane_masks():
        lane = lax.broadcasted_iota(jnp.int32, (1, LANES), 1)
        first = (lane < HD).astype(jnp.float32)
        return first, 1.0 - first

    def unrotate(value):
        lane = lax.broadcasted_iota(jnp.int32, value.shape, 1)
        other = jnp.where(
            lax.rem(lane, HD) < HD // 2,
            pltpu.roll(value, LANES - HD // 2, 1),
            pltpu.roll(value, HD // 2, 1),
        )
        return value * scr.cosine[...] + other * scr.sine[...]

    def d_attended():
        @pl.loop(0, query_tiles)
        def _(i):
            out_weights(i).wait()
            scr.d_att[:, aligned(i * TILE, TILE)] = against(
                scr.db_full[...], scr.down_w[lax.rem(i, 2)]
            ).astype(jnp.bfloat16)

            @pl.when(i + 2 < query_tiles)
            def _():
                out_weights(i + 2).start()

    def attend_back(kv):
        keys, values = scr.keys.at[kv], scr.values.at[kv]
        keys_acc, values_acc = scr.keys_acc.at[kv], scr.values_acc.at[kv]
        keys_acc[...] = jnp.zeros_like(keys_acc)
        values_acc[...] = jnp.zeros_like(values_acc)

        @pl.loop(0, pairs)
        def _(p):
            columns = aligned((kv * pairs + p) * LANES, LANES)
            d_query = jnp.zeros((tokens, LANES), jnp.float32)
            for lanes in lane_masks():
                lanes_low = lanes.astype(jnp.bfloat16)
                query = scr.query[:, columns] * lanes_low
                d_att = scr.d_att[:, columns] * lanes_low
                scores = against(query, keys[...]) * score_scale
                scores = jnp.where(scr.mask[...] > 0, scores, masked_score)
                expo = jnp.exp(scores - jnp.max(scores, axis=1, keepdims=True))
                probs = expo * (1.0 / jnp.sum(expo, axis=1, keepdims=True))
                d_probs = against(d_att, values[...])
                inner = jnp.sum(probs * d_probs, axis=1, keepdims=True)
                d_scores = (probs * (d_probs - inner)).astype(jnp.bfloat16)
                d_query = d_query + lanes * jnp.dot(
                    d_scores, keys[...], preferred_element_type=jnp.float32
                )
                keys_acc[...] += inner_rows(d_scores, query)
                values_acc[...] += inner_rows(probs.astype(jnp.bfloat16), d_att)
            every[4][pl.ds(0, tokens), columns] = unrotate(d_query * score_scale).astype(
                jnp.bfloat16
            )

    def finish_keys():
        lanes = lane_masks()
        d_key = jnp.zeros((tokens, LANES), jnp.float32)
        d_value = jnp.zeros((tokens, LANES), jnp.float32)
        for kv in range(kv_heads):
            for out in (0, 1):
                acc = (scr.keys_acc, scr.values_acc)[out][kv]
                acc = (acc + pltpu.roll(acc, HD, 1)) * lanes[kv]
                if out == 0:
                    d_key = d_key + acc
                else:
                    d_value = d_value + acc
        d_key = unrotate(d_key * score_scale)
        every[4][pl.ds(0, tokens), pl.ds(query_width, kv_width)] = d_key.astype(jnp.bfloat16)
        every[4][pl.ds(0, tokens), pl.ds(query_width + kv_width, kv_width)] = d_value.astype(
            jnp.bfloat16
        )

    def d_normed_one():
        for j in range(query_tiles + 1):
            for copy in query_weights(j):
                copy.wait()
            weights = query_buffer(j)
            grads = every[4][pl.ds(0, tokens), pl.ds(j * TILE, TILE)]

            @pl.loop(0, width // wide)
            def _(n):
                part = aligned(n * wide, wide)
                add = against(grads, weights[part, :])
                if j == 0:
                    scr.norm_acc[:, part] = add
                else:
                    scr.norm_acc[:, part] += add

            if j + 4 < query_tiles + 1:
                for copy in query_weights(j + 4):
                    copy.start()


    def mean_rows(value):
        return jnp.mean(value, axis=1, keepdims=True)

    def middle_back(row, full):
        grad = scr.norm_acc[full, :] + scr.x_came[0, row, :].astype(jnp.float32)
        middle = scr.middle[row, :]
        scale = lax.rsqrt(mean_rows(middle * middle) + norm_eps)
        normed = middle * scale
        scr.gain_part[0] += eight(grad * normed)
        scaled = grad * inp.mlp_gain[...]
        d_middle = scr.dy[full, :].astype(jnp.float32) + scale * (
            scaled - normed * mean_rows(scaled * normed)
        )
        scr.d_middle[row, :] = d_middle
        scr.db_full[full, :] = d_middle.astype(jnp.bfloat16)

    def finish_layer(row, full):
        mlp = scr.mlp_acc[full, :] + scr.x_came[1, row, :].astype(jnp.float32)
        scr.stage[row, :] = (scr.middle[row, :] + mlp).astype(jnp.bfloat16)

    def token_back(row, full):
        grad = scr.norm_acc[full, :] + scr.x_came[2, row, :].astype(jnp.float32)
        valid = scr.valid[full, :][:, :1]
        masked = scr.tok_full[full, :].astype(jnp.float32) * valid
        scale = lax.rsqrt(mean_rows(masked * masked) + norm_eps)
        normed = masked * scale
        scr.gain_part[1] += eight(grad * normed)
        scaled = grad * inp.attn_gain[...]
        out = scr.d_middle[row, :] + scale * (scaled - normed * mean_rows(scaled * normed))
        scr.stage[row, :] = (out * valid).astype(jnp.bfloat16)

    def gain_copy(i):
        src, dst = scr.gain_all.at[i], scr.gain_came.at[i]
        if i < bits + 2:
            return remote(src, dst, scr.gain_send.at[i], scr.gain_recv.at[i], 1 << i)
        return pltpu.make_async_remote_copy(
            src_ref=src,
            dst_ref=dst,
            send_sem=scr.gain_send.at[i],
            recv_sem=scr.gain_recv.at[i],
            device_id={"tensor": 1 - rank},
            device_id_type=MESH,
        )

    gain_steps = bits + 3

    def gain_next(i):
        gain_copy(i).wait_recv()
        scr.gain_all[i + 1] = scr.gain_all[i] + scr.gain_came[i]
        if i + 1 < gain_steps:
            gain_copy(i + 1).start()


    def prepare():
        ends = []
        for k in range(inp.lengths.shape[0]):
            ends.append(inp.lengths[k] + (ends[-1] if ends else 0))

        def segments(shape, axis):
            place = lax.broadcasted_iota(jnp.int32, shape, axis)
            return place, sum((place >= end).astype(jnp.int32) for end in ends)

        place, _ = segments((tokens, LANES), 0)
        start = jnp.zeros_like(place)
        for end in ends:
            start = jnp.maximum(start, jnp.where(place >= end, end, 0))
        scr.valid[...] = (place < ends[-1]).astype(jnp.float32)
        lane = lax.broadcasted_iota(jnp.int32, (tokens, LANES), 1)
        slow = lax.rem(lane, HD // 2).astype(jnp.float32)
        inverse = jnp.exp(slow * (-2.0 * math.log(10000.0) / HD))
        angles = (place - start).astype(jnp.float32) * inverse
        scr.cosine[...] = jnp.cos(angles)
        sine = jnp.sin(angles)
        scr.sine[...] = jnp.where(lax.rem(lane, HD) < HD // 2, sine, -sine)
        rows_at, row_segment = segments((tokens, tokens), 0)
        columns_at, column_segment = segments((tokens, tokens), 1)
        seen = (row_segment == column_segment) & (columns_at <= rows_at)
        scr.mask[...] = seen.astype(jnp.float32)


    base = jobs.groups[0][1] * TILE

    def query_half(k):
        return every[1].at[pl.ds(0, width // 2), pl.ds(base + k * query_width, query_width)]

    def out_all():
        return every[0].at[pl.ds(0, query_width), pl.ds(base, width)]

    def forward_weights():
        dst = scr.gate_w.at[1]
        copies = [
            pltpu.make_async_copy(
                inp.w_query.at[pl.ds(k * width // 2, width // 2), :],
                query_half(k),
                scr.first_sem.at[k],
            )
            for k in range(2)
        ]
        for k, ref in ((0, inp.w_key), (1, inp.w_value)):
            copies.append(
                pltpu.make_async_copy(
                    ref, dst.at[:, pl.ds(k * kv_width, kv_width)], scr.first_sem.at[2 + k]
                )
            )
        copies.append(pltpu.make_async_copy(inp.w_out, out_all(), scr.first_sem.at[4]))
        return copies

    def all_rows(body):
        @pl.loop(0, tokens // ROWS)
        def _(i):
            body(aligned(i * ROWS, ROWS))

    def first_norm(full):
        masked = scr.tok_full[full, :].astype(jnp.float32) * scr.valid[full, :][:, :1]
        scale = lax.rsqrt(mean_rows(masked * masked) + norm_eps)
        scr.one_full[full, :] = (masked * scale * inp.attn_gain[...]).astype(jnp.bfloat16)

    def mask_cotangent(full):
        dy = scr.dy[full, :].astype(jnp.float32) * scr.valid[full, :][:, :1]
        scr.dy[full, :] = dy.astype(jnp.bfloat16)

    def rotated(value):
        lane = lax.broadcasted_iota(jnp.int32, value.shape, 1)
        other = jnp.where(
            lax.rem(lane, HD) < HD // 2,
            pltpu.roll(value, LANES - HD // 2, 1),
            pltpu.roll(value, HD // 2, 1),
        )
        return value * scr.cosine[...] - other * scr.sine[...]

    def projections():
        middle_at = width // 2

        @pl.loop(0, query_tiles)
        def _(j):
            columns = aligned(j * TILE, TILE)
            out = jnp.dot(
                scr.one_full[:, :middle_at],
                query_half(0)[:, columns],
                preferred_element_type=jnp.float32,
            )
            out = out + jnp.dot(
                scr.one_full[:, middle_at:],
                query_half(1)[:, columns],
                preferred_element_type=jnp.float32,
            )
            for k in range(TILE // LANES):
                part = rotated(out[:, k * LANES : (k + 1) * LANES])
                scr.query[:, aligned(j * TILE + k * LANES, LANES)] = part.astype(jnp.bfloat16)

        out = jnp.dot(scr.one_full[...], scr.gate_w[1], preferred_element_type=jnp.float32)
        lane = lax.broadcasted_iota(jnp.int32, (tokens, LANES), 1)
        for k, ref in ((0, scr.keys), (1, scr.values)):
            part = out[:, k * LANES : (k + 1) * LANES]
            part = rotated(part) if k == 0 else part
            part = part.astype(jnp.bfloat16).astype(jnp.float32)
            turned = pltpu.roll(part, HD, 1)
            ref[0] = jnp.where(lane < HD, part, turned).astype(jnp.bfloat16)
            ref[1] = jnp.where(lane < HD, turned, part).astype(jnp.bfloat16)

    def attend(row):
        for kv in range(kv_heads):

            @pl.loop(0, pairs)
            def _(p):
                columns = aligned((kv * pairs + p) * LANES, LANES)
                out = jnp.zeros((own, LANES), jnp.float32)
                for lanes in lane_masks():
                    query = scr.query[row, columns] * lanes.astype(jnp.bfloat16)
                    scores = against(query, scr.keys[kv]) * score_scale
                    scores = jnp.where(scr.mask[row, :] > 0, scores, masked_score)
                    expo = jnp.exp(scores - jnp.max(scores, axis=1, keepdims=True))
                    probs = expo * (1.0 / jnp.sum(expo, axis=1, keepdims=True))
                    out = out + lanes * jnp.dot(
                        probs.astype(jnp.bfloat16), scr.values[kv], preferred_element_type=jnp.float32
                    )
                every[3][row, columns] = out.astype(jnp.bfloat16)

    def out_rows(row, store):
        @pl.loop(0, width // wide)
        def _(n):
            part = aligned(n * wide, wide)
            store(
                part,
                jnp.dot(
                    every[3][row, :],
                    every[0][pl.ds(0, query_width), pl.ds(pl.multiple_of(base + n * wide, TILE), wide)],
                    preferred_element_type=jnp.float32,
                ),
            )

    def middle_forward(row, full):
        masked = scr.tok_full[full, :].astype(jnp.float32) * scr.valid[full, :][:, :1]
        middle = masked + (scr.norm_acc[row, :] + scr.x_came[0, row, :].astype(jnp.float32))
        scale = lax.rsqrt(mean_rows(middle * middle) + norm_eps)
        scr.middle[row, :] = middle
        scr.two_full[full, :] = (middle * scale * inp.mlp_gain[...]).astype(jnp.bfloat16)


    first_copies = [
        (x_copy(ref, full.at[mine, :], i), pltpu.make_async_copy(ref, full.at[mine, :], local_sem.at[i]))
        for i, (ref, full) in enumerate(((inp.tokens, scr.tok_full), (inp.cotangent, scr.dy)))
    ]
    for copy in first_copies[0]:
        copy.start()
    loads = forward_weights()
    for copy in loads:
        copy.start()
    first_copies[1][1].start()
    prepare()
    first_copies[0][1].wait()
    first_copies[0][0].wait_recv()
    first_copies[1][0].start()
    all_rows(first_norm)
    for copy in loads:
        copy.wait()
    projections()
    theirs = aligned((1 - rank) * own, own)
    attend(theirs)

    def store_theirs(part, out):
        scr.x_sent[0, :, part] = out.astype(jnp.bfloat16)

    def store_mine(part, out):
        scr.norm_acc[pl.ds(0, own), part] = out

    out_rows(theirs, store_theirs)
    branch_copy = x_copy(scr.x_sent.at[0], scr.x_came.at[0], 2)
    branch_copy.start()
    attend(mine)
    out_job = jobs.first_attention
    begin(out_job)
    for copy in hidden_weights(0):
        copy.start()
    out_rows(mine, store_mine)
    first_copies[1][1].wait()
    first_copies[1][0].wait_recv()
    all_rows(mask_cotangent)
    spread(scr.dy, 0)
    branch_copy.wait_recv()
    row_loop(middle_forward)
    two_copy = x_copy(scr.two_full.at[mine, :], scr.two_full.at[mine, :], 3)
    two_copy.start()
    spread(scr.one_full, 3)
    scr.mlp_acc[...] = jnp.zeros_like(scr.mlp_acc)
    scr.norm_acc[...] = jnp.zeros_like(scr.norm_acc)
    scr.gain_part[...] = jnp.zeros_like(scr.gain_part)
    two_copy.wait_recv()
    hidden_part(*jobs.groups[0])
    begin(0)
    begin(1)
    for j in (1, 2, 3):
        feature_copy(0, j).wait_send()
    spread(scr.two_full, 1)
    hidden_part(*jobs.groups[1])
    step(0)
    hidden_part(*jobs.groups[2])
    branch_copy.wait_send()
    send_partial(scr.norm_acc, 0)
    norm_copy = x_copy(scr.x_sent.at[0], scr.x_came.at[0], 4)
    norm_copy.start()
    for i in range(2):
        out_weights(i).start()
    for j in range(4):
        for copy in query_weights(j):
            copy.start()
    send_partial(scr.mlp_acc, 1)
    step(1)
    norm_copy.wait_recv()
    row_loop(middle_back)
    db_copy = x_copy(scr.db_full.at[mine, :], scr.db_full.at[mine, :], 5)
    db_copy.start()
    mlp_copy = x_copy(scr.x_sent.at[1], scr.x_came.at[1], 6)
    step(2)
    for j in (1, 2, 3):
        feature_copy(3, j).wait_send()
    db_copy.wait_recv()
    mlp_copy.start()
    spread(scr.db_full, 2)
    d_attended()
    step(3)
    attend_back(0)
    step(4)
    attend_back(1)
    finish_keys()
    step(5)
    d_normed_one()
    norm_copy.wait_send()
    send_partial(scr.norm_acc, 0)
    one_copy = x_copy(scr.x_sent.at[0], scr.x_came.at[2], 7)
    one_copy.start()
    mlp_copy.wait_recv()
    row_loop(finish_layer)
    layer_copy = pltpu.make_async_copy(scr.stage, layer_out, scr.last_sem.at[0])
    layer_copy.start()
    step(6)
    layer_copy.wait()
    one_copy.wait_recv()
    row_loop(token_back)
    token_copy = pltpu.make_async_copy(scr.stage, token_grad, scr.last_sem.at[1])
    token_copy.start()
    gains = scr.gain_all.at[0]
    gains[...] = jnp.zeros_like(gains)
    for i in range(2):
        gains[pl.ds(i, 1), :] = jnp.sum(scr.gain_part[i], axis=0, keepdims=True)
    gain_copy(0).start()
    at = 7
    for i in range(gain_steps):
        if at < len(plan) - 1:
            step(at)
            at += 1
        gain_next(i)
    gains_copy = pltpu.make_async_copy(
        scr.gain_all.at[gain_steps], gains_out, local_sem.at[1]
    )
    gains_copy.start()
    for t in range(at, len(plan) + bits):
        step(t)


    for copy, _ in first_copies:
        copy.wait_send()
    two_copy.wait_send()
    db_copy.wait_send()
    mlp_copy.wait_send()
    one_copy.wait_send()
    token_copy.wait()
    gains_copy.wait()
    for i in range(gain_steps):
        gain_copy(i).wait_send()
    for f in (1, 2):
        for j in (1, 2, 3):
            feature_copy(f, j).wait_send()
    for t in range(len(plan)):
        for j in (1, 2, 3):
            near(t, j).wait_send()
        if t + ring_sent >= len(plan):
            for s in range(bits):
                far(t, s).wait_send()
        if t + ring_total >= len(plan):
            for copy in outputs(t):
                copy.wait()


def layer_call(jobs, args, tokens, width):
    count = lax.axis_size("dp")
    bits = (count // 4).bit_length() - 1
    rows = width // 4
    block = width // count
    own = tokens // 2
    plan = jobs.plan
    vmem, any_space = pl.BlockSpec(memory_space=pltpu.VMEM), pl.BlockSpec(memory_space=pl.ANY)
    bf16, f32 = jnp.bfloat16, jnp.float32
    late_rows = rows // 2 - (rows // 2 >> (bits - 1))
    ring_total = bits + 2
    kv_heads = jobs.outs[5] // HD
    dma = pltpu.SemaphoreType.DMA
    scratch = Scratch(
        tok_full=pltpu.VMEM((tokens, width), bf16),
        dy=pltpu.VMEM((tokens, width), bf16),
        one_full=pltpu.VMEM((tokens, width), bf16),
        middle=pltpu.VMEM((own, width), f32),
        query=pltpu.VMEM((tokens, jobs.outs[3]), bf16),
        keys=pltpu.VMEM((kv_heads, tokens, LANES), bf16),
        values=pltpu.VMEM((kv_heads, tokens, LANES), bf16),
        mask=pltpu.VMEM((tokens, tokens), f32),
        cosine=pltpu.VMEM((tokens, LANES), f32),
        sine=pltpu.VMEM((tokens, LANES), f32),
        valid=pltpu.VMEM((tokens, LANES), f32),
        source=pltpu.VMEM((2, 4, rows, tokens), bf16),
        sent=pltpu.VMEM((3, rows // 2, jobs.most), bf16),
        came=pltpu.VMEM((RING, rows // 2, jobs.most), bf16),
        sent_late=pltpu.VMEM((3, late_rows, jobs.most), bf16),
        came_late=pltpu.VMEM((RING, late_rows, jobs.most), bf16),
        total=pltpu.VMEM((ring_total, rows // 4, jobs.most), f32),
        gate_w=pltpu.VMEM((2, width, TILE), bf16),
        up_w=pltpu.VMEM((2, width, TILE), bf16),
        down_w=pltpu.VMEM((2, TILE, width), bf16),
        mlp_acc=pltpu.VMEM((tokens, width), f32),
        norm_acc=pltpu.VMEM((tokens, width), f32),
        two_full=pltpu.VMEM((tokens, width), bf16),
        db_full=pltpu.VMEM((tokens, width), bf16),
        x_came=pltpu.VMEM((3, own, width), bf16),
        x_sent=pltpu.VMEM((2, own, width), bf16),
        d_att=pltpu.VMEM((tokens, jobs.outs[3]), bf16),
        d_middle=pltpu.VMEM((own, width), f32),
        stage=pltpu.VMEM((own, width), bf16),
        gain_part=pltpu.VMEM((2, 8, width), f32),
        gain_all=pltpu.VMEM((bits + 4, 8, width), f32),
        gain_came=pltpu.VMEM((bits + 3, 8, width), f32),
        keys_acc=pltpu.VMEM((kv_heads, tokens, LANES), f32),
        values_acc=pltpu.VMEM((kv_heads, tokens, LANES), f32),
        local_sem=dma((2,)),
        feat_send=dma((4, 4)),
        feat_recv=dma((4, 4)),
        near_send=dma((len(plan), 4)),
        near_recv=dma((len(plan), 4)),
        far_send=dma((len(plan), bits)),
        far_recv=dma((len(plan), bits)),
        out_sem=dma((len(plan), jobs.pieces)),
        weight_sem=dma((3, 2)),
        x_send=dma((8,)),
        x_recv=dma((8,)),
        gain_send=dma((bits + 3,)),
        gain_recv=dma((bits + 3,)),
        last_sem=dma((3,)),
        first_sem=dma((5,)),
    )
    operands = [pltpu.VMEM((4 * tokens, w), bf16) for w in jobs.widths]
    operands += [pltpu.VMEM((rows, 4 * tokens), bf16)] * 4
    return pl.pallas_call(
        functools.partial(layer_kernel, jobs, bits),
        out_shape=[jax.ShapeDtypeStruct((block, w), f32) for w in jobs.outs]
        + [
            jax.ShapeDtypeStruct((own, width), bf16),
            jax.ShapeDtypeStruct((own, width), bf16),
            jax.ShapeDtypeStruct((8, width), f32),
        ],
        in_specs=[pl.BlockSpec(memory_space=pltpu.SMEM), vmem, vmem] + [any_space] * (len(args) - 3),
        out_specs=[any_space] * (len(jobs.outs) + 3),
        scratch_shapes=operands + list(scratch),
        compiler_params=pltpu.CompilerParams(
            collective_id=0, has_side_effects=True, vmem_limit_bytes=63 * 1024 * 1024
        ),
    )(*args)


def on_device(
    tokens,
    frag_lengths,
    attn_gain,
    w_query,
    w_key,
    w_value,
    w_out,
    mlp_gain,
    w_gate,
    w_up,
    w_down,
    out_cotangent,
):
    tok_rows, model_width = tokens.shape
    pack_rows = tok_rows * lax.axis_size("tensor")
    rank = lax.axis_index("tensor")
    jobs = Jobs(w_gate.shape[1], w_query.shape[1], w_key.shape[1])
    args = Inputs(
        lengths=frag_lengths,
        attn_gain=attn_gain[None, :],
        mlp_gain=mlp_gain[None, :],
        tokens=tokens,
        cotangent=out_cotangent,
        w_query=w_query,
        w_key=w_key,
        w_value=w_value,
        w_out=w_out,
        w_gate=w_gate,
        w_up=w_up,
        w_down=w_down,
    )
    out = layer_call(jobs, args, pack_rows, model_width)
    down_rows, g_gate, g_up, out_rows, g_query, g_key, g_value, layer_out, token_grad, gains = out
    gain_rows = model_width // (lax.axis_size("tensor") * lax.axis_size("dp"))
    place = (lax.axis_index("dp") * lax.axis_size("tensor") + rank) * gain_rows
    gains = lax.dynamic_slice_in_dim(gains[:2], place, gain_rows, axis=1)
    return (
        layer_out,
        token_grad,
        gains[1],
        g_query,
        g_key,
        g_value,
        out_rows.T,
        gains[0],
        g_gate,
        g_up,
        down_rows.T,
    )


def solution(mesh):
    placed = (
        P(("dp", "tensor"), None),
        P("dp"),
        P(),
        P(None, "tensor"),
        P(None, "tensor"),
        P(None, "tensor"),
        P("tensor", None),
        P(),
        P(None, "tensor"),
        P(None, "tensor"),
        P("tensor", None),
        P(("dp", "tensor"), None),
    )
    return jax.shard_map(
        on_device,
        mesh=mesh,
        in_specs=placed,
        out_specs=(
            P(("dp", "tensor"), None),
            P(("dp", "tensor"), None),
            P(("dp", "tensor")),
            P("dp", "tensor"),
            P("dp", "tensor"),
            P("dp", "tensor"),
            P("tensor", "dp"),
            P(("dp", "tensor")),
            P("dp", "tensor"),
            P("dp", "tensor"),
            P("tensor", "dp"),
        ),
        check_vma=False,
    )
```

```python
import functools
import math
from typing import Any, NamedTuple

import jax
import jax.numpy as jnp
from jax import lax
from jax.experimental import pallas as pl
from jax.experimental.pallas import tpu as pltpu
from jax.sharding import PartitionSpec as P

HD = 64
MESH = pl.DeviceIdType.MESH
TILE = 256
MOST = 1024
LANES = 128
RING = 4
ROWS = 16


norm_eps = 1e-05
masked_score = -1e30


def against(left, right):
    return lax.dot_general(
        left, right, (((1,), (1,)), ((), ())), preferred_element_type=jnp.float32
    )


def inner_rows(left, right):
    return lax.dot_general(
        left, right, (((0,), (0,)), ((), ())), preferred_element_type=jnp.float32
    )


def flip(value, by):
    for step in range(by.bit_length()):
        if by >> step & 1:
            value = value + (1 - 2 * lax.rem(lax.div(value, 2**step), 2)) * 2**step
    return value


def aligned(start, size):
    return pl.ds(pl.multiple_of(start, size), size)


def in_parts(tiles, shares):
    ends = [round(tiles * sum(shares[: i + 1]) / sum(shares)) for i in range(len(shares))]
    return [(start, end - start) for start, end in zip([0] + ends[:-1], ends)]


class Jobs:
    def __init__(self, hidden, query_width, kv_width):
        tiles = hidden // TILE
        self.groups = in_parts(tiles, (1, 2, 2, 3, 3))
        self.plan = []
        for array, feature, shares in (
            (0, 0, (1, 2, 2, 3, 3)),
            (1, 1, (2, 3, 3, 3)),
            (2, 1, (3, 4, 4)),
        ):
            for first, count in in_parts(tiles, shares):
                start, columns = first * TILE, count * TILE
                self.plan.append((array, feature, start, columns, ((array, start, columns),)))
        self.first_attention = len(self.plan)
        self.plan.append((3, 2, 0, query_width, ((3, 0, query_width),)))
        cut = 3 * TILE
        self.plan.append((4, 3, 0, cut, ((4, 0, cut),)))
        rest = query_width - cut
        self.plan.append(
            (4, 3, cut, rest + 2 * kv_width, ((4, cut, rest), (5, 0, kv_width), (6, 0, kv_width)))
        )
        self.widths = [hidden, hidden, hidden, query_width, query_width + 2 * kv_width]
        self.outs = [hidden, hidden, hidden, query_width, query_width, kv_width, kv_width]
        self.most = max(job[3] for job in self.plan)
        self.turned = [t for t, job in enumerate(self.plan) if job[0] in (0, 3)]
        self.pieces = max(len(job[4]) for job in self.plan)


class Inputs(NamedTuple):
    lengths: Any
    attn_gain: Any
    mlp_gain: Any
    tokens: Any
    cotangent: Any
    w_query: Any
    w_key: Any
    w_value: Any
    w_out: Any
    w_gate: Any
    w_up: Any
    w_down: Any


class Scratch(NamedTuple):
    tok_full: Any
    dy: Any
    one_full: Any
    middle: Any
    query: Any
    keys: Any
    values: Any
    mask: Any
    cosine: Any
    sine: Any
    valid: Any
    source: Any
    sent: Any
    came: Any
    sent_late: Any
    came_late: Any
    total: Any
    turned: Any
    gate_w: Any
    up_w: Any
    down_w: Any
    mlp_acc: Any
    norm_acc: Any
    two_full: Any
    db_full: Any
    x_came: Any
    x_sent: Any
    d_att: Any
    d_middle: Any
    stage: Any
    gain_part: Any
    gain_all: Any
    gain_came: Any
    keys_acc: Any
    values_acc: Any
    local_sem: Any
    feat_send: Any
    feat_recv: Any
    near_send: Any
    near_recv: Any
    far_send: Any
    far_recv: Any
    out_sem: Any
    weight_sem: Any
    x_send: Any
    x_recv: Any
    gain_send: Any
    gain_recv: Any
    last_sem: Any
    first_sem: Any


def layer_kernel(jobs, bits, *refs):
    plan = jobs.plan
    inp = Inputs(*refs[: len(Inputs._fields)])
    refs = refs[len(Inputs._fields) :]
    outs = refs[: len(jobs.outs)]
    layer_out, token_grad, gains_out = refs[len(jobs.outs) : len(jobs.outs) + 3]
    refs = refs[len(jobs.outs) + 3 :]
    every, left, scr = refs[:5], refs[5:9], Scratch(*refs[9:])
    sent, came, total = scr.sent, scr.came, scr.total
    sent_late, came_late = scr.sent_late, scr.came_late
    local_sem, near_send, near_recv = scr.local_sem, scr.near_send, scr.near_recv
    tokens, width = scr.dy.shape
    own = tokens // 2
    rows = left[0].shape[0]
    half, quarter = rows // 2, rows // 4
    ring_total = total.shape[0]
    ring_sent = sent.shape[0]

    me = lax.axis_index("dp")
    rank = lax.axis_index("tensor")
    low, high = lax.rem(me, 4), lax.div(me, 4)
    bit = [lax.rem(lax.div(high, 2**s), 2) for s in range(bits)]
    mine = aligned(rank * own, own)

    partners = [1, 2, 3] + [4 << s for s in range(bits)]
    barrier = pltpu.get_barrier_semaphore()
    for by in partners:
        pl.semaphore_signal(barrier, inc=1, device_id={"dp": flip(me, by)}, device_id_type=MESH)
    pl.semaphore_signal(barrier, inc=1, device_id={"tensor": 1 - rank}, device_id_type=MESH)
    pl.semaphore_wait(barrier, len(partners) + 1)

    def remote(src, dst, send, recv, by):
        return pltpu.make_async_remote_copy(
            src_ref=src,
            dst_ref=dst,
            send_sem=send,
            recv_sem=recv,
            device_id={"dp": flip(me, by)},
            device_id_type=MESH,
        )

    def x_copy(src, dst, i):
        return pltpu.make_async_remote_copy(
            src_ref=src,
            dst_ref=dst,
            send_sem=scr.x_send.at[i],
            recv_sem=scr.x_recv.at[i],
            device_id={"tensor": 1 - rank},
            device_id_type=MESH,
        )


    def slot(array, j, start, columns):
        return every[array].at[pl.ds(j * tokens, tokens), pl.ds(start, columns)]

    def near(t, j):
        array, _, start, columns, _ = plan[t]
        src = slot(array, 2 if j == 3 else 0, start, columns)
        dst = slot(array, j, start, columns)
        return remote(src, dst, near_send.at[t, j], near_recv.at[t, j], 2 if j == 2 else 1)

    def stage_rows(s):
        return half - (half >> (s - 1)), quarter >> (s - 1)

    def far(t, s):
        columns = plan[t][3]
        if s == 0:
            src, dst = sent.at[t % ring_sent], came.at[t % RING]
            at = (slice(None), pl.ds(0, columns))
        else:
            src, dst = sent_late.at[t % ring_sent], came_late.at[t % RING]
            at = (pl.ds(*stage_rows(s)), pl.ds(0, columns))
        return remote(
            src.at[at], dst.at[at], scr.far_send.at[t, s], scr.far_recv.at[t, s], 4 << s
        )

    def final_row():
        row = 0
        for s in range(2, bits):
            row = row + bit[s] * (quarter >> (s - 1))
        return row

    last_size = quarter >> (bits - 2)

    def outputs(t):
        copies = []
        done = 0
        for i, (out, first, columns) in enumerate(plan[t][4]):
            if t in jobs.turned:
                src = scr.turned.at[jobs.turned.index(t) % 3].at[pl.ds(done, columns), :]
                dst = outs[out].at[pl.ds(first, columns), :]
                copies.append(pltpu.make_async_copy(src, dst, scr.out_sem.at[t, i]))
                continue
            copies.append(
                pltpu.make_async_copy(
                    total.at[t % ring_total].at[
                        aligned(final_row(), last_size), pl.ds(done, columns)
                    ],
                    outs[out].at[:, pl.ds(first, columns)],
                    scr.out_sem.at[t, i],
                )
            )
            done += columns
        return copies

    def tiles(t, body):
        _, _, start, columns, _ = plan[t]

        @pl.loop(0, columns // TILE)
        def _(i):
            body(aligned(start + i * TILE, TILE), aligned(i * TILE, TILE))

    def dot(t, first, size, at):
        array, f = plan[t][:2]
        return jnp.dot(
            left[f][aligned(first, size), :], every[array][:, at], preferred_element_type=jnp.float32
        )

    def first_pass(t):
        if t >= ring_sent:
            far(t - ring_sent, 0).wait_send()

        def body(at, to):
            out = dot(t, (1 - bit[0]) * half, half, at)
            sent[t % ring_sent, :, to] = out.astype(jnp.bfloat16)

        tiles(t, body)
        far(t, 0).start()

    def second_pass(t):
        far(t, 0).wait_recv()
        if t >= ring_sent:
            far(t - ring_sent, 1).wait_send()
        if t >= ring_total:
            for copy in outputs(t - ring_total):
                copy.wait()
        base = bit[0] * half

        def body(at, to):
            away, kept = (1 - bit[1]) * quarter, bit[1] * quarter
            out = dot(t, base + away, quarter, at)
            out = out + came[t % RING, aligned(away, quarter), to].astype(jnp.float32)
            sent_late[t % ring_sent, pl.ds(0, quarter), to] = out.astype(jnp.bfloat16)
            out = dot(t, base + kept, quarter, at)
            out = out + came[t % RING, aligned(kept, quarter), to].astype(jnp.float32)
            total[t % ring_total, :, to] = out

        tiles(t, body)
        far(t, 1).start()

    def later_pass(t, s):
        far(t, s - 1).wait_recv()
        if t >= ring_sent:
            far(t - ring_sent, s).wait_send()
        first, size = stage_rows(s - 1)
        piece = size // 2
        at_row = 0
        for q in range(2, s):
            at_row = at_row + bit[q] * (quarter >> (q - 1))
        away, kept = (1 - bit[s]) * piece, bit[s] * piece

        def body(at, to):
            out = total[t % ring_total, aligned(at_row + away, piece), to]
            out = out + came_late[t % RING, aligned(first + away, piece), to].astype(jnp.float32)
            sent_late[t % ring_sent, pl.ds(first + size, piece), to] = out.astype(jnp.bfloat16)
            row = aligned(at_row + kept, piece)
            out = total[t % ring_total, row, to]
            out = out + came_late[t % RING, aligned(first + kept, piece), to].astype(jnp.float32)
            total[t % ring_total, row, to] = out

        tiles(t, body)
        far(t, s).start()

    def last_pass(t):
        far(t, bits - 1).wait_recv()
        first, size = stage_rows(bits - 1)

        def body(at, to):
            row = aligned(final_row(), last_size)
            out = total[t % ring_total, row, to]
            out = out + came_late[t % RING, pl.ds(first, size), to].astype(jnp.float32)
            if t in jobs.turned:
                scr.turned[jobs.turned.index(t) % 3, to, :] = out.T
            else:
                total[t % ring_total, row, to] = out

        tiles(t, body)
        for copy in outputs(t):
            copy.start()

    feature_waited = set()

    begun = set()
    ready = [0]

    def begin_to(t):
        for u in range(min(t + 1, ready[0])):
            if u not in begun:
                begun.add(u)
                near(u, 1).start()
                near(u, 2).start()

    def pass_on(t):
        near(t, 2).wait_recv()
        near(t, 3).start()
        begin_to(t + 2)

    def work(t):
        if t < len(plan):
            f = plan[t][1]
            if f not in feature_waited:
                feature_waited.add(f)
                for j in (1, 2, 3):
                    feature_copy(f, j).wait_recv()
            near(t, 1).wait_recv()
            near(t, 3).wait_recv()
            first_pass(t)
        if 0 <= t - 1 < len(plan):
            second_pass(t - 1)
        for s in range(2, bits):
            if 0 <= t - s < len(plan):
                later_pass(t - s, s)
        if 0 <= t - bits < len(plan):
            last_pass(t - bits)

    def step(t):
        if t < len(plan):
            pass_on(t)
        work(t)


    source_of = {0: 0, 3: 1, 1: 0, 2: 1}

    def feature_copy(f, j):
        return remote(
            scr.source.at[source_of[f], flip(low, j)],
            left[f].at[:, pl.ds(j * tokens, tokens)],
            scr.feat_send.at[f, j],
            scr.feat_recv.at[f, j],
            j,
        )

    def turn(ref, f):
        count = 4 << bits
        block = width // count
        source = scr.source.at[source_of[f]]

        @pl.loop(0, width // LANES)
        def _(c):
            turned = ref[:, aligned(c * LANES, LANES)].T
            for piece in range(LANES // block):
                d = c * (LANES // block) + piece
                group = lax.div(d, 4)
                place = 0
                for s in range(bits):
                    place = place + lax.rem(lax.div(group, 2**s), 2) * 2 ** (bits - 1 - s)
                source[lax.rem(d, 4), aligned(place * block, block), :] = turned[
                    piece * block : (piece + 1) * block
                ]

        left[f][:, pl.ds(0, tokens)] = source[low]

    def send_features(f):
        for j in (2, 3, 1):
            feature_copy(f, j).start()


    weight_sem = scr.weight_sem

    def hidden_weights(i):
        at = lax.rem(i, 2)
        columns = aligned(i * TILE, TILE)
        return (
            pltpu.make_async_copy(
                inp.w_gate.at[:, columns], scr.gate_w.at[at], weight_sem.at[0, at]
            ),
            pltpu.make_async_copy(
                inp.w_up.at[:, columns], scr.up_w.at[at], weight_sem.at[1, at]
            ),
            pltpu.make_async_copy(
                inp.w_down.at[columns, :], scr.down_w.at[at], weight_sem.at[2, at]
            ),
        )

    hidden_tiles = jobs.outs[0] // TILE
    wide = 512

    def hidden_part(first, count):
        @pl.loop(first, first + count)
        def _(i):
            at = lax.rem(i, 2)

            @pl.when(i + 1 < hidden_tiles)
            def _():
                for copy in hidden_weights(i + 1):
                    copy.start()

            for copy in hidden_weights(i):
                copy.wait()
            gate_w, up_w, down_w = scr.gate_w.at[at], scr.up_w.at[at], scr.down_w.at[at]
            two = scr.two_full[...]
            gate = jnp.dot(two, gate_w[...], preferred_element_type=jnp.float32)
            up = jnp.dot(two, up_w[...], preferred_element_type=jnp.float32)
            d_act = against(scr.dy[...], down_w[...])
            sig = jax.nn.sigmoid(gate)
            silu = gate * sig
            act = (silu * up).astype(jnp.bfloat16)
            d_gate = (d_act * up * sig * (1.0 + gate * (1.0 - sig))).astype(jnp.bfloat16)
            d_up = (d_act * silu).astype(jnp.bfloat16)
            columns = aligned(i * TILE, TILE)
            every[0][pl.ds(0, tokens), columns] = act
            every[1][pl.ds(0, tokens), columns] = d_gate
            every[2][pl.ds(0, tokens), columns] = d_up

            @pl.loop(0, width // wide)
            def _(n):
                part = aligned(n * wide, wide)
                scr.mlp_acc[:, part] += jnp.dot(
                    act, down_w[:, part], preferred_element_type=jnp.float32
                )
                scr.norm_acc[:, part] += against(d_gate, gate_w[part, :]) + against(
                    d_up, up_w[part, :]
                )

    def row_loop(body):
        @pl.loop(0, own // ROWS)
        def _(i):
            body(aligned(i * ROWS, ROWS), aligned(rank * own + i * ROWS, ROWS))

    def eight(value):
        return jnp.sum(value.reshape(ROWS // 8, 8, width), axis=0)

    def send_partial(acc, buffer):
        @pl.loop(0, own // ROWS)
        def _(i):
            row = aligned((1 - rank) * own + i * ROWS, ROWS)
            scr.x_sent[buffer, aligned(i * ROWS, ROWS), :] = acc[row, :].astype(
                jnp.bfloat16
            )


    def out_weights(i):
        return pltpu.make_async_copy(
            inp.w_out.at[aligned(i * TILE, TILE), :],
            scr.down_w.at[lax.rem(i, 2)],
            weight_sem.at[2, lax.rem(i, 2)],
        )

    def query_buffer(j):
        return (scr.gate_w, scr.up_w)[j % 4 // 2].at[j % 2]

    def query_weights(j):
        dst, sem = query_buffer(j), weight_sem.at[j % 4 // 2, j % 2]
        if j < query_tiles:
            return [
                pltpu.make_async_copy(inp.w_query.at[:, pl.ds(j * TILE, TILE)], dst, sem)
            ]
        kv = inp.w_key.shape[1]
        return [
            pltpu.make_async_copy(inp.w_key, dst.at[:, pl.ds(0, kv)], sem),
            pltpu.make_async_copy(inp.w_value, dst.at[:, pl.ds(kv, kv)], scr.last_sem.at[2]),
        ]

    query_width = jobs.outs[3]
    kv_width = jobs.outs[5]
    query_tiles = query_width // TILE
    kv_heads = kv_width // HD
    pairs = query_width // LANES // kv_heads
    score_scale = HD ** (-0.5)

    def lane_masks():
        lane = lax.broadcasted_iota(jnp.int32, (1, LANES), 1)
        first = (lane < HD).astype(jnp.float32)
        return first, 1.0 - first

    def unrotate(value):
        lane = lax.broadcasted_iota(jnp.int32, value.shape, 1)
        other = jnp.where(
            lax.rem(lane, HD) < HD // 2,
            pltpu.roll(value, LANES - HD // 2, 1),
            pltpu.roll(value, HD // 2, 1),
        )
        return value * scr.cosine[...] + other * scr.sine[...]

    def d_attended():
        @pl.loop(0, query_tiles)
        def _(i):
            out_weights(i).wait()
            scr.d_att[:, aligned(i * TILE, TILE)] = against(
                scr.db_full[...], scr.down_w[lax.rem(i, 2)]
            ).astype(jnp.bfloat16)

            @pl.when(i + 2 < query_tiles)
            def _():
                out_weights(i + 2).start()

    def attend_back(kv):
        keys, values = scr.keys.at[kv], scr.values.at[kv]
        keys_acc, values_acc = scr.keys_acc.at[kv], scr.values_acc.at[kv]
        keys_acc[...] = jnp.zeros_like(keys_acc)
        values_acc[...] = jnp.zeros_like(values_acc)

        @pl.loop(0, pairs)
        def _(p):
            columns = aligned((kv * pairs + p) * LANES, LANES)
            d_query = jnp.zeros((tokens, LANES), jnp.float32)
            for lanes in lane_masks():
                lanes_low = lanes.astype(jnp.bfloat16)
                query = scr.query[:, columns] * lanes_low
                d_att = scr.d_att[:, columns] * lanes_low
                scores = against(query, keys[...]) * score_scale
                scores = jnp.where(scr.mask[...] > 0, scores, masked_score)
                expo = jnp.exp(scores - jnp.max(scores, axis=1, keepdims=True))
                probs = expo * (1.0 / jnp.sum(expo, axis=1, keepdims=True))
                d_probs = against(d_att, values[...])
                inner = jnp.sum(probs * d_probs, axis=1, keepdims=True)
                d_scores = (probs * (d_probs - inner)).astype(jnp.bfloat16)
                d_query = d_query + lanes * jnp.dot(
                    d_scores, keys[...], preferred_element_type=jnp.float32
                )
                keys_acc[...] += inner_rows(d_scores, query)
                values_acc[...] += inner_rows(probs.astype(jnp.bfloat16), d_att)
            every[4][pl.ds(0, tokens), columns] = unrotate(d_query * score_scale).astype(
                jnp.bfloat16
            )

    def finish_keys():
        lanes = lane_masks()
        d_key = jnp.zeros((tokens, LANES), jnp.float32)
        d_value = jnp.zeros((tokens, LANES), jnp.float32)
        for kv in range(kv_heads):
            for out in (0, 1):
                acc = (scr.keys_acc, scr.values_acc)[out][kv]
                acc = (acc + pltpu.roll(acc, HD, 1)) * lanes[kv]
                if out == 0:
                    d_key = d_key + acc
                else:
                    d_value = d_value + acc
        d_key = unrotate(d_key * score_scale)
        every[4][pl.ds(0, tokens), pl.ds(query_width, kv_width)] = d_key.astype(jnp.bfloat16)
        every[4][pl.ds(0, tokens), pl.ds(query_width + kv_width, kv_width)] = d_value.astype(
            jnp.bfloat16
        )

    def d_normed_one():
        for j in range(query_tiles + 1):
            for copy in query_weights(j):
                copy.wait()
            weights = query_buffer(j)
            grads = every[4][pl.ds(0, tokens), pl.ds(j * TILE, TILE)]

            @pl.loop(0, width // wide)
            def _(n):
                part = aligned(n * wide, wide)
                add = against(grads, weights[part, :])
                if j == 0:
                    scr.norm_acc[:, part] = add
                else:
                    scr.norm_acc[:, part] += add

            if j + 4 < query_tiles + 1:
                for copy in query_weights(j + 4):
                    copy.start()


    def mean_rows(value):
        return jnp.mean(value, axis=1, keepdims=True)

    def middle_back(row, full):
        grad = scr.norm_acc[full, :] + scr.x_came[0, row, :].astype(jnp.float32)
        middle = scr.middle[row, :]
        scale = lax.rsqrt(mean_rows(middle * middle) + norm_eps)
        normed = middle * scale
        scr.gain_part[0] += eight(grad * normed)
        scaled = grad * inp.mlp_gain[...]
        d_middle = scr.dy[full, :].astype(jnp.float32) + scale * (
            scaled - normed * mean_rows(scaled * normed)
        )
        scr.d_middle[row, :] = d_middle
        scr.db_full[full, :] = d_middle.astype(jnp.bfloat16)

    def finish_layer(row, full):
        mlp = scr.mlp_acc[full, :] + scr.x_came[1, row, :].astype(jnp.float32)
        scr.stage[row, :] = (scr.middle[row, :] + mlp).astype(jnp.bfloat16)

    def token_back(row, full):
        grad = scr.norm_acc[full, :] + scr.x_came[2, row, :].astype(jnp.float32)
        valid = scr.valid[full, :][:, :1]
        masked = scr.tok_full[full, :].astype(jnp.float32) * valid
        scale = lax.rsqrt(mean_rows(masked * masked) + norm_eps)
        normed = masked * scale
        scr.gain_part[1] += eight(grad * normed)
        scaled = grad * inp.attn_gain[...]
        out = scr.d_middle[row, :] + scale * (scaled - normed * mean_rows(scaled * normed))
        scr.stage[row, :] = (out * valid).astype(jnp.bfloat16)

    def gain_copy(i):
        src, dst = scr.gain_all.at[i], scr.gain_came.at[i]
        if i < bits + 2:
            return remote(src, dst, scr.gain_send.at[i], scr.gain_recv.at[i], 1 << i)
        return pltpu.make_async_remote_copy(
            src_ref=src,
            dst_ref=dst,
            send_sem=scr.gain_send.at[i],
            recv_sem=scr.gain_recv.at[i],
            device_id={"tensor": 1 - rank},
            device_id_type=MESH,
        )

    gain_steps = bits + 3

    def gain_next(i):
        gain_copy(i).wait_recv()
        scr.gain_all[i + 1] = scr.gain_all[i] + scr.gain_came[i]
        if i + 1 < gain_steps:
            gain_copy(i + 1).start()


    def prepare():
        ends = []
        for k in range(inp.lengths.shape[0]):
            ends.append(inp.lengths[k] + (ends[-1] if ends else 0))

        def segments(shape, axis):
            place = lax.broadcasted_iota(jnp.int32, shape, axis)
            return place, sum((place >= end).astype(jnp.int32) for end in ends)

        place, _ = segments((tokens, LANES), 0)
        start = jnp.zeros_like(place)
        for end in ends:
            start = jnp.maximum(start, jnp.where(place >= end, end, 0))
        scr.valid[...] = (place < ends[-1]).astype(jnp.float32)
        lane = lax.broadcasted_iota(jnp.int32, (tokens, LANES), 1)
        slow = lax.rem(lane, HD // 2).astype(jnp.float32)
        inverse = jnp.exp(slow * (-2.0 * math.log(10000.0) / HD))
        angles = (place - start).astype(jnp.float32) * inverse
        scr.cosine[...] = jnp.cos(angles)
        sine = jnp.sin(angles)
        scr.sine[...] = jnp.where(lax.rem(lane, HD) < HD // 2, sine, -sine)
        rows_at, row_segment = segments((tokens, tokens), 0)
        columns_at, column_segment = segments((tokens, tokens), 1)
        seen = (row_segment == column_segment) & (columns_at <= rows_at)
        scr.mask[...] = seen.astype(jnp.float32)


    def query_half(k):
        return every[2].at[pl.ds(0, width // 2), pl.ds(k * query_width, query_width)]

    def out_all():
        return every[1].at[pl.ds(0, query_width), pl.ds(0, width)]

    def forward_weights():
        dst = scr.gate_w.at[1]
        copies = [
            pltpu.make_async_copy(
                inp.w_query.at[pl.ds(k * width // 2, width // 2), :],
                query_half(k),
                scr.first_sem.at[k],
            )
            for k in range(2)
        ]
        for k, ref in ((0, inp.w_key), (1, inp.w_value)):
            copies.append(
                pltpu.make_async_copy(
                    ref, dst.at[:, pl.ds(k * kv_width, kv_width)], scr.first_sem.at[2 + k]
                )
            )
        copies.append(pltpu.make_async_copy(inp.w_out, out_all(), scr.first_sem.at[4]))
        return copies

    def all_rows(body):
        @pl.loop(0, tokens // ROWS)
        def _(i):
            body(aligned(i * ROWS, ROWS))

    def first_norm(full):
        masked = scr.tok_full[full, :].astype(jnp.float32) * scr.valid[full, :][:, :1]
        scale = lax.rsqrt(mean_rows(masked * masked) + norm_eps)
        scr.one_full[full, :] = (masked * scale * inp.attn_gain[...]).astype(jnp.bfloat16)

    def mask_cotangent(full):
        dy = scr.dy[full, :].astype(jnp.float32) * scr.valid[full, :][:, :1]
        scr.dy[full, :] = dy.astype(jnp.bfloat16)

    def rotated(value):
        lane = lax.broadcasted_iota(jnp.int32, value.shape, 1)
        other = jnp.where(
            lax.rem(lane, HD) < HD // 2,
            pltpu.roll(value, LANES - HD // 2, 1),
            pltpu.roll(value, HD // 2, 1),
        )
        return value * scr.cosine[...] - other * scr.sine[...]

    def projections():
        middle_at = width // 2

        @pl.loop(0, query_tiles)
        def _(j):
            columns = aligned(j * TILE, TILE)
            out = jnp.dot(
                scr.one_full[:, :middle_at],
                query_half(0)[:, columns],
                preferred_element_type=jnp.float32,
            )
            out = out + jnp.dot(
                scr.one_full[:, middle_at:],
                query_half(1)[:, columns],
                preferred_element_type=jnp.float32,
            )
            for k in range(TILE // LANES):
                part = rotated(out[:, k * LANES : (k + 1) * LANES])
                scr.query[:, aligned(j * TILE + k * LANES, LANES)] = part.astype(jnp.bfloat16)

        out = jnp.dot(scr.one_full[...], scr.gate_w[1], preferred_element_type=jnp.float32)
        lane = lax.broadcasted_iota(jnp.int32, (tokens, LANES), 1)
        for k, ref in ((0, scr.keys), (1, scr.values)):
            part = out[:, k * LANES : (k + 1) * LANES]
            part = rotated(part) if k == 0 else part
            part = part.astype(jnp.bfloat16).astype(jnp.float32)
            turned = pltpu.roll(part, HD, 1)
            ref[0] = jnp.where(lane < HD, part, turned).astype(jnp.bfloat16)
            ref[1] = jnp.where(lane < HD, turned, part).astype(jnp.bfloat16)

    def attend(row):
        for kv in range(kv_heads):

            @pl.loop(0, pairs)
            def _(p):
                columns = aligned((kv * pairs + p) * LANES, LANES)
                out = jnp.zeros((own, LANES), jnp.float32)
                for lanes in lane_masks():
                    query = scr.query[row, columns] * lanes.astype(jnp.bfloat16)
                    scores = against(query, scr.keys[kv]) * score_scale
                    scores = jnp.where(scr.mask[row, :] > 0, scores, masked_score)
                    expo = jnp.exp(scores - jnp.max(scores, axis=1, keepdims=True))
                    probs = expo * (1.0 / jnp.sum(expo, axis=1, keepdims=True))
                    out = out + lanes * jnp.dot(
                        probs.astype(jnp.bfloat16), scr.values[kv], preferred_element_type=jnp.float32
                    )
                every[3][row, columns] = out.astype(jnp.bfloat16)

    def out_rows(row, store):
        @pl.loop(0, width // wide)
        def _(n):
            part = aligned(n * wide, wide)
            store(
                part,
                jnp.dot(
                    every[3][row, :],
                    every[1][pl.ds(0, query_width), part],
                    preferred_element_type=jnp.float32,
                ),
            )

    def middle_forward(row, full):
        masked = scr.tok_full[full, :].astype(jnp.float32) * scr.valid[full, :][:, :1]
        middle = masked + (scr.norm_acc[row, :] + scr.x_came[0, row, :].astype(jnp.float32))
        scale = lax.rsqrt(mean_rows(middle * middle) + norm_eps)
        scr.middle[row, :] = middle
        scr.two_full[full, :] = (middle * scale * inp.mlp_gain[...]).astype(jnp.bfloat16)


    first_copies = [
        (x_copy(ref, full.at[mine, :], i), pltpu.make_async_copy(ref, full.at[mine, :], local_sem.at[i]))
        for i, (ref, full) in enumerate(((inp.tokens, scr.tok_full), (inp.cotangent, scr.dy)))
    ]
    for copy in first_copies[0]:
        copy.start()
    loads = forward_weights()
    for copy in loads:
        copy.start()
    first_copies[1][1].start()
    prepare()
    first_copies[0][1].wait()
    first_copies[0][0].wait_recv()
    first_copies[1][0].start()
    all_rows(first_norm)
    for copy in loads:
        copy.wait()
    projections()
    theirs = aligned((1 - rank) * own, own)
    attend(theirs)

    def store_theirs(part, out):
        scr.x_sent[0, :, part] = out.astype(jnp.bfloat16)

    def store_mine(part, out):
        scr.norm_acc[pl.ds(0, own), part] = out

    out_rows(theirs, store_theirs)
    branch_copy = x_copy(scr.x_sent.at[0], scr.x_came.at[0], 2)
    branch_copy.start()
    first_copies[1][1].wait()
    first_copies[1][0].wait_recv()
    all_rows(mask_cotangent)
    turn(scr.dy, 0)
    send_features(0)
    turn(scr.one_full, 3)
    send_features(3)
    attend(mine)
    for copy in hidden_weights(0):
        copy.start()
    out_rows(mine, store_mine)
    branch_copy.wait_recv()
    row_loop(middle_forward)
    two_copy = x_copy(scr.two_full.at[mine, :], scr.two_full.at[mine, :], 3)
    two_copy.start()
    scr.mlp_acc[...] = jnp.zeros_like(scr.mlp_acc)
    scr.norm_acc[...] = jnp.zeros_like(scr.norm_acc)
    scr.gain_part[...] = jnp.zeros_like(scr.gain_part)
    two_copy.wait_recv()
    done = 0
    for part, (first, count) in enumerate(jobs.groups):
        if part >= 2:
            hidden_part(first, count - 1)
            pass_on(part - 2)
            hidden_part(first + count - 1, 1)
        else:
            hidden_part(first, count)
        ready[0] = part + 1
        begin_to(part)
        if part >= 2:
            work(part - 2)
    at = len(jobs.groups) - 2
    branch_copy.wait_send()
    send_partial(scr.norm_acc, 0)
    norm_copy = x_copy(scr.x_sent.at[0], scr.x_came.at[0], 4)
    norm_copy.start()
    for i in range(2):
        out_weights(i).start()
    for j in range(4):
        for copy in query_weights(j):
            copy.start()
    for j in (1, 2, 3):
        feature_copy(0, j).wait_send()
    turn(scr.two_full, 1)
    pass_on(at)
    send_features(1)
    work(at)
    send_partial(scr.mlp_acc, 1)
    ready[0] = jobs.first_attention + 1
    step(at + 1)
    norm_copy.wait_recv()
    row_loop(middle_back)
    db_copy = x_copy(scr.db_full.at[mine, :], scr.db_full.at[mine, :], 5)
    db_copy.start()
    mlp_copy = x_copy(scr.x_sent.at[1], scr.x_came.at[1], 6)
    step(at + 2)
    for j in (1, 2, 3):
        feature_copy(3, j).wait_send()
    db_copy.wait_recv()
    mlp_copy.start()
    turn(scr.db_full, 2)
    d_attended()
    step(at + 3)
    attend_back(0)
    step(at + 4)
    attend_back(1)
    finish_keys()
    ready[0] = len(plan)
    step(at + 5)
    send_features(2)
    d_normed_one()
    norm_copy.wait_send()
    send_partial(scr.norm_acc, 0)
    one_copy = x_copy(scr.x_sent.at[0], scr.x_came.at[2], 7)
    one_copy.start()
    mlp_copy.wait_recv()
    row_loop(finish_layer)
    layer_copy = pltpu.make_async_copy(scr.stage, layer_out, scr.last_sem.at[0])
    layer_copy.start()
    step(at + 6)
    layer_copy.wait()
    one_copy.wait_recv()
    row_loop(token_back)
    token_copy = pltpu.make_async_copy(scr.stage, token_grad, scr.last_sem.at[1])
    token_copy.start()
    gains = scr.gain_all.at[0]
    gains[...] = jnp.zeros_like(gains)
    for i in range(2):
        gains[pl.ds(i, 1), :] = jnp.sum(scr.gain_part[i], axis=0, keepdims=True)
    gain_copy(0).start()
    at = at + 7
    for i in range(gain_steps):
        if at < len(plan):
            step(at)
            at += 1
        gain_next(i)
    gains_copy = pltpu.make_async_copy(scr.gain_all.at[gain_steps], gains_out, local_sem.at[1])
    gains_copy.start()
    for t in range(at, len(plan) + bits):
        step(t)


    for copy, _ in first_copies:
        copy.wait_send()
    two_copy.wait_send()
    db_copy.wait_send()
    mlp_copy.wait_send()
    one_copy.wait_send()
    token_copy.wait()
    gains_copy.wait()
    for i in range(gain_steps):
        gain_copy(i).wait_send()
    for f in (1, 2):
        for j in (1, 2, 3):
            feature_copy(f, j).wait_send()
    for t in range(len(plan)):
        for j in (1, 2, 3):
            near(t, j).wait_send()
        if t + ring_sent >= len(plan):
            for s in range(bits):
                far(t, s).wait_send()
        if t + ring_total >= len(plan):
            for copy in outputs(t):
                copy.wait()


def layer_call(jobs, args, tokens, width):
    count = lax.axis_size("dp")
    bits = (count // 4).bit_length() - 1
    rows = width // 4
    block = width // count
    own = tokens // 2
    plan = jobs.plan
    vmem, any_space = pl.BlockSpec(memory_space=pltpu.VMEM), pl.BlockSpec(memory_space=pl.ANY)
    bf16, f32 = jnp.bfloat16, jnp.float32
    late_rows = rows // 2 - (rows // 2 >> (bits - 1))
    ring_total = max(4, bits + 1)
    kv_heads = jobs.outs[5] // HD
    dma = pltpu.SemaphoreType.DMA
    scratch = Scratch(
        tok_full=pltpu.VMEM((tokens, width), bf16),
        dy=pltpu.VMEM((tokens, width), bf16),
        one_full=pltpu.VMEM((tokens, width), bf16),
        middle=pltpu.VMEM((own, width), f32),
        query=pltpu.VMEM((tokens, jobs.outs[3]), bf16),
        keys=pltpu.VMEM((kv_heads, tokens, LANES), bf16),
        values=pltpu.VMEM((kv_heads, tokens, LANES), bf16),
        mask=pltpu.VMEM((tokens, tokens), f32),
        cosine=pltpu.VMEM((tokens, LANES), f32),
        sine=pltpu.VMEM((tokens, LANES), f32),
        valid=pltpu.VMEM((tokens, LANES), f32),
        source=pltpu.VMEM((2, 4, rows, tokens), bf16),
        sent=pltpu.VMEM((3, rows // 2, jobs.most), bf16),
        came=pltpu.VMEM((RING, rows // 2, jobs.most), bf16),
        sent_late=pltpu.VMEM((3, late_rows, jobs.most), bf16),
        came_late=pltpu.VMEM((RING, late_rows, jobs.most), bf16),
        total=pltpu.VMEM((ring_total, rows // 4, jobs.most), f32),
        turned=pltpu.VMEM((3, jobs.most, block), f32),
        gate_w=pltpu.VMEM((2, width, TILE), bf16),
        up_w=pltpu.VMEM((2, width, TILE), bf16),
        down_w=pltpu.VMEM((2, TILE, width), bf16),
        mlp_acc=pltpu.VMEM((tokens, width), f32),
        norm_acc=pltpu.VMEM((tokens, width), f32),
        two_full=pltpu.VMEM((tokens, width), bf16),
        db_full=pltpu.VMEM((tokens, width), bf16),
        x_came=pltpu.VMEM((3, own, width), bf16),
        x_sent=pltpu.VMEM((2, own, width), bf16),
        d_att=pltpu.VMEM((tokens, jobs.outs[3]), bf16),
        d_middle=pltpu.VMEM((own, width), f32),
        stage=pltpu.VMEM((own, width), bf16),
        gain_part=pltpu.VMEM((2, 8, width), f32),
        gain_all=pltpu.VMEM((bits + 4, 8, width), f32),
        gain_came=pltpu.VMEM((bits + 3, 8, width), f32),
        keys_acc=pltpu.VMEM((kv_heads, tokens, LANES), f32),
        values_acc=pltpu.VMEM((kv_heads, tokens, LANES), f32),
        local_sem=dma((2,)),
        feat_send=dma((4, 4)),
        feat_recv=dma((4, 4)),
        near_send=dma((len(plan), 4)),
        near_recv=dma((len(plan), 4)),
        far_send=dma((len(plan), bits)),
        far_recv=dma((len(plan), bits)),
        out_sem=dma((len(plan), jobs.pieces)),
        weight_sem=dma((3, 2)),
        x_send=dma((8,)),
        x_recv=dma((8,)),
        gain_send=dma((bits + 3,)),
        gain_recv=dma((bits + 3,)),
        last_sem=dma((3,)),
        first_sem=dma((5,)),
    )
    operands = [pltpu.VMEM((4 * tokens, w), bf16) for w in jobs.widths]
    operands += [pltpu.VMEM((rows, 4 * tokens), bf16)] * 4
    return pl.pallas_call(
        functools.partial(layer_kernel, jobs, bits),
        out_shape=[
            jax.ShapeDtypeStruct((w, block) if i in (0, 3) else (block, w), f32)
            for i, w in enumerate(jobs.outs)
        ]
        + [
            jax.ShapeDtypeStruct((own, width), bf16),
            jax.ShapeDtypeStruct((own, width), bf16),
            jax.ShapeDtypeStruct((8, width), f32),
        ],
        in_specs=[pl.BlockSpec(memory_space=pltpu.SMEM), vmem, vmem] + [any_space] * (len(args) - 3),
        out_specs=[any_space] * (len(jobs.outs) + 3),
        scratch_shapes=operands + list(scratch),
        compiler_params=pltpu.CompilerParams(
            collective_id=0, has_side_effects=True, vmem_limit_bytes=63 * 1024 * 1024
        ),
    )(*args)


def on_device(
    tokens,
    frag_lengths,
    attn_gain,
    w_query,
    w_key,
    w_value,
    w_out,
    mlp_gain,
    w_gate,
    w_up,
    w_down,
    out_cotangent,
):
    tok_rows, model_width = tokens.shape
    pack_rows = tok_rows * lax.axis_size("tensor")
    rank = lax.axis_index("tensor")
    jobs = Jobs(w_gate.shape[1], w_query.shape[1], w_key.shape[1])
    args = Inputs(
        lengths=frag_lengths,
        attn_gain=attn_gain[None, :],
        mlp_gain=mlp_gain[None, :],
        tokens=tokens,
        cotangent=out_cotangent,
        w_query=w_query,
        w_key=w_key,
        w_value=w_value,
        w_out=w_out,
        w_gate=w_gate,
        w_up=w_up,
        w_down=w_down,
    )
    out = layer_call(jobs, args, pack_rows, model_width)
    down_rows, g_gate, g_up, out_rows, g_query, g_key, g_value, layer_out, token_grad, gains = out
    gain_rows = model_width // (lax.axis_size("tensor") * lax.axis_size("dp"))
    place = (lax.axis_index("dp") * lax.axis_size("tensor") + rank) * gain_rows
    gains = lax.dynamic_slice_in_dim(gains[:2], place, gain_rows, axis=1)
    return (
        layer_out,
        token_grad,
        gains[1],
        g_query,
        g_key,
        g_value,
        out_rows,
        gains[0],
        g_gate,
        g_up,
        down_rows,
    )


def solution(mesh):
    placed = (
        P(("dp", "tensor"), None),
        P("dp"),
        P(),
        P(None, "tensor"),
        P(None, "tensor"),
        P(None, "tensor"),
        P("tensor", None),
        P(),
        P(None, "tensor"),
        P(None, "tensor"),
        P("tensor", None),
        P(("dp", "tensor"), None),
    )
    return jax.shard_map(
        on_device,
        mesh=mesh,
        in_specs=placed,
        out_specs=(
            P(("dp", "tensor"), None),
            P(("dp", "tensor"), None),
            P(("dp", "tensor")),
            P("dp", "tensor"),
            P("dp", "tensor"),
            P("dp", "tensor"),
            P("tensor", "dp"),
            P(("dp", "tensor")),
            P("dp", "tensor"),
            P("dp", "tensor"),
            P("tensor", "dp"),
        ),
        check_vma=False,
    )
```

```python
import functools
import math
from typing import Any, NamedTuple

import jax
import jax.numpy as jnp
from jax import lax
from jax.experimental import pallas as pl
from jax.experimental.pallas import tpu as pltpu
from jax.sharding import PartitionSpec as P

HD = 64
MESH = pl.DeviceIdType.MESH
TILE = 256
MOST = 1024
LANES = 128
RING = 4
ROWS = 16


norm_eps = 1e-05
masked_score = -1e30


def against(left, right):
    return lax.dot_general(
        left, right, (((1,), (1,)), ((), ())), preferred_element_type=jnp.float32
    )


def inner_rows(left, right):
    return lax.dot_general(
        left, right, (((0,), (0,)), ((), ())), preferred_element_type=jnp.float32
    )


def flip(value, by):
    for step in range(by.bit_length()):
        if by >> step & 1:
            value = value + (1 - 2 * lax.rem(lax.div(value, 2**step), 2)) * 2**step
    return value


def aligned(start, size):
    return pl.ds(pl.multiple_of(start, size), size)


def in_parts(tiles, shares):
    ends = [round(tiles * sum(shares[: i + 1]) / sum(shares)) for i in range(len(shares))]
    return [(start, end - start) for start, end in zip([0] + ends[:-1], ends)]


class Jobs:
    def __init__(self, hidden, query_width, kv_width):
        tiles = hidden // TILE
        self.groups = in_parts(tiles, (1, 2, 2, 3, 3))
        self.plan = []
        for first, count in self.groups:
            self.plan.append((0, 0, first * LANES, count * LANES, ()))
        self.halved = len(self.plan)
        for array, feature, shares in ((1, 1, (2, 3, 3, 3)), (2, 1, (3, 4, 4))):
            for first, count in in_parts(tiles, shares):
                start, columns = first * TILE, count * TILE
                self.plan.append((array, feature, start, columns, ((array, start, columns),)))
        self.first_attention = len(self.plan)
        self.plan.append((3, 2, 0, query_width, ((3, 0, query_width),)))
        cut = 3 * TILE
        self.plan.append((4, 3, 0, cut, ((4, 0, cut),)))
        rest = query_width - cut
        self.plan.append(
            (4, 3, cut, rest + 2 * kv_width, ((4, cut, rest), (5, 0, kv_width), (6, 0, kv_width)))
        )
        self.widths = [hidden, hidden, hidden, query_width, query_width + 2 * kv_width]
        self.outs = [hidden, hidden, hidden, query_width, query_width, kv_width, kv_width]
        self.most = max(job[3] for job in self.plan)
        self.turned = [t for t, job in enumerate(self.plan) if job[0] in (0, 3)]
        self.most_halved = max(job[3] for job in self.plan[: self.halved])
        self.pieces = 3


class Inputs(NamedTuple):
    lengths: Any
    attn_gain: Any
    mlp_gain: Any
    tokens: Any
    cotangent: Any
    w_query: Any
    w_key: Any
    w_value: Any
    w_out: Any
    w_gate: Any
    w_up: Any
    w_down: Any


class Scratch(NamedTuple):
    tok_full: Any
    dy: Any
    one_full: Any
    middle: Any
    query: Any
    keys: Any
    values: Any
    mask: Any
    cosine: Any
    sine: Any
    valid: Any
    source: Any
    sent: Any
    came: Any
    sent_late: Any
    came_late: Any
    total: Any
    turned: Any
    gate_w: Any
    up_w: Any
    down_w: Any
    mlp_acc: Any
    norm_acc: Any
    two_full: Any
    x_came: Any
    x_sent: Any
    d_att: Any
    gain_part: Any
    gain_all: Any
    gain_came: Any
    gain_own: Any
    pair_sent: Any
    pair_came: Any
    pair_send: Any
    pair_recv: Any
    keys_acc: Any
    values_acc: Any
    local_sem: Any
    feat_send: Any
    feat_recv: Any
    near_send: Any
    near_recv: Any
    far_send: Any
    far_recv: Any
    out_sem: Any
    weight_sem: Any
    x_send: Any
    x_recv: Any
    gain_send: Any
    gain_recv: Any
    last_sem: Any
    first_sem: Any


def layer_kernel(jobs, bits, *refs):
    plan = jobs.plan
    inp = Inputs(*refs[: len(Inputs._fields)])
    refs = refs[len(Inputs._fields) :]
    outs = refs[: len(jobs.outs)]
    layer_out, token_grad, gains_out = refs[len(jobs.outs) : len(jobs.outs) + 3]
    refs = refs[len(jobs.outs) + 3 :]
    every, left, scr = refs[:5], refs[5:9], Scratch(*refs[9:])
    sent, came, total = scr.sent, scr.came, scr.total
    sent_late, came_late = scr.sent_late, scr.came_late
    local_sem, near_send, near_recv = scr.local_sem, scr.near_send, scr.near_recv
    tokens, width = scr.dy.shape
    own = tokens // 2
    rows = left[0].shape[0]
    half, quarter = rows // 2, rows // 4
    ring_total = total.shape[0]
    ring_sent = sent.shape[0]

    me = lax.axis_index("dp")
    rank = lax.axis_index("tensor")
    low, high = lax.rem(me, 4), lax.div(me, 4)
    bit = [lax.rem(lax.div(high, 2**s), 2) for s in range(bits)]
    mine = aligned(rank * own, own)

    partners = [1, 2, 3, 4, 5, 6, 7] + [8 << s for s in range(bits - 1)]
    barrier = pltpu.get_barrier_semaphore()
    for by in partners:
        pl.semaphore_signal(barrier, inc=1, device_id={"dp": flip(me, by)}, device_id_type=MESH)
    pl.semaphore_signal(barrier, inc=1, device_id={"tensor": 1 - rank}, device_id_type=MESH)
    pl.semaphore_wait(barrier, len(partners) + 1)

    def remote(src, dst, send, recv, by):
        return pltpu.make_async_remote_copy(
            src_ref=src,
            dst_ref=dst,
            send_sem=send,
            recv_sem=recv,
            device_id={"dp": flip(me, by)},
            device_id_type=MESH,
        )

    def x_copy(src, dst, i):
        return pltpu.make_async_remote_copy(
            src_ref=src,
            dst_ref=dst,
            send_sem=scr.x_send.at[i],
            recv_sem=scr.x_recv.at[i],
            device_id={"tensor": 1 - rank},
            device_id_type=MESH,
        )


    def slot(array, j, start, columns):
        return every[array].at[pl.ds(j * tokens, tokens), pl.ds(start, columns)]

    def near(t, j):
        array, _, start, columns, _ = plan[t]
        by = 4 if j == 4 else 2 if j in (2, 6) else 1
        src = slot(array, 8 if j == 4 else j - by, start, columns)
        dst = slot(array, j, start, columns)
        return remote(src, dst, near_send.at[t, j], near_recv.at[t, j], by)

    def stage_rows(s):
        return half - (half >> (s - 1)), quarter >> (s - 1)

    def far(t, s):
        columns = plan[t][3] * (2 if t < jobs.halved else 1)
        if s == 0:
            src, dst = sent.at[t % ring_sent], came.at[t % RING]
            at = (slice(None), pl.ds(0, columns))
        else:
            src, dst = sent_late.at[t % ring_sent], came_late.at[t % RING]
            at = (pl.ds(*stage_rows(s)), pl.ds(0, columns))
        return remote(
            src.at[at], dst.at[at], scr.far_send.at[t, s], scr.far_recv.at[t, s], 4 << s
        )

    def final_row():
        row = 0
        for s in range(2, bits):
            row = row + bit[s] * (quarter >> (s - 1))
        return row

    last_size = quarter >> (bits - 2)
    half_hidden = jobs.outs[0] // 2

    def outputs(t):
        copies = []
        done = 0
        if t < jobs.halved:
            _, _, start, columns, _ = plan[t]
            for i, side in enumerate((bit[0], 1 - bit[0])):
                src = scr.turned.at[t % 3].at[pl.ds(i * columns, columns), :]
                dst = outs[0].at[pl.ds(pl.multiple_of(side * half_hidden + start, LANES), columns), :]
                copies.append(pltpu.make_async_copy(src, dst, scr.out_sem.at[t, i]))
            return copies
        for i, (out, first, columns) in enumerate(plan[t][4]):
            if t in jobs.turned:
                src = scr.turned.at[jobs.turned.index(t) % 3].at[pl.ds(done, columns), :]
                dst = outs[out].at[pl.ds(first, columns), :]
                copies.append(pltpu.make_async_copy(src, dst, scr.out_sem.at[t, i]))
                continue
            copies.append(
                pltpu.make_async_copy(
                    total.at[t % ring_total].at[
                        aligned(final_row(), last_size), pl.ds(done, columns)
                    ],
                    outs[out].at[:, pl.ds(first, columns)],
                    scr.out_sem.at[t, i],
                )
            )
            done += columns
        return copies

    def tiles(t, body):
        start, columns = plan[t][2:4]
        if t < jobs.halved:
            start, columns = 0, 2 * columns

        @pl.loop(0, columns // TILE)
        def _(i):
            body(aligned(start + i * TILE, TILE), aligned(i * TILE, TILE))

    def dot(t, first, size, at):
        array, f = plan[t][:2]
        return jnp.dot(
            left[f][aligned(first, size), :], every[array][:, at], preferred_element_type=jnp.float32
        )

    def first_pass(t):
        if t >= ring_sent + jobs.halved:
            far(t - ring_sent, 0).wait_send()

        def body(at, to):
            out = dot(t, (1 - bit[0]) * half, half, at)
            sent[t % ring_sent, :, to] = out.astype(jnp.bfloat16)

        tiles(t, body)
        far(t, 0).start()

    def second_pass(t):
        far(t, 0).wait_recv()
        if t >= ring_sent:
            far(t - ring_sent, 1).wait_send()
        if t >= ring_total:
            for copy in outputs(t - ring_total):
                copy.wait()
        base = bit[0] * half

        def body(at, to):
            away, kept = (1 - bit[1]) * quarter, bit[1] * quarter
            out = dot(t, base + away, quarter, at)
            out = out + came[t % RING, aligned(away, quarter), to].astype(jnp.float32)
            sent_late[t % ring_sent, pl.ds(0, quarter), to] = out.astype(jnp.bfloat16)
            out = dot(t, base + kept, quarter, at)
            out = out + came[t % RING, aligned(kept, quarter), to].astype(jnp.float32)
            total[t % ring_total, :, to] = out

        tiles(t, body)
        far(t, 1).start()

    def later_pass(t, s):
        far(t, s - 1).wait_recv()
        if t >= ring_sent:
            far(t - ring_sent, s).wait_send()
        first, size = stage_rows(s - 1)
        piece = size // 2
        at_row = 0
        for q in range(2, s):
            at_row = at_row + bit[q] * (quarter >> (q - 1))
        away, kept = (1 - bit[s]) * piece, bit[s] * piece

        def body(at, to):
            out = total[t % ring_total, aligned(at_row + away, piece), to]
            out = out + came_late[t % RING, aligned(first + away, piece), to].astype(jnp.float32)
            sent_late[t % ring_sent, pl.ds(first + size, piece), to] = out.astype(jnp.bfloat16)
            row = aligned(at_row + kept, piece)
            out = total[t % ring_total, row, to]
            out = out + came_late[t % RING, aligned(first + kept, piece), to].astype(jnp.float32)
            total[t % ring_total, row, to] = out

        tiles(t, body)
        far(t, s).start()

    def last_pass(t):
        far(t, bits - 1).wait_recv()
        first, size = stage_rows(bits - 1)

        def body(at, to):
            row = aligned(final_row(), last_size)
            out = total[t % ring_total, row, to]
            out = out + came_late[t % RING, pl.ds(first, size), to].astype(jnp.float32)
            if t in jobs.turned:
                scr.turned[jobs.turned.index(t) % 3, to, :] = out.T
            else:
                total[t % ring_total, row, to] = out

        tiles(t, body)
        for copy in outputs(t):
            copy.start()

    def halved_first(t):
        if t >= ring_sent:
            far(t - ring_sent, 1).wait_send()
        if t >= ring_total:
            for copy in outputs(t - ring_total):
                copy.wait()
        array, f, start, columns, _ = plan[t]

        @pl.loop(0, columns // LANES)
        def _(i):
            right = every[array][pl.ds(0, 8 * tokens), aligned(start + i * LANES, LANES)]
            for side in range(2):
                to = aligned(side * columns + i * LANES, LANES)
                for row, kept in ((1 - bit[1], False), (bit[1], True)):
                    at = aligned(side * half + row * quarter, quarter)
                    out = jnp.dot(left[f][at, :], right, preferred_element_type=jnp.float32)
                    if kept:
                        total[t % ring_total, :, to] = out
                    else:
                        sent_late[t % ring_sent, pl.ds(0, quarter), to] = out.astype(jnp.bfloat16)

        far(t, 1).start()

    def pair_copy(t):
        columns = pl.ds(0, plan[t][3])
        return remote(
            scr.pair_sent.at[t].at[:, columns],
            scr.pair_came.at[t].at[:, columns],
            scr.pair_send.at[t],
            scr.pair_recv.at[t],
            4,
        )

    def halved_sum(t):
        far(t, bits - 1).wait_recv()
        columns = plan[t][3]
        first, size = stage_rows(bits - 1)
        row = aligned(final_row(), last_size)

        @pl.loop(0, columns // LANES)
        def _(i):
            for side in (bit[0], 1 - bit[0]):
                to = aligned(side * columns + i * LANES, LANES)
                out = total[t % ring_total, row, to]
                out = out + came_late[t % RING, pl.ds(first, size), to].astype(jnp.float32)
                total[t % ring_total, row, to] = out
            scr.pair_sent[t, :, aligned(i * LANES, LANES)] = out.astype(jnp.bfloat16)

        pair_copy(t).start()

    def halved_last(t):
        pair_copy(t).wait_recv()
        columns = plan[t][3]
        row = aligned(final_row(), last_size)

        @pl.loop(0, columns // LANES)
        def _(i):
            at = aligned(i * LANES, LANES)
            mine_at = aligned(bit[0] * columns + i * LANES, LANES)
            scr.turned[t % 3, at, :] = total[t % ring_total, row, mine_at].T
            theirs = scr.pair_came[t, :, at].astype(jnp.float32)
            scr.turned[t % 3, aligned(columns + i * LANES, LANES), :] = theirs.T

        for copy in outputs(t):
            copy.start()

    feature_waited = set()

    begun = set()
    ready = [0]

    def begin_to(t):
        for u in range(min(t + 1, ready[0])):
            if u not in begun:
                begun.add(u)
                if u < jobs.halved:
                    near(u, 4).start()
                near(u, 1).start()
                near(u, 2).start()

    def pass_on(t):
        if t < jobs.halved:
            near(t, 4).wait_recv()
            near(t, 6).start()
            near(t, 5).start()
        near(t, 2).wait_recv()
        near(t, 3).start()
        begin_to(t + 2)

    def pass_again(t):
        if t < jobs.halved:
            near(t, 6).wait_recv()
            near(t, 7).start()

    def feature_slots(f):
        return range(1, 8 if f == 0 else 4)

    def work(t):
        if t < len(plan):
            f = plan[t][1]
            if f not in feature_waited:
                feature_waited.add(f)
                for j in feature_slots(f):
                    feature_copy(f, j).wait_recv()
            for j in (1, 3, 5, 7) if t < jobs.halved else (1, 3):
                near(t, j).wait_recv()
            if t < jobs.halved:
                halved_first(t)
            else:
                first_pass(t)
        for u in range(min(t, len(plan)) - 1, max(t - bits, 0) - 1, -1):
            gap = t - u
            if u < jobs.halved:
                if gap < bits - 1:
                    later_pass(u, gap + 1)
                elif gap == bits - 1:
                    halved_sum(u)
                else:
                    halved_last(u)
            elif gap == 1:
                second_pass(u)
            elif gap < bits:
                later_pass(u, gap)
            else:
                last_pass(u)

    def step(t):
        if t < len(plan):
            pass_on(t)
            pass_again(t)
        work(t)


    source_of = {0: 0, 3: 1, 1: 0, 2: 1}

    def feature_copy(f, j):
        return remote(
            scr.source.at[source_of[f], flip(low, j % 4)],
            left[f].at[:, pl.ds(j * tokens, tokens)],
            scr.feat_send.at[f, j],
            scr.feat_recv.at[f, j],
            j,
        )

    def turn(ref, f):
        count = 4 << bits
        block = width // count
        source = scr.source.at[source_of[f]]

        @pl.loop(0, width // LANES)
        def _(c):
            turned = ref[:, aligned(c * LANES, LANES)].T
            for piece in range(LANES // block):
                d = c * (LANES // block) + piece
                group = lax.div(d, 4)
                place = 0
                for s in range(bits):
                    place = place + lax.rem(lax.div(group, 2**s), 2) * 2 ** (bits - 1 - s)
                source[lax.rem(d, 4), aligned(place * block, block), :] = turned[
                    piece * block : (piece + 1) * block
                ]

        left[f][:, pl.ds(0, tokens)] = source[low]

    def send_features(f):
        for j in (6, 7, 2, 3, 4, 5, 1) if f == 0 else (2, 3, 1):
            feature_copy(f, j).start()


    weight_sem = scr.weight_sem

    def hidden_weights(i):
        at = lax.rem(i, 2)
        copies = []
        for side in range(2):
            columns = aligned(side * half_hidden + i * LANES, LANES)
            to = pl.ds(side * LANES, LANES)
            for k, (src, dst) in enumerate(
                (
                    (inp.w_gate.at[:, columns], scr.gate_w.at[at].at[:, to]),
                    (inp.w_up.at[:, columns], scr.up_w.at[at].at[:, to]),
                    (inp.w_down.at[columns, :], scr.down_w.at[at].at[to, :]),
                )
            ):
                copies.append(pltpu.make_async_copy(src, dst, weight_sem.at[k + 3 * side, at]))
        return copies

    hidden_tiles = jobs.outs[0] // TILE
    wide = 512

    def hidden_part(first, count):
        @pl.loop(first, first + count)
        def _(i):
            at = lax.rem(i, 2)

            @pl.when(i + 1 < hidden_tiles)
            def _():
                for copy in hidden_weights(i + 1):
                    copy.start()

            for copy in hidden_weights(i):
                copy.wait()
            gate_w, up_w, down_w = scr.gate_w.at[at], scr.up_w.at[at], scr.down_w.at[at]
            two = scr.two_full[...]
            gate = jnp.dot(two, gate_w[...], preferred_element_type=jnp.float32)
            up = jnp.dot(two, up_w[...], preferred_element_type=jnp.float32)
            d_act = against(scr.dy[...], down_w[...])
            sig = jax.nn.sigmoid(gate)
            silu = gate * sig
            act = (silu * up).astype(jnp.bfloat16)
            d_gate = (d_act * up * sig * (1.0 + gate * (1.0 - sig))).astype(jnp.bfloat16)
            d_up = (d_act * silu).astype(jnp.bfloat16)
            for side in range(2):
                part = slice(side * LANES, (side + 1) * LANES)
                away = bit[0] if side == 0 else 1 - bit[0]
                at_rows = aligned(away * 8 * tokens, tokens)
                every[0][at_rows, aligned(i * LANES, LANES)] = act[:, part]
                columns = aligned(side * half_hidden + i * LANES, LANES)
                every[1][pl.ds(0, tokens), columns] = d_gate[:, part]
                every[2][pl.ds(0, tokens), columns] = d_up[:, part]

            @pl.loop(0, width // wide)
            def _(n):
                part = aligned(n * wide, wide)
                scr.mlp_acc[:, part] += jnp.dot(
                    act, down_w[:, part], preferred_element_type=jnp.float32
                )
                scr.norm_acc[:, part] += against(d_gate, gate_w[part, :]) + against(
                    d_up, up_w[part, :]
                )

    def row_loop(body):
        @pl.loop(0, own // ROWS)
        def _(i):
            body(*[aligned(base + i * ROWS, ROWS) for base in (0, rank * own, (1 - rank) * own)])

    def eight(value):
        return jnp.sum(value.reshape(ROWS // 8, 8, width), axis=0)

    def send_partial(acc, buffer):
        @pl.loop(0, own // ROWS)
        def _(i):
            row = aligned((1 - rank) * own + i * ROWS, ROWS)
            scr.x_sent[buffer, aligned(i * ROWS, ROWS), :] = acc[row, :].astype(
                jnp.bfloat16
            )


    def out_weights(i):
        return pltpu.make_async_copy(
            inp.w_out.at[aligned(i * TILE, TILE), :],
            scr.down_w.at[lax.rem(i, 2)],
            weight_sem.at[2, lax.rem(i, 2)],
        )

    def query_buffer(j):
        return (scr.gate_w, scr.up_w)[j % 4 // 2].at[j % 2]

    def query_weights(j):
        dst, sem = query_buffer(j), weight_sem.at[j % 4 // 2, j % 2]
        if j < query_tiles:
            return [
                pltpu.make_async_copy(inp.w_query.at[:, pl.ds(j * TILE, TILE)], dst, sem)
            ]
        kv = inp.w_key.shape[1]
        return [
            pltpu.make_async_copy(inp.w_key, dst.at[:, pl.ds(0, kv)], sem),
            pltpu.make_async_copy(inp.w_value, dst.at[:, pl.ds(kv, kv)], scr.last_sem.at[2]),
        ]

    query_width = jobs.outs[3]
    kv_width = jobs.outs[5]
    query_tiles = query_width // TILE
    kv_heads = kv_width // HD
    pairs = query_width // LANES // kv_heads
    score_scale = HD ** (-0.5)

    def lane_masks():
        lane = lax.broadcasted_iota(jnp.int32, (1, LANES), 1)
        first = (lane < HD).astype(jnp.float32)
        return first, 1.0 - first

    def unrotate(value):
        lane = lax.broadcasted_iota(jnp.int32, value.shape, 1)
        other = jnp.where(
            lax.rem(lane, HD) < HD // 2,
            pltpu.roll(value, LANES - HD // 2, 1),
            pltpu.roll(value, HD // 2, 1),
        )
        return value * scr.cosine[...] + other * scr.sine[...]

    def d_attended():
        @pl.loop(0, query_tiles)
        def _(i):
            out_weights(i).wait()
            scr.d_att[:, aligned(i * TILE, TILE)] = against(
                scr.one_full[...], scr.down_w[lax.rem(i, 2)]
            ).astype(jnp.bfloat16)

            @pl.when(i + 2 < query_tiles)
            def _():
                out_weights(i + 2).start()

    def attend_back(kv):
        keys, values = scr.keys.at[kv], scr.values.at[kv]
        keys_acc, values_acc = scr.keys_acc.at[kv], scr.values_acc.at[kv]
        keys_acc[...] = jnp.zeros_like(keys_acc)
        values_acc[...] = jnp.zeros_like(values_acc)

        @pl.loop(0, pairs)
        def _(p):
            columns = aligned((kv * pairs + p) * LANES, LANES)
            d_query = jnp.zeros((tokens, LANES), jnp.float32)
            for lanes in lane_masks():
                lanes_low = lanes.astype(jnp.bfloat16)
                query = scr.query[:, columns] * lanes_low
                d_att = scr.d_att[:, columns] * lanes_low
                scores = against(query, keys[...]) * score_scale
                scores = jnp.where(scr.mask[...] > 0, scores, masked_score)
                expo = jnp.exp(scores - jnp.max(scores, axis=1, keepdims=True))
                probs = expo * (1.0 / jnp.sum(expo, axis=1, keepdims=True))
                d_probs = against(d_att, values[...])
                inner = jnp.sum(probs * d_probs, axis=1, keepdims=True)
                d_scores = (probs * (d_probs - inner)).astype(jnp.bfloat16)
                d_query = d_query + lanes * jnp.dot(
                    d_scores, keys[...], preferred_element_type=jnp.float32
                )
                keys_acc[...] += inner_rows(d_scores, query)
                values_acc[...] += inner_rows(probs.astype(jnp.bfloat16), d_att)
            every[4][pl.ds(0, tokens), columns] = unrotate(d_query * score_scale).astype(
                jnp.bfloat16
            )

    def finish_keys():
        lanes = lane_masks()
        d_key = jnp.zeros((tokens, LANES), jnp.float32)
        d_value = jnp.zeros((tokens, LANES), jnp.float32)
        for kv in range(kv_heads):
            for out in (0, 1):
                acc = (scr.keys_acc, scr.values_acc)[out][kv]
                acc = (acc + pltpu.roll(acc, HD, 1)) * lanes[kv]
                if out == 0:
                    d_key = d_key + acc
                else:
                    d_value = d_value + acc
        d_key = unrotate(d_key * score_scale)
        every[4][pl.ds(0, tokens), pl.ds(query_width, kv_width)] = d_key.astype(jnp.bfloat16)
        every[4][pl.ds(0, tokens), pl.ds(query_width + kv_width, kv_width)] = d_value.astype(
            jnp.bfloat16
        )

    def d_normed_one():
        for j in range(query_tiles + 1):
            for copy in query_weights(j):
                copy.wait()
            weights = query_buffer(j)
            grads = every[4][pl.ds(0, tokens), pl.ds(j * TILE, TILE)]

            @pl.loop(0, width // wide)
            def _(n):
                part = aligned(n * wide, wide)
                add = against(grads, weights[part, :])
                if j == 0:
                    scr.norm_acc[:, part] = add
                else:
                    scr.norm_acc[:, part] += add

            if j + 4 < query_tiles + 1:
                for copy in query_weights(j + 4):
                    copy.start()


    def mean_rows(value):
        return jnp.mean(value, axis=1, keepdims=True)

    def middle_back(row, full, other):
        grad = scr.norm_acc[full, :] + scr.x_came[0, row, :].astype(jnp.float32)
        middle = scr.middle[row, :]
        scale = lax.rsqrt(mean_rows(middle * middle) + norm_eps)
        normed = middle * scale
        scr.gain_part[0] += eight(grad * normed)
        scaled = grad * inp.mlp_gain[...]
        d_middle = scr.dy[full, :].astype(jnp.float32) + scale * (
            scaled - normed * mean_rows(scaled * normed)
        )
        scr.mlp_acc[other, :] = d_middle
        scr.one_full[full, :] = d_middle.astype(jnp.bfloat16)

    def finish_layer(row, full, other):
        mlp = scr.mlp_acc[full, :] + scr.x_came[1, row, :].astype(jnp.float32)
        scr.x_sent[1, row, :] = (scr.middle[row, :] + mlp).astype(jnp.bfloat16)

    def token_back(row, full, other):
        grad = scr.norm_acc[full, :] + scr.x_came[2, row, :].astype(jnp.float32)
        valid = scr.valid[full, :][:, :1]
        masked = scr.tok_full[full, :].astype(jnp.float32) * valid
        scale = lax.rsqrt(mean_rows(masked * masked) + norm_eps)
        normed = masked * scale
        scr.gain_part[1] += eight(grad * normed)
        scaled = grad * inp.attn_gain[...]
        out = scr.mlp_acc[other, :] + scale * (scaled - normed * mean_rows(scaled * normed))
        scr.x_sent[1, row, :] = (out * valid).astype(jnp.bfloat16)

    def gain_copy(i):
        src, dst = scr.gain_all.at[i], scr.gain_came.at[i]
        if i < bits + 2:
            return remote(src, dst, scr.gain_send.at[i], scr.gain_recv.at[i], 1 << i)
        return pltpu.make_async_remote_copy(
            src_ref=src,
            dst_ref=dst,
            send_sem=scr.gain_send.at[i],
            recv_sem=scr.gain_recv.at[i],
            device_id={"tensor": 1 - rank},
            device_id_type=MESH,
        )

    gain_steps = bits + 3

    def gain_next(i):
        gain_copy(i).wait_recv()
        scr.gain_all[i + 1] = scr.gain_all[i] + scr.gain_came[i]
        if i + 1 < gain_steps:
            gain_copy(i + 1).start()


    def prepare():
        ends = []
        for k in range(inp.lengths.shape[0]):
            ends.append(inp.lengths[k] + (ends[-1] if ends else 0))

        def segments(shape, axis):
            place = lax.broadcasted_iota(jnp.int32, shape, axis)
            return place, sum((place >= end).astype(jnp.int32) for end in ends)

        place, _ = segments((tokens, LANES), 0)
        start = jnp.zeros_like(place)
        for end in ends:
            start = jnp.maximum(start, jnp.where(place >= end, end, 0))
        scr.valid[...] = (place < ends[-1]).astype(jnp.float32)
        lane = lax.broadcasted_iota(jnp.int32, (tokens, LANES), 1)
        slow = lax.rem(lane, HD // 2).astype(jnp.float32)
        inverse = jnp.exp(slow * (-2.0 * math.log(10000.0) / HD))
        angles = (place - start).astype(jnp.float32) * inverse
        scr.cosine[...] = jnp.cos(angles)
        sine = jnp.sin(angles)
        scr.sine[...] = jnp.where(lax.rem(lane, HD) < HD // 2, sine, -sine)
        rows_at, row_segment = segments((tokens, tokens), 0)
        columns_at, column_segment = segments((tokens, tokens), 1)
        seen = (row_segment == column_segment) & (columns_at <= rows_at)
        scr.mask[...] = seen.astype(jnp.float32)


    def query_half(k):
        return every[2].at[pl.ds(0, width // 2), pl.ds(k * query_width, query_width)]

    def out_all():
        return every[1].at[pl.ds(0, query_width), pl.ds(0, width)]

    def forward_weights():
        dst = scr.gate_w.at[1]
        copies = [
            pltpu.make_async_copy(
                inp.w_query.at[pl.ds(k * width // 2, width // 2), :],
                query_half(k),
                scr.first_sem.at[k],
            )
            for k in range(2)
        ]
        for k, ref in ((0, inp.w_key), (1, inp.w_value)):
            copies.append(
                pltpu.make_async_copy(
                    ref, dst.at[:, pl.ds(k * kv_width, kv_width)], scr.first_sem.at[2 + k]
                )
            )
        copies.append(pltpu.make_async_copy(inp.w_out, out_all(), scr.first_sem.at[4]))
        return copies

    def all_rows(body):
        @pl.loop(0, tokens // ROWS)
        def _(i):
            body(aligned(i * ROWS, ROWS))

    def first_norm(row, full, other):
        one_rows(full)

    def first_norm_other(row, full, other):
        one_rows(other)

    def one_rows(full):
        masked = scr.tok_full[full, :].astype(jnp.float32) * scr.valid[full, :][:, :1]
        scale = lax.rsqrt(mean_rows(masked * masked) + norm_eps)
        scr.one_full[full, :] = (masked * scale * inp.attn_gain[...]).astype(jnp.bfloat16)

    def mask_cotangent(full):
        dy = scr.dy[full, :].astype(jnp.float32) * scr.valid[full, :][:, :1]
        scr.dy[full, :] = dy.astype(jnp.bfloat16)

    def rotated(value, row):
        lane = lax.broadcasted_iota(jnp.int32, value.shape, 1)
        other = jnp.where(
            lax.rem(lane, HD) < HD // 2,
            pltpu.roll(value, LANES - HD // 2, 1),
            pltpu.roll(value, HD // 2, 1),
        )
        return value * scr.cosine[row, :] - other * scr.sine[row, :]

    def projections(row):
        @pl.loop(0, query_tiles)
        def _(j):
            columns = aligned(j * TILE, TILE)
            out = jnp.dot(
                scr.one_full[row, : width // 2],
                query_half(0)[:, columns],
                preferred_element_type=jnp.float32,
            )
            out = out + jnp.dot(
                scr.one_full[row, width // 2 :],
                query_half(1)[:, columns],
                preferred_element_type=jnp.float32,
            )
            for k in range(TILE // LANES):
                part = rotated(out[:, k * LANES : (k + 1) * LANES], row)
                scr.query[row, aligned(j * TILE + k * LANES, LANES)] = part.astype(jnp.bfloat16)

        out = jnp.dot(scr.one_full[row, :], scr.gate_w[1], preferred_element_type=jnp.float32)
        lane = lax.broadcasted_iota(jnp.int32, (own, LANES), 1)
        for k, ref in ((0, scr.keys), (1, scr.values)):
            part = out[:, k * LANES : (k + 1) * LANES]
            part = rotated(part, row) if k == 0 else part
            part = part.astype(jnp.bfloat16).astype(jnp.float32)
            turned = pltpu.roll(part, HD, 1)
            ref[0, row, :] = jnp.where(lane < HD, part, turned).astype(jnp.bfloat16)
            ref[1, row, :] = jnp.where(lane < HD, turned, part).astype(jnp.bfloat16)

    def attend(row):
        for kv in range(kv_heads):

            @pl.loop(0, pairs)
            def _(p):
                columns = aligned((kv * pairs + p) * LANES, LANES)
                out = jnp.zeros((own, LANES), jnp.float32)
                for lanes in lane_masks():
                    query = scr.query[row, columns] * lanes.astype(jnp.bfloat16)
                    scores = against(query, scr.keys[kv]) * score_scale
                    scores = jnp.where(scr.mask[row, :] > 0, scores, masked_score)
                    expo = jnp.exp(scores - jnp.max(scores, axis=1, keepdims=True))
                    probs = expo * (1.0 / jnp.sum(expo, axis=1, keepdims=True))
                    out = out + lanes * jnp.dot(
                        probs.astype(jnp.bfloat16), scr.values[kv], preferred_element_type=jnp.float32
                    )
                every[3][row, columns] = out.astype(jnp.bfloat16)

    def out_rows(row, store):
        @pl.loop(0, width // wide)
        def _(n):
            part = aligned(n * wide, wide)
            store(
                part,
                jnp.dot(
                    every[3][row, :],
                    every[1][pl.ds(0, query_width), part],
                    preferred_element_type=jnp.float32,
                ),
            )

    def middle_forward(row, full, other):
        masked = scr.tok_full[full, :].astype(jnp.float32) * scr.valid[full, :][:, :1]
        middle = masked + (scr.norm_acc[row, :] + scr.x_came[0, row, :].astype(jnp.float32))
        scale = lax.rsqrt(mean_rows(middle * middle) + norm_eps)
        scr.middle[row, :] = middle
        scr.two_full[full, :] = (middle * scale * inp.mlp_gain[...]).astype(jnp.bfloat16)


    first_copies = [
        (x_copy(ref, full.at[mine, :], i), pltpu.make_async_copy(ref, full.at[mine, :], local_sem.at[i]))
        for i, (ref, full) in enumerate(((inp.tokens, scr.tok_full), (inp.cotangent, scr.dy)))
    ]
    for copy in first_copies[0]:
        copy.start()
    loads = forward_weights()
    for copy in loads:
        copy.start()
    first_copies[1][1].start()
    prepare()
    first_copies[0][1].wait()
    row_loop(first_norm)
    for copy in loads:
        copy.wait()
    projections(mine)
    theirs = aligned((1 - rank) * own, own)
    first_copies[0][0].wait_recv()
    first_copies[1][0].start()
    row_loop(first_norm_other)
    projections(theirs)
    turn(scr.one_full, 3)
    send_features(3)
    attend(theirs)

    def store_theirs(part, out):
        scr.x_sent[0, :, part] = out.astype(jnp.bfloat16)

    def store_mine(part, out):
        scr.norm_acc[pl.ds(0, own), part] = out

    out_rows(theirs, store_theirs)
    branch_copy = x_copy(scr.x_sent.at[0], scr.x_came.at[0], 2)
    branch_copy.start()
    first_copies[1][1].wait()
    first_copies[1][0].wait_recv()
    all_rows(mask_cotangent)
    turn(scr.dy, 0)
    send_features(0)
    attend(mine)
    for copy in hidden_weights(0):
        copy.start()
    out_rows(mine, store_mine)
    branch_copy.wait_recv()
    row_loop(middle_forward)
    two_copy = x_copy(scr.two_full.at[mine, :], scr.two_full.at[mine, :], 3)
    two_copy.start()
    scr.mlp_acc[...] = jnp.zeros_like(scr.mlp_acc)
    scr.norm_acc[...] = jnp.zeros_like(scr.norm_acc)
    scr.gain_part[...] = jnp.zeros_like(scr.gain_part)
    two_copy.wait_recv()
    for part, (first, count) in enumerate(jobs.groups):
        hidden_part(first, count)
        ready[0] = part + 1
        begin_to(part)
        if part >= 1:
            pass_on(part - 1)
        if part >= 2:
            pass_again(part - 2)
            work(part - 2)
    at = len(jobs.groups) - 2
    pass_again(at)
    branch_copy.wait_send()
    send_partial(scr.norm_acc, 0)
    norm_copy = x_copy(scr.x_sent.at[0], scr.x_came.at[0], 4)
    norm_copy.start()
    for i in range(2):
        out_weights(i).start()
    for j in range(4):
        for copy in query_weights(j):
            copy.start()
    for j in feature_slots(0):
        feature_copy(0, j).wait_send()
    turn(scr.two_full, 1)
    pass_on(at + 1)
    send_features(1)
    work(at)
    pass_again(at + 1)
    send_partial(scr.mlp_acc, 1)
    ready[0] = jobs.first_attention + 1
    work(at + 1)
    begin_to(at + 3)
    norm_copy.wait_recv()
    row_loop(middle_back)
    db_copy = x_copy(scr.one_full.at[mine, :], scr.one_full.at[mine, :], 5)
    db_copy.start()
    mlp_copy = x_copy(scr.x_sent.at[1], scr.x_came.at[1], 6)
    step(at + 2)
    for j in (1, 2, 3):
        feature_copy(3, j).wait_send()
    db_copy.wait_recv()
    mlp_copy.start()
    turn(scr.one_full, 2)
    d_attended()
    step(at + 3)
    attend_back(0)
    step(at + 4)
    attend_back(1)
    finish_keys()
    ready[0] = len(plan)
    step(at + 5)
    send_features(2)
    d_normed_one()
    norm_copy.wait_send()
    send_partial(scr.norm_acc, 0)
    one_copy = x_copy(scr.x_sent.at[0], scr.x_came.at[2], 7)
    one_copy.start()
    mlp_copy.wait_send()
    mlp_copy.wait_recv()
    row_loop(finish_layer)
    layer_copy = pltpu.make_async_copy(scr.x_sent.at[1], layer_out, scr.last_sem.at[0])
    layer_copy.start()
    step(at + 6)
    layer_copy.wait()
    one_copy.wait_recv()
    row_loop(token_back)
    token_copy = pltpu.make_async_copy(scr.x_sent.at[1], token_grad, scr.last_sem.at[1])
    token_copy.start()
    gains = scr.gain_all.at[0]
    gains[...] = jnp.zeros_like(gains)
    for i in range(2):
        gains[pl.ds(i, 1), :] = jnp.sum(scr.gain_part[i], axis=0, keepdims=True)
    gain_copy(0).start()
    at = at + 7
    for i in range(gain_steps):
        if at < len(plan):
            step(at)
            at += 1
        gain_next(i)
    gain_rows = width // (2 * (4 << bits))
    place = (2 * me + rank) * gain_rows
    block = scr.gain_all[gain_steps, :, aligned(lax.div(place, LANES) * LANES, LANES)]
    scr.gain_own[...] = pltpu.roll(block, lax.rem(LANES - lax.rem(place, LANES), LANES), 1)
    gains_copy = pltpu.make_async_copy(scr.gain_own, gains_out, local_sem.at[1])
    gains_copy.start()
    for t in range(at, len(plan) + bits):
        step(t)


    for copy, _ in first_copies:
        copy.wait_send()
    two_copy.wait_send()
    db_copy.wait_send()
    one_copy.wait_send()
    token_copy.wait()
    gains_copy.wait()
    for i in range(gain_steps):
        gain_copy(i).wait_send()
    for f in (1, 2):
        for j in (1, 2, 3):
            feature_copy(f, j).wait_send()
    for t in range(len(plan)):
        for j in range(1, 8 if t < jobs.halved else 4):
            near(t, j).wait_send()
        if t < jobs.halved:
            pair_copy(t).wait_send()
        if t + ring_sent >= len(plan):
            for s in range(bits):
                far(t, s).wait_send()
        if t + ring_total >= len(plan):
            for copy in outputs(t):
                copy.wait()


def layer_call(jobs, args, tokens, width):
    count = lax.axis_size("dp")
    bits = (count // 4).bit_length() - 1
    rows = width // 4
    block = width // count
    own = tokens // 2
    plan = jobs.plan
    vmem, any_space = pl.BlockSpec(memory_space=pltpu.VMEM), pl.BlockSpec(memory_space=pl.ANY)
    bf16, f32 = jnp.bfloat16, jnp.float32
    late_rows = rows // 2 - (rows // 2 >> (bits - 1))
    ring_total = max(4, bits + 1)
    kv_heads = jobs.outs[5] // HD
    dma = pltpu.SemaphoreType.DMA
    scratch = Scratch(
        tok_full=pltpu.VMEM((tokens, width), bf16),
        dy=pltpu.VMEM((tokens, width), bf16),
        one_full=pltpu.VMEM((tokens, width), bf16),
        middle=pltpu.VMEM((own, width), f32),
        query=pltpu.VMEM((tokens, jobs.outs[3]), bf16),
        keys=pltpu.VMEM((kv_heads, tokens, LANES), bf16),
        values=pltpu.VMEM((kv_heads, tokens, LANES), bf16),
        mask=pltpu.VMEM((tokens, tokens), f32),
        cosine=pltpu.VMEM((tokens, LANES), f32),
        sine=pltpu.VMEM((tokens, LANES), f32),
        valid=pltpu.VMEM((tokens, LANES), f32),
        source=pltpu.VMEM((2, 4, rows, tokens), bf16),
        sent=pltpu.VMEM((3, rows // 2, jobs.most), bf16),
        came=pltpu.VMEM((RING, rows // 2, jobs.most), bf16),
        sent_late=pltpu.VMEM((3, late_rows, jobs.most), bf16),
        came_late=pltpu.VMEM((RING, late_rows, jobs.most), bf16),
        total=pltpu.VMEM((ring_total, rows // 4, jobs.most), f32),
        turned=pltpu.VMEM((3, jobs.most, block), f32),
        gate_w=pltpu.VMEM((2, width, TILE), bf16),
        up_w=pltpu.VMEM((2, width, TILE), bf16),
        down_w=pltpu.VMEM((2, TILE, width), bf16),
        mlp_acc=pltpu.VMEM((tokens, width), f32),
        norm_acc=pltpu.VMEM((tokens, width), f32),
        two_full=pltpu.VMEM((tokens, width), bf16),
        x_came=pltpu.VMEM((3, own, width), bf16),
        x_sent=pltpu.VMEM((2, own, width), bf16),
        d_att=pltpu.VMEM((tokens, jobs.outs[3]), bf16),
        gain_part=pltpu.VMEM((2, 8, width), f32),
        gain_all=pltpu.VMEM((bits + 4, 8, width), f32),
        gain_came=pltpu.VMEM((bits + 3, 8, width), f32),
        gain_own=pltpu.VMEM((8, LANES), f32),
        pair_sent=pltpu.VMEM((jobs.halved, block, jobs.most_halved), bf16),
        pair_came=pltpu.VMEM((jobs.halved, block, jobs.most_halved), bf16),
        pair_send=dma((jobs.halved,)),
        pair_recv=dma((jobs.halved,)),
        keys_acc=pltpu.VMEM((kv_heads, tokens, LANES), f32),
        values_acc=pltpu.VMEM((kv_heads, tokens, LANES), f32),
        local_sem=dma((2,)),
        feat_send=dma((4, 8)),
        feat_recv=dma((4, 8)),
        near_send=dma((len(plan), 8)),
        near_recv=dma((len(plan), 8)),
        far_send=dma((len(plan), bits)),
        far_recv=dma((len(plan), bits)),
        out_sem=dma((len(plan), jobs.pieces)),
        weight_sem=dma((6, 2)),
        x_send=dma((8,)),
        x_recv=dma((8,)),
        gain_send=dma((bits + 3,)),
        gain_recv=dma((bits + 3,)),
        last_sem=dma((3,)),
        first_sem=dma((5,)),
    )
    operands = [pltpu.VMEM((9 * tokens, jobs.widths[0] // 2), bf16)]
    operands += [pltpu.VMEM((4 * tokens, w), bf16) for w in jobs.widths[1:]]
    operands += [pltpu.VMEM((rows, 8 * tokens), bf16)] + [pltpu.VMEM((rows, 4 * tokens), bf16)] * 3
    return pl.pallas_call(
        functools.partial(layer_kernel, jobs, bits),
        out_shape=[
            jax.ShapeDtypeStruct((w, block) if i in (0, 3) else (block, w), f32)
            for i, w in enumerate(jobs.outs)
        ]
        + [
            jax.ShapeDtypeStruct((own, width), bf16),
            jax.ShapeDtypeStruct((own, width), bf16),
            jax.ShapeDtypeStruct((8, LANES), f32),
        ],
        in_specs=[pl.BlockSpec(memory_space=pltpu.SMEM), vmem, vmem] + [any_space] * (len(args) - 3),
        out_specs=[any_space] * (len(jobs.outs) + 3),
        scratch_shapes=operands + list(scratch),
        compiler_params=pltpu.CompilerParams(
            collective_id=0, has_side_effects=True, vmem_limit_bytes=63 * 1024 * 1024
        ),
    )(*args)


PIECES = 2


def hand_over_kernel(count, gain_rows, *refs):
    gains, refs = refs[0], refs[1:]
    inputs, outs = refs[:count], refs[count : 2 * count]
    attn_out, mlp_out = refs[2 * count : 2 * count + 2]
    held = refs[2 * count + 2 : 3 * count + 2]
    in_sem, out_sem = refs[3 * count + 2 :]
    pairs = []
    for i in range(count):
        rows = inputs[i].shape[0] // PIECES
        for piece in range(PIECES):
            at = pl.ds(piece * rows, rows)
            pairs.append(
                (
                    pltpu.make_async_copy(inputs[i].at[at], held[i].at[at], in_sem.at[i, piece]),
                    pltpu.make_async_copy(held[i].at[at], outs[i].at[at], out_sem.at[i, piece]),
                )
            )
    for copy, _ in pairs:
        copy.start()
    mlp_out[...] = gains[0:1, :gain_rows]
    attn_out[...] = gains[1:2, :gain_rows]
    for come, go in pairs:
        come.wait()
        go.start()
    for _, copy in pairs:
        copy.wait()


def hand_over(arrays, gains, gain_rows):
    any_space, vmem = pl.BlockSpec(memory_space=pl.ANY), pl.BlockSpec(memory_space=pltpu.VMEM)
    gain = jax.ShapeDtypeStruct((1, gain_rows), jnp.float32)
    return pl.pallas_call(
        functools.partial(hand_over_kernel, len(arrays), gain_rows),
        out_shape=[jax.ShapeDtypeStruct(x.shape, x.dtype) for x in arrays] + [gain, gain],
        in_specs=[vmem] + [any_space] * len(arrays),
        out_specs=[any_space] * len(arrays) + [vmem, vmem],
        scratch_shapes=[pltpu.VMEM(x.shape, x.dtype) for x in arrays]
        + [pltpu.SemaphoreType.DMA((len(arrays), PIECES))] * 2,
    )(gains, *arrays)


def on_device(
    tokens,
    frag_lengths,
    attn_gain,
    w_query,
    w_key,
    w_value,
    w_out,
    mlp_gain,
    w_gate,
    w_up,
    w_down,
    out_cotangent,
):
    tok_rows, model_width = tokens.shape
    pack_rows = tok_rows * lax.axis_size("tensor")
    rank = lax.axis_index("tensor")
    jobs = Jobs(w_gate.shape[1], w_query.shape[1], w_key.shape[1])
    args = Inputs(
        lengths=frag_lengths,
        attn_gain=attn_gain[None, :],
        mlp_gain=mlp_gain[None, :],
        tokens=tokens,
        cotangent=out_cotangent,
        w_query=w_query,
        w_key=w_key,
        w_value=w_value,
        w_out=w_out,
        w_gate=w_gate,
        w_up=w_up,
        w_down=w_down,
    )
    out = layer_call(jobs, args, pack_rows, model_width)
    gain_rows = model_width // (lax.axis_size("tensor") * lax.axis_size("dp"))
    out = hand_over(out[:-1], out[-1], gain_rows)
    g_down, g_gate, g_up, g_out, g_query, g_key, g_value, layer_out, token_grad = out[:9]
    return (
        layer_out,
        token_grad,
        out[9][0],
        g_query,
        g_key,
        g_value,
        g_out,
        out[10][0],
        g_gate,
        g_up,
        g_down,
    )


def solution(mesh):
    placed = (
        P(("dp", "tensor"), None),
        P("dp"),
        P(),
        P(None, "tensor"),
        P(None, "tensor"),
        P(None, "tensor"),
        P("tensor", None),
        P(),
        P(None, "tensor"),
        P(None, "tensor"),
        P("tensor", None),
        P(("dp", "tensor"), None),
    )
    return jax.shard_map(
        on_device,
        mesh=mesh,
        in_specs=placed,
        out_specs=(
            P(("dp", "tensor"), None),
            P(("dp", "tensor"), None),
            P(("dp", "tensor")),
            P("dp", "tensor"),
            P("dp", "tensor"),
            P("dp", "tensor"),
            P("tensor", "dp"),
            P(("dp", "tensor")),
            P("dp", "tensor"),
            P("dp", "tensor"),
            P("tensor", "dp"),
        ),
        check_vma=False,
    )
```

```python
import functools
import math
from typing import Any, NamedTuple

import jax
import jax.numpy as jnp
from jax import lax
from jax.experimental import pallas as pl
from jax.experimental.pallas import tpu as pltpu
from jax.sharding import PartitionSpec as P

HD = 64
MESH = pl.DeviceIdType.MESH
TILE = 256
MOST = 1024
LANES = 128
RING = 4
ROWS = 16


norm_eps = 1e-05
masked_score = -1e30


def against(left, right):
    return lax.dot_general(
        left, right, (((1,), (1,)), ((), ())), preferred_element_type=jnp.float32
    )


def inner_rows(left, right):
    return lax.dot_general(
        left, right, (((0,), (0,)), ((), ())), preferred_element_type=jnp.float32
    )


def flip(value, by):
    for step in range(by.bit_length()):
        if by >> step & 1:
            value = value + (1 - 2 * lax.rem(lax.div(value, 2**step), 2)) * 2**step
    return value


def aligned(start, size):
    return pl.ds(pl.multiple_of(start, size), size)


def in_parts(tiles, shares):
    ends = [round(tiles * sum(shares[: i + 1]) / sum(shares)) for i in range(len(shares))]
    return [(start, end - start) for start, end in zip([0] + ends[:-1], ends)]


SHARES = ((1, 2, 2, 3, 3), (2, 3, 3, 3), (3, 3, 3, 2), (2, 2), (2, 2, 1))

TILES, BEGIN, PASS, FIRST, SECOND, LAST, SEND, CHAIN, GAIN = range(0, 900, 100)
ORDER = (
    0, 100, 1, 2, 101, 3, 200, 4, 300, 102, 5, 6, 201, 400, 7, 103,
    301, 202, 8, 9, 302, 10, 104, 500, 401, 203, 303, 601, 204, 501, 105, 701,
    402, 304, 502, 403, 205, 106, 305, 404, 702, 107, 206, 306, 503, 108, 207, 405,
    109, 307, 703, 208, 504, 406, 110, 308, 209, 505, 704, 407, 111, 705, 112, 309,
    506, 408, 113, 210, 211, 507, 706, 310, 115, 707, 409, 508, 602, 212, 311, 116,
    509, 410, 213, 708, 312, 114, 216, 215, 800, 411, 510, 313, 801, 412, 214, 511,
    802, 314, 117, 413, 315, 512, 414, 513, 316, 415, 803, 514, 217, 317, 416, 804,
    805, 515, 417, 516, 517,
)


class Jobs:
    def __init__(self, hidden, query_width, kv_width):
        tiles = hidden // TILE
        last = query_width + 2 * kv_width
        whole = ((4, 0, query_width), (5, query_width, kv_width), (6, query_width + kv_width, kv_width))
        self.plan = []
        for array, feature, width, shares in (
            (0, 0, hidden, SHARES[0]),
            (1, 1, hidden, SHARES[1]),
            (2, 1, hidden, SHARES[2]),
            (3, 2, query_width, SHARES[3]),
            (4, 3, last, SHARES[4]),
        ):
            for first, count in in_parts(width // TILE, shares):
                start, columns = first * TILE, count * TILE
                pieces = []
                for out, at, size in whole if array == 4 else ((array, 0, width),):
                    low, high = max(at, start), min(at + size, start + columns)
                    if low < high:
                        pieces.append((out, low - at, high - low))
                self.plan.append((array, feature, start, columns, tuple(pieces)))
        self.widths = [hidden, hidden, hidden, query_width, last]
        self.outs = [hidden, hidden, hidden, query_width, query_width, kv_width, kv_width]
        self.most = max(job[3] for job in self.plan)
        self.turned = [t for t, job in enumerate(self.plan) if job[0] in (0, 3)]
        self.pieces = max(len(job[4]) for job in self.plan)


class Inputs(NamedTuple):
    lengths: Any
    attn_gain: Any
    mlp_gain: Any
    tokens: Any
    cotangent: Any
    w_query: Any
    w_key: Any
    w_value: Any
    w_out: Any
    w_gate: Any
    w_up: Any
    w_down: Any


class Scratch(NamedTuple):
    tok_full: Any
    dy: Any
    one_full: Any
    middle: Any
    query: Any
    keys: Any
    values: Any
    mask: Any
    cosine: Any
    sine: Any
    valid: Any
    source: Any
    sent: Any
    came: Any
    sent_late: Any
    came_late: Any
    total: Any
    turned: Any
    gate_w: Any
    up_w: Any
    down_w: Any
    mlp_acc: Any
    norm_acc: Any
    two_full: Any
    db_full: Any
    x_came: Any
    x_sent: Any
    d_att: Any
    d_middle: Any
    stage: Any
    gain_part: Any
    gain_all: Any
    gain_came: Any
    gain_own: Any
    keys_acc: Any
    values_acc: Any
    local_sem: Any
    feat_send: Any
    feat_recv: Any
    near_send: Any
    near_recv: Any
    far_send: Any
    far_recv: Any
    out_sem: Any
    weight_sem: Any
    x_send: Any
    x_recv: Any
    gain_send: Any
    gain_recv: Any
    last_sem: Any
    first_sem: Any


def layer_kernel(jobs, bits, *refs):
    plan = jobs.plan
    inp = Inputs(*refs[: len(Inputs._fields)])
    refs = refs[len(Inputs._fields) :]
    outs = refs[: len(jobs.outs)]
    layer_out, token_grad, gains_out = refs[len(jobs.outs) : len(jobs.outs) + 3]
    refs = refs[len(jobs.outs) + 3 :]
    every, left, scr = refs[:5], refs[5:9], Scratch(*refs[9:])
    sent, came, total = scr.sent, scr.came, scr.total
    sent_late, came_late = scr.sent_late, scr.came_late
    local_sem, near_send, near_recv = scr.local_sem, scr.near_send, scr.near_recv
    tokens, width = scr.dy.shape
    own = tokens // 2
    rows = left[0].shape[0]
    half, quarter = rows // 2, rows // 4
    ring_total = total.shape[0]
    ring_sent = sent.shape[0]

    me = lax.axis_index("dp")
    rank = lax.axis_index("tensor")
    low, high = lax.rem(me, 4), lax.div(me, 4)
    bit = [lax.rem(lax.div(high, 2**s), 2) for s in range(bits)]
    mine = aligned(rank * own, own)

    partners = [1, 2, 3] + [4 << s for s in range(bits)]
    barrier = pltpu.get_barrier_semaphore()
    for by in partners:
        pl.semaphore_signal(barrier, inc=1, device_id={"dp": flip(me, by)}, device_id_type=MESH)
    pl.semaphore_signal(barrier, inc=1, device_id={"tensor": 1 - rank}, device_id_type=MESH)
    pl.semaphore_wait(barrier, len(partners) + 1)

    def remote(src, dst, send, recv, by):
        return pltpu.make_async_remote_copy(
            src_ref=src,
            dst_ref=dst,
            send_sem=send,
            recv_sem=recv,
            device_id={"dp": flip(me, by)},
            device_id_type=MESH,
        )

    def x_copy(src, dst, i):
        return pltpu.make_async_remote_copy(
            src_ref=src,
            dst_ref=dst,
            send_sem=scr.x_send.at[i],
            recv_sem=scr.x_recv.at[i],
            device_id={"tensor": 1 - rank},
            device_id_type=MESH,
        )


    def slot(array, j, start, columns):
        return every[array].at[pl.ds(j * tokens, tokens), pl.ds(start, columns)]

    def near(t, j):
        array, _, start, columns, _ = plan[t]
        src = slot(array, 2 if j == 3 else 0, start, columns)
        dst = slot(array, j, start, columns)
        return remote(src, dst, near_send.at[t, j], near_recv.at[t, j], 2 if j == 2 else 1)

    def stage_rows(s):
        return half - (half >> (s - 1)), quarter >> (s - 1)

    def far(t, s):
        columns = plan[t][3]
        if s == 0:
            src, dst = sent.at[t % ring_sent], came.at[t % RING]
            at = (slice(None), pl.ds(0, columns))
        else:
            src, dst = sent_late.at[t % ring_sent], came_late.at[t % RING]
            at = (pl.ds(*stage_rows(s)), pl.ds(0, columns))
        return remote(
            src.at[at], dst.at[at], scr.far_send.at[t, s], scr.far_recv.at[t, s], 4 << s
        )

    def final_row():
        row = 0
        for s in range(2, bits):
            row = row + bit[s] * (quarter >> (s - 1))
        return row

    last_size = quarter >> (bits - 2)

    def outputs(t):
        copies = []
        done = 0
        for i, (out, first, columns) in enumerate(plan[t][4]):
            if t in jobs.turned:
                src = scr.turned.at[jobs.turned.index(t) % 3].at[pl.ds(done, columns), :]
                dst = outs[out].at[pl.ds(first, columns), :]
                copies.append(pltpu.make_async_copy(src, dst, scr.out_sem.at[t, i]))
                continue
            copies.append(
                pltpu.make_async_copy(
                    total.at[t % ring_total].at[
                        aligned(final_row(), last_size), pl.ds(done, columns)
                    ],
                    outs[out].at[:, pl.ds(first, columns)],
                    scr.out_sem.at[t, i],
                )
            )
            done += columns
        return copies

    output_waited = set()

    def wait_outputs(t):
        if t >= 0 and t not in output_waited:
            output_waited.add(t)
            for copy in outputs(t):
                copy.wait()

    def tiles(t, body):
        _, _, start, columns, _ = plan[t]

        @pl.loop(0, columns // TILE)
        def _(i):
            body(aligned(start + i * TILE, TILE), aligned(i * TILE, TILE))

    def dot(t, first, size, at):
        array, f = plan[t][:2]
        return jnp.dot(
            left[f][aligned(first, size), :], every[array][:, at], preferred_element_type=jnp.float32
        )

    def first_pass(t):
        if t >= ring_sent:
            far(t - ring_sent, 0).wait_send()

        def body(at, to):
            out = dot(t, (1 - bit[0]) * half, half, at)
            sent[t % ring_sent, :, to] = out.astype(jnp.bfloat16)

        tiles(t, body)
        far(t, 0).start()

    def second_pass(t):
        far(t, 0).wait_recv()
        if t >= ring_sent:
            far(t - ring_sent, 1).wait_send()
        wait_outputs(t - ring_total)
        base = bit[0] * half

        def body(at, to):
            away, kept = (1 - bit[1]) * quarter, bit[1] * quarter
            out = dot(t, base + away, quarter, at)
            out = out + came[t % RING, aligned(away, quarter), to].astype(jnp.float32)
            sent_late[t % ring_sent, pl.ds(0, quarter), to] = out.astype(jnp.bfloat16)
            out = dot(t, base + kept, quarter, at)
            out = out + came[t % RING, aligned(kept, quarter), to].astype(jnp.float32)
            total[t % ring_total, :, to] = out

        tiles(t, body)
        far(t, 1).start()

    def later_pass(t, s):
        far(t, s - 1).wait_recv()
        if t >= ring_sent:
            far(t - ring_sent, s).wait_send()
        first, size = stage_rows(s - 1)
        piece = size // 2
        at_row = 0
        for q in range(2, s):
            at_row = at_row + bit[q] * (quarter >> (q - 1))
        away, kept = (1 - bit[s]) * piece, bit[s] * piece

        def body(at, to):
            out = total[t % ring_total, aligned(at_row + away, piece), to]
            out = out + came_late[t % RING, aligned(first + away, piece), to].astype(jnp.float32)
            sent_late[t % ring_sent, pl.ds(first + size, piece), to] = out.astype(jnp.bfloat16)
            row = aligned(at_row + kept, piece)
            out = total[t % ring_total, row, to]
            out = out + came_late[t % RING, aligned(first + kept, piece), to].astype(jnp.float32)
            total[t % ring_total, row, to] = out

        tiles(t, body)
        far(t, s).start()

    def last_pass(t):
        for s in range(2, bits):
            later_pass(t, s)
        far(t, bits - 1).wait_recv()
        first, size = stage_rows(bits - 1)
        if t in jobs.turned[3:]:
            wait_outputs(jobs.turned[jobs.turned.index(t) - 3])

        def body(at, to):
            row = aligned(final_row(), last_size)
            out = total[t % ring_total, row, to]
            out = out + came_late[t % RING, pl.ds(first, size), to].astype(jnp.float32)
            if t in jobs.turned:
                scr.turned[jobs.turned.index(t) % 3, to, :] = out.T
            else:
                total[t % ring_total, row, to] = out

        tiles(t, body)
        for copy in outputs(t):
            copy.start()

    feature_waited = set()

    def begin(t):
        near(t, 1).start()
        near(t, 2).start()

    def pass_on(t):
        near(t, 2).wait_recv()
        near(t, 3).start()

    def first_product(t):
        f = plan[t][1]
        if f not in feature_waited:
            feature_waited.add(f)
            for j in (1, 2, 3):
                feature_copy(f, j).wait_recv()
        near(t, 1).wait_recv()
        near(t, 3).wait_recv()
        first_pass(t)


    source_of = {0: 0, 3: 1, 1: 0, 2: 1}

    def feature_copy(f, j):
        return remote(
            scr.source.at[source_of[f], flip(low, j)],
            left[f].at[:, pl.ds(j * tokens, tokens)],
            scr.feat_send.at[f, j],
            scr.feat_recv.at[f, j],
            j,
        )

    def turn(ref, f):
        count = 4 << bits
        block = width // count
        source = scr.source.at[source_of[f]]

        @pl.loop(0, width // LANES)
        def _(c):
            turned = ref[:, aligned(c * LANES, LANES)].T
            for piece in range(LANES // block):
                d = c * (LANES // block) + piece
                group = lax.div(d, 4)
                place = 0
                for s in range(bits):
                    place = place + lax.rem(lax.div(group, 2**s), 2) * 2 ** (bits - 1 - s)
                source[lax.rem(d, 4), aligned(place * block, block), :] = turned[
                    piece * block : (piece + 1) * block
                ]

        left[f][:, pl.ds(0, tokens)] = source[low]

    def send_features(f):
        for j in (2, 3, 1):
            feature_copy(f, j).start()


    weight_sem = scr.weight_sem

    def hidden_weights(i):
        at = lax.rem(i, 2)
        columns = aligned(i * TILE, TILE)
        return (
            pltpu.make_async_copy(
                inp.w_gate.at[:, columns], scr.gate_w.at[at], weight_sem.at[0, at]
            ),
            pltpu.make_async_copy(
                inp.w_up.at[:, columns], scr.up_w.at[at], weight_sem.at[1, at]
            ),
            pltpu.make_async_copy(
                inp.w_down.at[columns, :], scr.down_w.at[at], weight_sem.at[2, at]
            ),
        )

    hidden_tiles = jobs.outs[0] // TILE
    wide = 512

    def hidden_part(first, count):
        @pl.loop(first, first + count)
        def _(i):
            at = lax.rem(i, 2)

            @pl.when(i + 1 < hidden_tiles)
            def _():
                for copy in hidden_weights(i + 1):
                    copy.start()

            for copy in hidden_weights(i):
                copy.wait()
            gate_w, up_w, down_w = scr.gate_w.at[at], scr.up_w.at[at], scr.down_w.at[at]
            two = scr.two_full[...]
            gate = jnp.dot(two, gate_w[...], preferred_element_type=jnp.float32)
            up = jnp.dot(two, up_w[...], preferred_element_type=jnp.float32)
            d_act = against(scr.dy[...], down_w[...])
            sig = jax.nn.sigmoid(gate)
            silu = gate * sig
            act = (silu * up).astype(jnp.bfloat16)
            d_gate = (d_act * up * sig * (1.0 + gate * (1.0 - sig))).astype(jnp.bfloat16)
            d_up = (d_act * silu).astype(jnp.bfloat16)
            columns = aligned(i * TILE, TILE)
            every[0][pl.ds(0, tokens), columns] = act
            every[1][pl.ds(0, tokens), columns] = d_gate
            every[2][pl.ds(0, tokens), columns] = d_up

            @pl.loop(0, width // wide)
            def _(n):
                part = aligned(n * wide, wide)
                scr.mlp_acc[:, part] += jnp.dot(
                    act, down_w[:, part], preferred_element_type=jnp.float32
                )
                scr.norm_acc[:, part] += against(d_gate, gate_w[part, :]) + against(
                    d_up, up_w[part, :]
                )

    def row_loop(body):
        @pl.loop(0, own // ROWS)
        def _(i):
            body(aligned(i * ROWS, ROWS), aligned(rank * own + i * ROWS, ROWS))

    def eight(value):
        return jnp.sum(value.reshape(ROWS // 8, 8, width), axis=0)

    def send_partial(acc, buffer):
        @pl.loop(0, own // ROWS)
        def _(i):
            row = aligned((1 - rank) * own + i * ROWS, ROWS)
            scr.x_sent[buffer, aligned(i * ROWS, ROWS), :] = acc[row, :].astype(
                jnp.bfloat16
            )


    def out_weights(i):
        return pltpu.make_async_copy(
            inp.w_out.at[aligned(i * TILE, TILE), :],
            scr.down_w.at[lax.rem(i, 2)],
            weight_sem.at[2, lax.rem(i, 2)],
        )

    def query_buffer(j):
        return (scr.gate_w, scr.up_w)[j % 4 // 2].at[j % 2]

    def query_weights(j):
        dst, sem = query_buffer(j), weight_sem.at[j % 4 // 2, j % 2]
        if j < query_tiles:
            return [
                pltpu.make_async_copy(inp.w_query.at[:, pl.ds(j * TILE, TILE)], dst, sem)
            ]
        kv = inp.w_key.shape[1]
        return [
            pltpu.make_async_copy(inp.w_key, dst.at[:, pl.ds(0, kv)], sem),
            pltpu.make_async_copy(inp.w_value, dst.at[:, pl.ds(kv, kv)], scr.last_sem.at[2]),
        ]

    query_width = jobs.outs[3]
    kv_width = jobs.outs[5]
    query_tiles = query_width // TILE
    kv_heads = kv_width // HD
    pairs = query_width // LANES // kv_heads
    score_scale = HD ** (-0.5)

    def lane_masks():
        lane = lax.broadcasted_iota(jnp.int32, (1, LANES), 1)
        first = (lane < HD).astype(jnp.float32)
        return first, 1.0 - first

    def unrotate(value):
        lane = lax.broadcasted_iota(jnp.int32, value.shape, 1)
        other = jnp.where(
            lax.rem(lane, HD) < HD // 2,
            pltpu.roll(value, LANES - HD // 2, 1),
            pltpu.roll(value, HD // 2, 1),
        )
        return value * scr.cosine[...] + other * scr.sine[...]

    def d_attended():
        @pl.loop(0, query_tiles)
        def _(i):
            out_weights(i).wait()
            scr.d_att[:, aligned(i * TILE, TILE)] = against(
                scr.db_full[...], scr.down_w[lax.rem(i, 2)]
            ).astype(jnp.bfloat16)

            @pl.when(i + 2 < query_tiles)
            def _():
                out_weights(i + 2).start()

    def attend_back(kv):
        keys, values = scr.keys.at[kv], scr.values.at[kv]
        keys_acc, values_acc = scr.keys_acc.at[kv], scr.values_acc.at[kv]
        keys_acc[...] = jnp.zeros_like(keys_acc)
        values_acc[...] = jnp.zeros_like(values_acc)

        @pl.loop(0, pairs)
        def _(p):
            columns = aligned((kv * pairs + p) * LANES, LANES)
            d_query = jnp.zeros((tokens, LANES), jnp.float32)
            for lanes in lane_masks():
                lanes_low = lanes.astype(jnp.bfloat16)
                query = scr.query[:, columns] * lanes_low
                d_att = scr.d_att[:, columns] * lanes_low
                scores = against(query, keys[...]) * score_scale
                scores = jnp.where(scr.mask[...] > 0, scores, masked_score)
                expo = jnp.exp(scores - jnp.max(scores, axis=1, keepdims=True))
                probs = expo * (1.0 / jnp.sum(expo, axis=1, keepdims=True))
                d_probs = against(d_att, values[...])
                inner = jnp.sum(probs * d_probs, axis=1, keepdims=True)
                d_scores = (probs * (d_probs - inner)).astype(jnp.bfloat16)
                d_query = d_query + lanes * jnp.dot(
                    d_scores, keys[...], preferred_element_type=jnp.float32
                )
                keys_acc[...] += inner_rows(d_scores, query)
                values_acc[...] += inner_rows(probs.astype(jnp.bfloat16), d_att)
            every[4][pl.ds(0, tokens), columns] = unrotate(d_query * score_scale).astype(
                jnp.bfloat16
            )

    def finish_keys():
        lanes = lane_masks()
        d_key = jnp.zeros((tokens, LANES), jnp.float32)
        d_value = jnp.zeros((tokens, LANES), jnp.float32)
        for kv in range(kv_heads):
            for out in (0, 1):
                acc = (scr.keys_acc, scr.values_acc)[out][kv]
                acc = (acc + pltpu.roll(acc, HD, 1)) * lanes[kv]
                if out == 0:
                    d_key = d_key + acc
                else:
                    d_value = d_value + acc
        d_key = unrotate(d_key * score_scale)
        every[4][pl.ds(0, tokens), pl.ds(query_width, kv_width)] = d_key.astype(jnp.bfloat16)
        every[4][pl.ds(0, tokens), pl.ds(query_width + kv_width, kv_width)] = d_value.astype(
            jnp.bfloat16
        )

    def d_normed_one():
        for j in range(query_tiles + 1):
            for copy in query_weights(j):
                copy.wait()
            weights = query_buffer(j)
            grads = every[4][pl.ds(0, tokens), pl.ds(j * TILE, TILE)]

            @pl.loop(0, width // wide)
            def _(n):
                part = aligned(n * wide, wide)
                add = against(grads, weights[part, :])
                if j == 0:
                    scr.norm_acc[:, part] = add
                else:
                    scr.norm_acc[:, part] += add

            if j + 4 < query_tiles + 1:
                for copy in query_weights(j + 4):
                    copy.start()


    def mean_rows(value):
        return jnp.mean(value, axis=1, keepdims=True)

    def middle_back(row, full):
        grad = scr.norm_acc[full, :] + scr.x_came[0, row, :].astype(jnp.float32)
        middle = scr.middle[row, :]
        scale = lax.rsqrt(mean_rows(middle * middle) + norm_eps)
        normed = middle * scale
        scr.gain_part[0] += eight(grad * normed)
        scaled = grad * inp.mlp_gain[...]
        d_middle = scr.dy[full, :].astype(jnp.float32) + scale * (
            scaled - normed * mean_rows(scaled * normed)
        )
        scr.d_middle[row, :] = d_middle
        scr.db_full[full, :] = d_middle.astype(jnp.bfloat16)

    def finish_layer(row, full):
        mlp = scr.mlp_acc[full, :] + scr.x_came[1, row, :].astype(jnp.float32)
        scr.stage[row, :] = (scr.middle[row, :] + mlp).astype(jnp.bfloat16)

    def token_back(row, full):
        grad = scr.norm_acc[full, :] + scr.x_came[2, row, :].astype(jnp.float32)
        valid = scr.valid[full, :][:, :1]
        masked = scr.tok_full[full, :].astype(jnp.float32) * valid
        scale = lax.rsqrt(mean_rows(masked * masked) + norm_eps)
        normed = masked * scale
        scr.gain_part[1] += eight(grad * normed)
        scaled = grad * inp.attn_gain[...]
        out = scr.d_middle[row, :] + scale * (scaled - normed * mean_rows(scaled * normed))
        scr.stage[row, :] = (out * valid).astype(jnp.bfloat16)

    def gain_copy(i):
        src, dst = scr.gain_all.at[i], scr.gain_came.at[i]
        if i < bits + 2:
            return remote(src, dst, scr.gain_send.at[i], scr.gain_recv.at[i], 1 << i)
        return pltpu.make_async_remote_copy(
            src_ref=src,
            dst_ref=dst,
            send_sem=scr.gain_send.at[i],
            recv_sem=scr.gain_recv.at[i],
            device_id={"tensor": 1 - rank},
            device_id_type=MESH,
        )

    gain_steps = bits + 3

    def gain_next(i):
        gain_copy(i).wait_recv()
        scr.gain_all[i + 1] = scr.gain_all[i] + scr.gain_came[i]
        if i + 1 < gain_steps:
            gain_copy(i + 1).start()


    def prepare():
        ends = []
        for k in range(inp.lengths.shape[0]):
            ends.append(inp.lengths[k] + (ends[-1] if ends else 0))

        def segments(shape, axis):
            place = lax.broadcasted_iota(jnp.int32, shape, axis)
            return place, sum((place >= end).astype(jnp.int32) for end in ends)

        place, _ = segments((tokens, LANES), 0)
        start = jnp.zeros_like(place)
        for end in ends:
            start = jnp.maximum(start, jnp.where(place >= end, end, 0))
        scr.valid[...] = (place < ends[-1]).astype(jnp.float32)
        lane = lax.broadcasted_iota(jnp.int32, (tokens, LANES), 1)
        slow = lax.rem(lane, HD // 2).astype(jnp.float32)
        inverse = jnp.exp(slow * (-2.0 * math.log(10000.0) / HD))
        angles = (place - start).astype(jnp.float32) * inverse
        scr.cosine[...] = jnp.cos(angles)
        sine = jnp.sin(angles)
        scr.sine[...] = jnp.where(lax.rem(lane, HD) < HD // 2, sine, -sine)
        rows_at, row_segment = segments((tokens, tokens), 0)
        columns_at, column_segment = segments((tokens, tokens), 1)
        seen = (row_segment == column_segment) & (columns_at <= rows_at)
        scr.mask[...] = seen.astype(jnp.float32)


    def query_half(k):
        return every[2].at[pl.ds(0, width // 2), pl.ds(k * query_width, query_width)]

    def out_all():
        return every[1].at[pl.ds(0, query_width), pl.ds(0, width)]

    def forward_weights():
        dst = scr.gate_w.at[1]
        copies = [
            pltpu.make_async_copy(
                inp.w_query.at[pl.ds(k * width // 2, width // 2), :],
                query_half(k),
                scr.first_sem.at[k],
            )
            for k in range(2)
        ]
        for k, ref in ((0, inp.w_key), (1, inp.w_value)):
            copies.append(
                pltpu.make_async_copy(
                    ref, dst.at[:, pl.ds(k * kv_width, kv_width)], scr.first_sem.at[2 + k]
                )
            )
        copies.append(pltpu.make_async_copy(inp.w_out, out_all(), scr.first_sem.at[4]))
        return copies

    def all_rows(body):
        @pl.loop(0, tokens // ROWS)
        def _(i):
            body(aligned(i * ROWS, ROWS))

    def first_norm(row, full):
        one_rows(full)

    def one_rows(full):
        masked = scr.tok_full[full, :].astype(jnp.float32) * scr.valid[full, :][:, :1]
        scale = lax.rsqrt(mean_rows(masked * masked) + norm_eps)
        scr.one_full[full, :] = (masked * scale * inp.attn_gain[...]).astype(jnp.bfloat16)

    def mask_cotangent(full):
        dy = scr.dy[full, :].astype(jnp.float32) * scr.valid[full, :][:, :1]
        scr.dy[full, :] = dy.astype(jnp.bfloat16)

    def rotated(value, row):
        lane = lax.broadcasted_iota(jnp.int32, value.shape, 1)
        other = jnp.where(
            lax.rem(lane, HD) < HD // 2,
            pltpu.roll(value, LANES - HD // 2, 1),
            pltpu.roll(value, HD // 2, 1),
        )
        return value * scr.cosine[row, :] - other * scr.sine[row, :]

    def projections(row):
        @pl.loop(0, query_tiles)
        def _(j):
            columns = aligned(j * TILE, TILE)
            out = jnp.dot(
                scr.one_full[row, : width // 2],
                query_half(0)[:, columns],
                preferred_element_type=jnp.float32,
            )
            out = out + jnp.dot(
                scr.one_full[row, width // 2 :],
                query_half(1)[:, columns],
                preferred_element_type=jnp.float32,
            )
            for k in range(TILE // LANES):
                part = rotated(out[:, k * LANES : (k + 1) * LANES], row)
                scr.query[row, aligned(j * TILE + k * LANES, LANES)] = part.astype(jnp.bfloat16)

        out = jnp.dot(scr.one_full[row, :], scr.gate_w[1], preferred_element_type=jnp.float32)
        lane = lax.broadcasted_iota(jnp.int32, (own, LANES), 1)
        for k, ref in ((0, scr.keys), (1, scr.values)):
            part = out[:, k * LANES : (k + 1) * LANES]
            part = rotated(part, row) if k == 0 else part
            part = part.astype(jnp.bfloat16).astype(jnp.float32)
            turned = pltpu.roll(part, HD, 1)
            ref[0, row, :] = jnp.where(lane < HD, part, turned).astype(jnp.bfloat16)
            ref[1, row, :] = jnp.where(lane < HD, turned, part).astype(jnp.bfloat16)

    def attend(row):
        for kv in range(kv_heads):

            @pl.loop(0, pairs)
            def _(p):
                columns = aligned((kv * pairs + p) * LANES, LANES)
                out = jnp.zeros((own, LANES), jnp.float32)
                for lanes in lane_masks():
                    query = scr.query[row, columns] * lanes.astype(jnp.bfloat16)
                    scores = against(query, scr.keys[kv]) * score_scale
                    scores = jnp.where(scr.mask[row, :] > 0, scores, masked_score)
                    expo = jnp.exp(scores - jnp.max(scores, axis=1, keepdims=True))
                    probs = expo * (1.0 / jnp.sum(expo, axis=1, keepdims=True))
                    out = out + lanes * jnp.dot(
                        probs.astype(jnp.bfloat16), scr.values[kv], preferred_element_type=jnp.float32
                    )
                every[3][row, columns] = out.astype(jnp.bfloat16)

    def out_rows(row, store):
        @pl.loop(0, width // wide)
        def _(n):
            part = aligned(n * wide, wide)
            store(
                part,
                jnp.dot(
                    every[3][row, :],
                    every[1][pl.ds(0, query_width), part],
                    preferred_element_type=jnp.float32,
                ),
            )

    def middle_forward(row, full):
        masked = scr.tok_full[full, :].astype(jnp.float32) * scr.valid[full, :][:, :1]
        middle = masked + (scr.norm_acc[row, :] + scr.x_came[0, row, :].astype(jnp.float32))
        scale = lax.rsqrt(mean_rows(middle * middle) + norm_eps)
        scr.middle[row, :] = middle
        scr.two_full[full, :] = (middle * scale * inp.mlp_gain[...]).astype(jnp.bfloat16)


    first_copies = [
        (x_copy(ref, full.at[mine, :], i), pltpu.make_async_copy(ref, full.at[mine, :], local_sem.at[i]))
        for i, (ref, full) in enumerate(((inp.tokens, scr.tok_full), (inp.cotangent, scr.dy)))
    ]
    for copy in first_copies[0]:
        copy.start()
    loads = forward_weights()
    for copy in loads:
        copy.start()
    first_copies[1][1].start()
    prepare()
    first_copies[0][1].wait()
    row_loop(first_norm)
    for copy in loads:
        copy.wait()
    projections(mine)
    theirs = aligned((1 - rank) * own, own)
    first_copies[0][0].wait_recv()
    first_copies[1][0].start()

    @pl.loop(0, own // ROWS)
    def _(i):
        one_rows(aligned((1 - rank) * own + i * ROWS, ROWS))

    projections(theirs)
    turn(scr.one_full, 3)
    send_features(3)
    attend(theirs)

    def store_theirs(part, out):
        scr.x_sent[0, :, part] = out.astype(jnp.bfloat16)

    def store_mine(part, out):
        scr.norm_acc[pl.ds(0, own), part] = out

    out_rows(theirs, store_theirs)
    branch_copy = x_copy(scr.x_sent.at[0], scr.x_came.at[0], 2)
    branch_copy.start()
    first_copies[1][1].wait()
    first_copies[1][0].wait_recv()
    all_rows(mask_cotangent)
    turn(scr.dy, 0)
    send_features(0)
    attend(mine)
    for copy in hidden_weights(0):
        copy.start()
    out_rows(mine, store_mine)
    branch_copy.wait_recv()
    row_loop(middle_forward)
    two_copy = x_copy(scr.two_full.at[mine, :], scr.two_full.at[mine, :], 3)
    two_copy.start()
    scr.mlp_acc[...] = jnp.zeros_like(scr.mlp_acc)
    scr.norm_acc[...] = jnp.zeros_like(scr.norm_acc)
    scr.gain_part[...] = jnp.zeros_like(scr.gain_part)
    two_copy.wait_recv()
    norm_copy = x_copy(scr.x_sent.at[0], scr.x_came.at[0], 4)
    db_copy = x_copy(scr.db_full.at[mine, :], scr.db_full.at[mine, :], 5)
    mlp_copy = x_copy(scr.x_sent.at[1], scr.x_came.at[1], 6)
    one_copy = x_copy(scr.x_sent.at[0], scr.x_came.at[2], 7)
    layer_copy = pltpu.make_async_copy(scr.stage, layer_out, scr.last_sem.at[0])
    token_copy = pltpu.make_async_copy(scr.stage, token_grad, scr.last_sem.at[1])
    gains_copy = pltpu.make_async_copy(scr.gain_own, gains_out, local_sem.at[1])

    def send_norm():
        branch_copy.wait_send()
        send_partial(scr.norm_acc, 0)
        norm_copy.start()
        for i in range(2):
            out_weights(i).start()
        for j in range(4):
            for copy in query_weights(j):
                copy.start()

    def middle_grads():
        norm_copy.wait_recv()
        row_loop(middle_back)
        db_copy.start()

    def attended_grads():
        db_copy.wait_recv()
        mlp_copy.start()
        d_attended()

    def last_keys():
        attend_back(1)
        finish_keys()

    def layer_end():
        d_normed_one()
        norm_copy.wait_send()
        send_partial(scr.norm_acc, 0)
        one_copy.start()
        mlp_copy.wait_recv()
        row_loop(finish_layer)
        layer_copy.start()

    def token_end():
        layer_copy.wait()
        one_copy.wait_recv()
        row_loop(token_back)
        token_copy.start()
        gains = scr.gain_all.at[0]
        gains[...] = jnp.zeros_like(gains)
        for i in range(2):
            gains[pl.ds(i, 1), :] = jnp.sum(scr.gain_part[i], axis=0, keepdims=True)

    chain = {
        1: send_norm,
        2: lambda: send_partial(scr.mlp_acc, 1),
        3: middle_grads,
        4: attended_grads,
        5: lambda: attend_back(0),
        6: last_keys,
        7: layer_end,
        8: token_end,
    }

    def send(f):
        for j in (1, 2, 3):
            feature_copy({1: 0, 2: 3}[f], j).wait_send()
        turn({1: scr.two_full, 2: scr.db_full}[f], f)
        send_features(f)

    def gain(i):
        if i == 0:
            gain_copy(0).start()
        elif i < 5:
            gain_next(i - 1)
        else:
            for step in range(4, gain_steps):
                gain_next(step)
            gain_rows = width // (2 * (4 << bits))
            place = (2 * me + rank) * gain_rows
            block = scr.gain_all[gain_steps, :, aligned(lax.div(place, LANES) * LANES, LANES)]
            scr.gain_own[...] = pltpu.roll(block, lax.rem(LANES - lax.rem(place, LANES), LANES), 1)
            gains_copy.start()

    steps = {
        BEGIN: begin,
        PASS: pass_on,
        FIRST: first_product,
        SECOND: second_pass,
        LAST: last_pass,
        SEND: send,
        CHAIN: lambda i: chain[i](),
        GAIN: gain,
    }
    at = 0
    while at < len(ORDER):
        kind, number = ORDER[at] // 100 * 100, ORDER[at] % 100
        at += 1
        if kind == TILES:
            count = 1
            while at < len(ORDER) and ORDER[at] == number + count:
                count, at = count + 1, at + 1
            hidden_part(number, count)
        else:
            steps[kind](number)


    for copy, _ in first_copies:
        copy.wait_send()
    two_copy.wait_send()
    db_copy.wait_send()
    mlp_copy.wait_send()
    one_copy.wait_send()
    token_copy.wait()
    gains_copy.wait()
    for i in range(gain_steps):
        gain_copy(i).wait_send()
    for f in (1, 2):
        for j in (1, 2, 3):
            feature_copy(f, j).wait_send()
    for t in range(len(plan)):
        for j in (1, 2, 3):
            near(t, j).wait_send()
        if t + ring_sent >= len(plan):
            for s in range(bits):
                far(t, s).wait_send()
        wait_outputs(t)


def layer_call(jobs, args, tokens, width):
    count = lax.axis_size("dp")
    bits = (count // 4).bit_length() - 1
    rows = width // 4
    block = width // count
    own = tokens // 2
    plan = jobs.plan
    vmem, any_space = pl.BlockSpec(memory_space=pltpu.VMEM), pl.BlockSpec(memory_space=pl.ANY)
    bf16, f32 = jnp.bfloat16, jnp.float32
    late_rows = rows // 2 - (rows // 2 >> (bits - 1))
    ring_total = max(4, bits + 1)
    kv_heads = jobs.outs[5] // HD
    dma = pltpu.SemaphoreType.DMA
    scratch = Scratch(
        tok_full=pltpu.VMEM((tokens, width), bf16),
        dy=pltpu.VMEM((tokens, width), bf16),
        one_full=pltpu.VMEM((tokens, width), bf16),
        middle=pltpu.VMEM((own, width), f32),
        query=pltpu.VMEM((tokens, jobs.outs[3]), bf16),
        keys=pltpu.VMEM((kv_heads, tokens, LANES), bf16),
        values=pltpu.VMEM((kv_heads, tokens, LANES), bf16),
        mask=pltpu.VMEM((tokens, tokens), f32),
        cosine=pltpu.VMEM((tokens, LANES), f32),
        sine=pltpu.VMEM((tokens, LANES), f32),
        valid=pltpu.VMEM((tokens, LANES), f32),
        source=pltpu.VMEM((2, 4, rows, tokens), bf16),
        sent=pltpu.VMEM((3, rows // 2, jobs.most), bf16),
        came=pltpu.VMEM((RING, rows // 2, jobs.most), bf16),
        sent_late=pltpu.VMEM((3, late_rows, jobs.most), bf16),
        came_late=pltpu.VMEM((RING, late_rows, jobs.most), bf16),
        total=pltpu.VMEM((ring_total, rows // 4, jobs.most), f32),
        turned=pltpu.VMEM((3, jobs.most, block), f32),
        gate_w=pltpu.VMEM((2, width, TILE), bf16),
        up_w=pltpu.VMEM((2, width, TILE), bf16),
        down_w=pltpu.VMEM((2, TILE, width), bf16),
        mlp_acc=pltpu.VMEM((tokens, width), f32),
        norm_acc=pltpu.VMEM((tokens, width), f32),
        two_full=pltpu.VMEM((tokens, width), bf16),
        db_full=pltpu.VMEM((tokens, width), bf16),
        x_came=pltpu.VMEM((3, own, width), bf16),
        x_sent=pltpu.VMEM((2, own, width), bf16),
        d_att=pltpu.VMEM((tokens, jobs.outs[3]), bf16),
        d_middle=pltpu.VMEM((own, width), f32),
        stage=pltpu.VMEM((own, width), bf16),
        gain_part=pltpu.VMEM((2, 8, width), f32),
        gain_all=pltpu.VMEM((bits + 4, 8, width), f32),
        gain_came=pltpu.VMEM((bits + 3, 8, width), f32),
        gain_own=pltpu.VMEM((8, LANES), f32),
        keys_acc=pltpu.VMEM((kv_heads, tokens, LANES), f32),
        values_acc=pltpu.VMEM((kv_heads, tokens, LANES), f32),
        local_sem=dma((2,)),
        feat_send=dma((4, 4)),
        feat_recv=dma((4, 4)),
        near_send=dma((len(plan), 4)),
        near_recv=dma((len(plan), 4)),
        far_send=dma((len(plan), bits)),
        far_recv=dma((len(plan), bits)),
        out_sem=dma((len(plan), jobs.pieces)),
        weight_sem=dma((3, 2)),
        x_send=dma((8,)),
        x_recv=dma((8,)),
        gain_send=dma((bits + 3,)),
        gain_recv=dma((bits + 3,)),
        last_sem=dma((3,)),
        first_sem=dma((5,)),
    )
    operands = [pltpu.VMEM((4 * tokens, w), bf16) for w in jobs.widths]
    operands += [pltpu.VMEM((rows, 4 * tokens), bf16)] * 4
    return pl.pallas_call(
        functools.partial(layer_kernel, jobs, bits),
        out_shape=[
            jax.ShapeDtypeStruct((w, block) if i in (0, 3) else (block, w), f32)
            for i, w in enumerate(jobs.outs)
        ]
        + [
            jax.ShapeDtypeStruct((own, width), bf16),
            jax.ShapeDtypeStruct((own, width), bf16),
            jax.ShapeDtypeStruct((8, LANES), f32),
        ],
        in_specs=[pl.BlockSpec(memory_space=pltpu.SMEM), vmem, vmem] + [any_space] * (len(args) - 3),
        out_specs=[any_space] * (len(jobs.outs) + 3),
        scratch_shapes=operands + list(scratch),
        compiler_params=pltpu.CompilerParams(
            collective_id=0, has_side_effects=True, vmem_limit_bytes=63 * 1024 * 1024
        ),
    )(*args)


PIECES = 2


def hand_over_kernel(count, gain_rows, *refs):
    gains, refs = refs[0], refs[1:]
    inputs, outs = refs[:count], refs[count : 2 * count]
    attn_out, mlp_out = refs[2 * count : 2 * count + 2]
    held = refs[2 * count + 2 : 3 * count + 2]
    in_sem, out_sem = refs[3 * count + 2 :]
    pairs = []
    for i in range(count):
        rows = inputs[i].shape[0] // PIECES
        for piece in range(PIECES):
            at = pl.ds(piece * rows, rows)
            pairs.append(
                (
                    pltpu.make_async_copy(inputs[i].at[at], held[i].at[at], in_sem.at[i, piece]),
                    pltpu.make_async_copy(held[i].at[at], outs[i].at[at], out_sem.at[i, piece]),
                )
            )
    for copy, _ in pairs:
        copy.start()
    mlp_out[...] = gains[0:1, :gain_rows]
    attn_out[...] = gains[1:2, :gain_rows]
    for come, go in pairs:
        come.wait()
        go.start()
    for _, copy in pairs:
        copy.wait()


def hand_over(arrays, gains, gain_rows):
    any_space, vmem = pl.BlockSpec(memory_space=pl.ANY), pl.BlockSpec(memory_space=pltpu.VMEM)
    gain = jax.ShapeDtypeStruct((1, gain_rows), jnp.float32)
    return pl.pallas_call(
        functools.partial(hand_over_kernel, len(arrays), gain_rows),
        out_shape=[jax.ShapeDtypeStruct(x.shape, x.dtype) for x in arrays] + [gain, gain],
        in_specs=[vmem] + [any_space] * len(arrays),
        out_specs=[any_space] * len(arrays) + [vmem, vmem],
        scratch_shapes=[pltpu.VMEM(x.shape, x.dtype) for x in arrays]
        + [pltpu.SemaphoreType.DMA((len(arrays), PIECES))] * 2,
    )(gains, *arrays)


def on_device(
    tokens,
    frag_lengths,
    attn_gain,
    w_query,
    w_key,
    w_value,
    w_out,
    mlp_gain,
    w_gate,
    w_up,
    w_down,
    out_cotangent,
):
    tok_rows, model_width = tokens.shape
    pack_rows = tok_rows * lax.axis_size("tensor")
    rank = lax.axis_index("tensor")
    jobs = Jobs(w_gate.shape[1], w_query.shape[1], w_key.shape[1])
    args = Inputs(
        lengths=frag_lengths,
        attn_gain=attn_gain[None, :],
        mlp_gain=mlp_gain[None, :],
        tokens=tokens,
        cotangent=out_cotangent,
        w_query=w_query,
        w_key=w_key,
        w_value=w_value,
        w_out=w_out,
        w_gate=w_gate,
        w_up=w_up,
        w_down=w_down,
    )
    out = layer_call(jobs, args, pack_rows, model_width)
    gain_rows = model_width // (lax.axis_size("tensor") * lax.axis_size("dp"))
    out = hand_over(out[:-1], out[-1], gain_rows)
    g_down, g_gate, g_up, g_out, g_query, g_key, g_value, layer_out, token_grad = out[:9]
    return (
        layer_out,
        token_grad,
        out[9][0],
        g_query,
        g_key,
        g_value,
        g_out,
        out[10][0],
        g_gate,
        g_up,
        g_down,
    )


def solution(mesh):
    placed = (
        P(("dp", "tensor"), None),
        P("dp"),
        P(),
        P(None, "tensor"),
        P(None, "tensor"),
        P(None, "tensor"),
        P("tensor", None),
        P(),
        P(None, "tensor"),
        P(None, "tensor"),
        P("tensor", None),
        P(("dp", "tensor"), None),
    )
    return jax.shard_map(
        on_device,
        mesh=mesh,
        in_specs=placed,
        out_specs=(
            P(("dp", "tensor"), None),
            P(("dp", "tensor"), None),
            P(("dp", "tensor")),
            P("dp", "tensor"),
            P("dp", "tensor"),
            P("dp", "tensor"),
            P("tensor", "dp"),
            P(("dp", "tensor")),
            P("dp", "tensor"),
            P("dp", "tensor"),
            P("tensor", "dp"),
        ),
        check_vma=False,
    )
```

```python
import functools
import math
from typing import Any, NamedTuple

import jax
import jax.numpy as jnp
from jax import lax
from jax.experimental import pallas as pl
from jax.experimental.pallas import tpu as pltpu
from jax.sharding import PartitionSpec as P

HD = 64
MESH = pl.DeviceIdType.MESH
TILE = 256
MOST = 1024
LANES = 128
RING = 4
ROWS = 16


norm_eps = 1e-05
masked_score = -1e30


def against(left, right):
    return lax.dot_general(
        left, right, (((1,), (1,)), ((), ())), preferred_element_type=jnp.float32
    )


def inner_rows(left, right):
    return lax.dot_general(
        left, right, (((0,), (0,)), ((), ())), preferred_element_type=jnp.float32
    )


def flip(value, by):
    for step in range(by.bit_length()):
        if by >> step & 1:
            value = value + (1 - 2 * lax.rem(lax.div(value, 2**step), 2)) * 2**step
    return value


def aligned(start, size):
    return pl.ds(pl.multiple_of(start, size), size)


def in_parts(tiles, shares):
    ends = [round(tiles * sum(shares[: i + 1]) / sum(shares)) for i in range(len(shares))]
    return [(start, end - start) for start, end in zip([0] + ends[:-1], ends)]


SHARES = ((1, 2, 2, 3, 3), (2, 3, 3, 3), (3, 3, 3, 2), (2, 2), (2, 2, 1))

TILES, BEGIN, PASS, FIRST, SECOND, LAST, SEND, CHAIN, GAIN, PAIR, AGAIN, ACROSS = range(0, 1200, 100)
ORDER = (
    601, 0, 100, 1, 2, 3, 900, 101, 4, 200, 5, 901, 1101, 6, 102, 1000,
    7, 201, 103, 1001, 300, 8, 202, 902, 9, 301, 903, 10, 1002, 203, 400, 701,
    104, 302, 105, 702, 500, 1003, 303, 904, 401, 205, 204, 703, 402, 106, 501, 1004,
    403, 304, 305, 502, 107, 503, 206, 306, 108, 207, 404, 704, 405, 109, 307, 705,
    110, 112, 208, 406, 706, 308, 504, 505, 407, 111, 506, 209, 707, 309, 210, 602,
    114, 408, 310, 507, 211, 113, 409, 1102, 116, 508, 708, 311, 509, 214, 216, 800,
    213, 410, 212, 312, 801, 115, 411, 215, 313, 510, 412, 802, 314, 117, 511, 803,
    413, 315, 512, 414, 513, 804, 316, 415, 514, 805, 217, 317, 416, 515, 417, 516,
    517,
)


class Jobs:
    def __init__(self, hidden, query_width, kv_width):
        tiles = hidden // TILE
        last = query_width + 2 * kv_width
        whole = ((4, 0, query_width), (5, query_width, kv_width), (6, query_width + kv_width, kv_width))
        self.plan = []
        for first, count in in_parts(tiles, SHARES[0]):
            self.plan.append((0, 0, first * LANES, count * LANES, ()))
        self.halved = len(self.plan)
        for array, feature, width, shares in (
            (1, 1, hidden, SHARES[1]),
            (2, 1, hidden, SHARES[2]),
            (3, 2, query_width, SHARES[3]),
            (4, 3, last, SHARES[4]),
        ):
            for first, count in in_parts(width // TILE, shares):
                start, columns = first * TILE, count * TILE
                pieces = []
                for out, at, size in whole if array == 4 else ((array, 0, width),):
                    low, high = max(at, start), min(at + size, start + columns)
                    if low < high:
                        pieces.append((out, low - at, high - low))
                self.plan.append((array, feature, start, columns, tuple(pieces)))
        self.widths = [hidden, hidden, hidden, query_width, last]
        self.outs = [hidden, hidden, hidden, query_width, query_width, kv_width, kv_width]
        self.most = max(job[3] for job in self.plan)
        self.turned = [t for t, job in enumerate(self.plan) if job[0] in (0, 3)]
        self.most_halved = max(job[3] for job in self.plan[: self.halved])
        self.pieces = 3


class Inputs(NamedTuple):
    lengths: Any
    attn_gain: Any
    mlp_gain: Any
    tokens: Any
    cotangent: Any
    w_query: Any
    w_key: Any
    w_value: Any
    w_out: Any
    w_gate: Any
    w_up: Any
    w_down: Any


class Scratch(NamedTuple):
    tok_full: Any
    dy: Any
    one_full: Any
    middle: Any
    query: Any
    keys: Any
    values: Any
    mask: Any
    cosine: Any
    sine: Any
    valid: Any
    source: Any
    sent: Any
    came: Any
    sent_late: Any
    came_late: Any
    total: Any
    turned: Any
    gate_w: Any
    up_w: Any
    down_w: Any
    mlp_acc: Any
    norm_acc: Any
    two_full: Any
    x_came: Any
    x_sent: Any
    d_att: Any
    gain_part: Any
    gain_all: Any
    gain_came: Any
    gain_own: Any
    pair_sent: Any
    pair_came: Any
    pair_send: Any
    pair_recv: Any
    keys_acc: Any
    values_acc: Any
    local_sem: Any
    feat_send: Any
    feat_recv: Any
    across_send: Any
    across_recv: Any
    near_send: Any
    near_recv: Any
    far_send: Any
    far_recv: Any
    out_sem: Any
    weight_sem: Any
    x_send: Any
    x_recv: Any
    gain_send: Any
    gain_recv: Any
    last_sem: Any
    first_sem: Any


def layer_kernel(jobs, bits, *refs):
    plan = jobs.plan
    inp = Inputs(*refs[: len(Inputs._fields)])
    refs = refs[len(Inputs._fields) :]
    outs = refs[: len(jobs.outs)]
    layer_out, token_grad, gains_out = refs[len(jobs.outs) : len(jobs.outs) + 3]
    refs = refs[len(jobs.outs) + 3 :]
    every, left, scr = refs[:5], refs[5:9], Scratch(*refs[9:])
    sent, came, total = scr.sent, scr.came, scr.total
    sent_late, came_late = scr.sent_late, scr.came_late
    local_sem, near_send, near_recv = scr.local_sem, scr.near_send, scr.near_recv
    tokens, width = scr.dy.shape
    own = tokens // 2
    rows = left[0].shape[0]
    half, quarter = rows // 2, rows // 4
    ring_total = total.shape[0]
    ring_sent = sent.shape[0]

    me = lax.axis_index("dp")
    rank = lax.axis_index("tensor")
    low, high = lax.rem(me, 4), lax.div(me, 4)
    bit = [lax.rem(lax.div(high, 2**s), 2) for s in range(bits)]
    mine = aligned(rank * own, own)

    partners = [1, 2, 3, 4, 5, 6, 7] + [8 << s for s in range(bits - 1)]
    barrier = pltpu.get_barrier_semaphore()
    for by in partners:
        pl.semaphore_signal(barrier, inc=1, device_id={"dp": flip(me, by)}, device_id_type=MESH)
    pl.semaphore_signal(barrier, inc=1, device_id={"tensor": 1 - rank}, device_id_type=MESH)
    pl.semaphore_wait(barrier, len(partners) + 1)

    def remote(src, dst, send, recv, by):
        return pltpu.make_async_remote_copy(
            src_ref=src,
            dst_ref=dst,
            send_sem=send,
            recv_sem=recv,
            device_id={"dp": flip(me, by)},
            device_id_type=MESH,
        )

    def x_copy(src, dst, i):
        return pltpu.make_async_remote_copy(
            src_ref=src,
            dst_ref=dst,
            send_sem=scr.x_send.at[i],
            recv_sem=scr.x_recv.at[i],
            device_id={"tensor": 1 - rank},
            device_id_type=MESH,
        )


    def slot(array, j, start, columns):
        return every[array].at[pl.ds(j * tokens, tokens), pl.ds(start, columns)]

    def near(t, j):
        array, _, start, columns, _ = plan[t]
        by = 4 if j == 4 else 2 if j in (2, 6) else 1
        src = slot(array, 8 if j == 4 else j - by, start, columns)
        dst = slot(array, j, start, columns)
        return remote(src, dst, near_send.at[t, j], near_recv.at[t, j], by)

    def stage_rows(s):
        return half - (half >> (s - 1)), quarter >> (s - 1)

    def far(t, s):
        columns = plan[t][3] * (2 if t < jobs.halved else 1)
        if s == 0:
            src, dst = sent.at[t % ring_sent], came.at[t % RING]
            at = (slice(None), pl.ds(0, columns))
        else:
            src, dst = sent_late.at[t % ring_sent], came_late.at[t % RING]
            at = (pl.ds(*stage_rows(s)), pl.ds(0, columns))
        return remote(
            src.at[at], dst.at[at], scr.far_send.at[t, s], scr.far_recv.at[t, s], 4 << s
        )

    def final_row():
        row = 0
        for s in range(2, bits):
            row = row + bit[s] * (quarter >> (s - 1))
        return row

    last_size = quarter >> (bits - 2)
    half_hidden = jobs.outs[0] // 2

    def outputs(t):
        copies = []
        done = 0
        if t < jobs.halved:
            _, _, start, columns, _ = plan[t]
            for i, side in enumerate((bit[0], 1 - bit[0])):
                src = scr.turned.at[jobs.turned.index(t) % 3].at[pl.ds(i * columns, columns), :]
                dst = outs[0].at[pl.ds(pl.multiple_of(side * half_hidden + start, LANES), columns), :]
                copies.append(pltpu.make_async_copy(src, dst, scr.out_sem.at[t, i]))
            return copies
        for i, (out, first, columns) in enumerate(plan[t][4]):
            if t in jobs.turned:
                src = scr.turned.at[jobs.turned.index(t) % 3].at[pl.ds(done, columns), :]
                dst = outs[out].at[pl.ds(first, columns), :]
                copies.append(pltpu.make_async_copy(src, dst, scr.out_sem.at[t, i]))
                continue
            copies.append(
                pltpu.make_async_copy(
                    total.at[t % ring_total].at[
                        aligned(final_row(), last_size), pl.ds(done, columns)
                    ],
                    outs[out].at[:, pl.ds(first, columns)],
                    scr.out_sem.at[t, i],
                )
            )
            done += columns
        return copies

    output_waited = set()

    def wait_outputs(t):
        if t >= 0 and t not in output_waited:
            output_waited.add(t)
            for copy in outputs(t):
                copy.wait()

    def wait_turned(t):
        index = jobs.turned.index(t)
        if index >= 3:
            wait_outputs(jobs.turned[index - 3])

    def tiles(t, body):
        start, columns = plan[t][2:4]
        if t < jobs.halved:
            start, columns = 0, 2 * columns

        @pl.loop(0, columns // TILE)
        def _(i):
            body(aligned(start + i * TILE, TILE), aligned(i * TILE, TILE))

    def dot(t, first, size, at):
        array, f = plan[t][:2]
        return jnp.dot(
            left[f][aligned(first, size), :], every[array][:, at], preferred_element_type=jnp.float32
        )

    def first_pass(t):
        if t >= ring_sent + jobs.halved:
            far(t - ring_sent, 0).wait_send()

        def body(at, to):
            out = dot(t, (1 - bit[0]) * half, half, at)
            sent[t % ring_sent, :, to] = out.astype(jnp.bfloat16)

        tiles(t, body)
        far(t, 0).start()

    def second_pass(t):
        far(t, 0).wait_recv()
        if t >= ring_sent:
            far(t - ring_sent, 1).wait_send()
        wait_outputs(t - ring_total)
        base = bit[0] * half

        def body(at, to):
            away, kept = (1 - bit[1]) * quarter, bit[1] * quarter
            out = dot(t, base + away, quarter, at)
            out = out + came[t % RING, aligned(away, quarter), to].astype(jnp.float32)
            sent_late[t % ring_sent, pl.ds(0, quarter), to] = out.astype(jnp.bfloat16)
            out = dot(t, base + kept, quarter, at)
            out = out + came[t % RING, aligned(kept, quarter), to].astype(jnp.float32)
            total[t % ring_total, :, to] = out

        tiles(t, body)
        far(t, 1).start()

    def later_pass(t, s):
        far(t, s - 1).wait_recv()
        if t >= ring_sent:
            far(t - ring_sent, s).wait_send()
        first, size = stage_rows(s - 1)
        piece = size // 2
        at_row = 0
        for q in range(2, s):
            at_row = at_row + bit[q] * (quarter >> (q - 1))
        away, kept = (1 - bit[s]) * piece, bit[s] * piece

        def body(at, to):
            out = total[t % ring_total, aligned(at_row + away, piece), to]
            out = out + came_late[t % RING, aligned(first + away, piece), to].astype(jnp.float32)
            sent_late[t % ring_sent, pl.ds(first + size, piece), to] = out.astype(jnp.bfloat16)
            row = aligned(at_row + kept, piece)
            out = total[t % ring_total, row, to]
            out = out + came_late[t % RING, aligned(first + kept, piece), to].astype(jnp.float32)
            total[t % ring_total, row, to] = out

        tiles(t, body)
        far(t, s).start()

    def last_pass(t):
        for s in range(2, bits):
            later_pass(t, s)
        far(t, bits - 1).wait_recv()
        first, size = stage_rows(bits - 1)
        if t in jobs.turned:
            wait_turned(t)

        def body(at, to):
            row = aligned(final_row(), last_size)
            out = total[t % ring_total, row, to]
            out = out + came_late[t % RING, pl.ds(first, size), to].astype(jnp.float32)
            if t in jobs.turned:
                scr.turned[jobs.turned.index(t) % 3, to, :] = out.T
            else:
                total[t % ring_total, row, to] = out

        tiles(t, body)
        for copy in outputs(t):
            copy.start()

    def halved_first(t):
        if t >= ring_sent:
            far(t - ring_sent, 1).wait_send()
        wait_outputs(t - ring_total)
        array, f, start, columns, _ = plan[t]

        @pl.loop(0, columns // LANES)
        def _(i):
            right = every[array][pl.ds(0, 8 * tokens), aligned(start + i * LANES, LANES)]
            for side in range(2):
                to = aligned(side * columns + i * LANES, LANES)
                out = jnp.dot(
                    left[f][pl.ds(side * half, half), :], right, preferred_element_type=jnp.float32
                )
                upper, lower = out[:quarter], out[quarter:]
                kept = lax.select(bit[1] == 0, upper, lower)
                away = lax.select(bit[1] == 0, lower, upper)
                total[t % ring_total, :, to] = kept
                sent_late[t % ring_sent, pl.ds(0, quarter), to] = away.astype(jnp.bfloat16)

        far(t, 1).start()

    def pair_copy(t):
        columns = pl.ds(0, plan[t][3])
        return remote(
            scr.pair_sent.at[t].at[:, columns],
            scr.pair_came.at[t].at[:, columns],
            scr.pair_send.at[t],
            scr.pair_recv.at[t],
            4,
        )

    def halved_sum(t):
        for s in range(2, bits):
            later_pass(t, s)
        far(t, bits - 1).wait_recv()
        columns = plan[t][3]
        first, size = stage_rows(bits - 1)
        row = aligned(final_row(), last_size)

        @pl.loop(0, columns // LANES)
        def _(i):
            for side in (bit[0], 1 - bit[0]):
                to = aligned(side * columns + i * LANES, LANES)
                out = total[t % ring_total, row, to]
                out = out + came_late[t % RING, pl.ds(first, size), to].astype(jnp.float32)
                total[t % ring_total, row, to] = out
            scr.pair_sent[t, :, aligned(i * LANES, LANES)] = out.astype(jnp.bfloat16)

        pair_copy(t).start()

    def halved_last(t):
        pair_copy(t).wait_recv()
        wait_turned(t)
        columns = plan[t][3]
        row = aligned(final_row(), last_size)

        @pl.loop(0, columns // LANES)
        def _(i):
            at = aligned(i * LANES, LANES)
            mine_at = aligned(bit[0] * columns + i * LANES, LANES)
            scr.turned[jobs.turned.index(t) % 3, at, :] = total[t % ring_total, row, mine_at].T
            theirs = scr.pair_came[t, :, at].astype(jnp.float32)
            scr.turned[jobs.turned.index(t) % 3, aligned(columns + i * LANES, LANES), :] = theirs.T

        for copy in outputs(t):
            copy.start()

    feature_waited = set()

    def begin(t):
        if t < jobs.halved:
            near(t, 4).start()
        near(t, 1).start()
        near(t, 2).start()

    def pass_on(t):
        near(t, 2).wait_recv()
        near(t, 3).start()

    def pass_pair(t):
        near(t, 4).wait_recv()
        near(t, 5).start()
        near(t, 6).start()

    def pass_again(t):
        near(t, 6).wait_recv()
        near(t, 7).start()

    def feature_slots(f):
        return range(1, 8 if f == 0 else 4)

    def first_product(t):
        f = plan[t][1]
        if f not in feature_waited:
            feature_waited.add(f)
            for j in feature_slots(f):
                if not (f in by_halves and j > 1):
                    feature_copy(f, j).wait_recv()
            if f in by_halves:
                for j in (2, 3):
                    feature_across(f, j).wait_recv()
        for j in (1, 3, 5, 7) if t < jobs.halved else (1, 3):
            near(t, j).wait_recv()
        if t < jobs.halved:
            halved_first(t)
        else:
            first_pass(t)

    def second(t):
        if t < jobs.halved:
            halved_sum(t)
        else:
            second_pass(t)

    def last(t):
        if t < jobs.halved:
            halved_last(t)
        else:
            last_pass(t)


    source_of = {0: 0, 3: 1, 1: 0, 2: 1}

    by_halves = (1, 2)

    def feature_across(f, j):
        at = left[f].at[:, aligned(j * tokens + rank * own, own)]
        return pltpu.make_async_remote_copy(
            src_ref=at,
            dst_ref=at,
            send_sem=scr.across_send.at[f, j],
            recv_sem=scr.across_recv.at[f, j],
            device_id={"tensor": 1 - rank},
            device_id_type=MESH,
        )

    def send_across(f):
        for j in (2, 3):
            feature_copy(f, j).wait_recv()
            feature_across(f, j).start()

    def feature_copy(f, j):
        src = scr.source.at[source_of[f], flip(low, j % 4)]
        dst = left[f].at[:, pl.ds(j * tokens, tokens)]
        if f in by_halves and j > 1:
            src = src.at[:, aligned(rank * own, own)]
            dst = left[f].at[:, aligned(j * tokens + rank * own, own)]
        return remote(
            src,
            dst,
            scr.feat_send.at[f, j],
            scr.feat_recv.at[f, j],
            j,
        )

    def turn(ref, f):
        count = 4 << bits
        block = width // count
        source = scr.source.at[source_of[f]]

        @pl.loop(0, width // LANES)
        def _(c):
            turned = ref[:, aligned(c * LANES, LANES)].T
            for piece in range(LANES // block):
                d = c * (LANES // block) + piece
                group = lax.div(d, 4)
                place = 0
                for s in range(bits):
                    place = place + lax.rem(lax.div(group, 2**s), 2) * 2 ** (bits - 1 - s)
                source[lax.rem(d, 4), aligned(place * block, block), :] = turned[
                    piece * block : (piece + 1) * block
                ]

        left[f][:, pl.ds(0, tokens)] = source[low]

    def send_features(f):
        for j in (6, 7, 2, 3, 4, 5, 1) if f == 0 else (2, 3, 1):
            feature_copy(f, j).start()


    weight_sem = scr.weight_sem

    def hidden_weights(i):
        at = lax.rem(i, 2)
        copies = []
        for side in range(2):
            columns = aligned(side * half_hidden + i * LANES, LANES)
            to = pl.ds(side * LANES, LANES)
            for k, (src, dst) in enumerate(
                (
                    (inp.w_gate.at[:, columns], scr.gate_w.at[at].at[:, to]),
                    (inp.w_up.at[:, columns], scr.up_w.at[at].at[:, to]),
                    (inp.w_down.at[columns, :], scr.down_w.at[at].at[to, :]),
                )
            ):
                copies.append(pltpu.make_async_copy(src, dst, weight_sem.at[k + 3 * side, at]))
        return copies

    hidden_tiles = jobs.outs[0] // TILE
    wide = 512

    def hidden_part(first, count):
        @pl.loop(first, first + count)
        def _(i):
            at = lax.rem(i, 2)

            @pl.when(i + 1 < hidden_tiles)
            def _():
                for copy in hidden_weights(i + 1):
                    copy.start()

            for copy in hidden_weights(i):
                copy.wait()
            gate_w, up_w, down_w = scr.gate_w.at[at], scr.up_w.at[at], scr.down_w.at[at]
            two = scr.two_full[...]
            gate = jnp.dot(two, gate_w[...], preferred_element_type=jnp.float32)
            up = jnp.dot(two, up_w[...], preferred_element_type=jnp.float32)
            d_act = against(scr.dy[...], down_w[...])
            sig = jax.nn.sigmoid(gate)
            silu = gate * sig
            act = (silu * up).astype(jnp.bfloat16)
            d_gate = (d_act * up * sig * (1.0 + gate * (1.0 - sig))).astype(jnp.bfloat16)
            d_up = (d_act * silu).astype(jnp.bfloat16)
            for side in range(2):
                part = slice(side * LANES, (side + 1) * LANES)
                away = bit[0] if side == 0 else 1 - bit[0]
                at_rows = aligned(away * 8 * tokens, tokens)
                every[0][at_rows, aligned(i * LANES, LANES)] = act[:, part]
                columns = aligned(side * half_hidden + i * LANES, LANES)
                every[1][pl.ds(0, tokens), columns] = d_gate[:, part]
                every[2][pl.ds(0, tokens), columns] = d_up[:, part]

            @pl.loop(0, width // wide)
            def _(n):
                part = aligned(n * wide, wide)
                scr.mlp_acc[:, part] += jnp.dot(
                    act, down_w[:, part], preferred_element_type=jnp.float32
                )
                scr.norm_acc[:, part] += against(d_gate, gate_w[part, :]) + against(
                    d_up, up_w[part, :]
                )

    def row_loop(body):
        @pl.loop(0, own // ROWS)
        def _(i):
            body(*[aligned(base + i * ROWS, ROWS) for base in (0, rank * own, (1 - rank) * own)])

    def eight(value):
        return jnp.sum(value.reshape(ROWS // 8, 8, width), axis=0)

    def send_partial(acc, buffer):
        @pl.loop(0, own // ROWS)
        def _(i):
            row = aligned((1 - rank) * own + i * ROWS, ROWS)
            scr.x_sent[buffer, aligned(i * ROWS, ROWS), :] = acc[row, :].astype(
                jnp.bfloat16
            )


    def out_weights(i):
        return pltpu.make_async_copy(
            inp.w_out.at[aligned(i * TILE, TILE), :],
            scr.down_w.at[lax.rem(i, 2)],
            weight_sem.at[2, lax.rem(i, 2)],
        )

    def query_buffer(j):
        return (scr.gate_w, scr.up_w)[j % 4 // 2].at[j % 2]

    def query_weights(j):
        dst, sem = query_buffer(j), weight_sem.at[j % 4 // 2, j % 2]
        if j < query_tiles:
            return [
                pltpu.make_async_copy(inp.w_query.at[:, pl.ds(j * TILE, TILE)], dst, sem)
            ]
        kv = inp.w_key.shape[1]
        return [
            pltpu.make_async_copy(inp.w_key, dst.at[:, pl.ds(0, kv)], sem),
            pltpu.make_async_copy(inp.w_value, dst.at[:, pl.ds(kv, kv)], scr.last_sem.at[2]),
        ]

    query_width = jobs.outs[3]
    kv_width = jobs.outs[5]
    query_tiles = query_width // TILE
    kv_heads = kv_width // HD
    pairs = query_width // LANES // kv_heads
    score_scale = HD ** (-0.5)

    def lane_masks():
        lane = lax.broadcasted_iota(jnp.int32, (1, LANES), 1)
        first = (lane < HD).astype(jnp.float32)
        return first, 1.0 - first

    def unrotate(value):
        lane = lax.broadcasted_iota(jnp.int32, value.shape, 1)
        other = jnp.where(
            lax.rem(lane, HD) < HD // 2,
            pltpu.roll(value, LANES - HD // 2, 1),
            pltpu.roll(value, HD // 2, 1),
        )
        return value * scr.cosine[...] + other * scr.sine[...]

    def d_attended():
        @pl.loop(0, query_tiles)
        def _(i):
            out_weights(i).wait()
            scr.d_att[:, aligned(i * TILE, TILE)] = against(
                scr.one_full[...], scr.down_w[lax.rem(i, 2)]
            ).astype(jnp.bfloat16)

            @pl.when(i + 2 < query_tiles)
            def _():
                out_weights(i + 2).start()

    def attend_back(kv):
        keys, values = scr.keys.at[kv], scr.values.at[kv]
        keys_acc, values_acc = scr.keys_acc.at[kv], scr.values_acc.at[kv]
        keys_acc[...] = jnp.zeros_like(keys_acc)
        values_acc[...] = jnp.zeros_like(values_acc)

        @pl.loop(0, pairs)
        def _(p):
            columns = aligned((kv * pairs + p) * LANES, LANES)
            d_query = jnp.zeros((tokens, LANES), jnp.float32)
            for lanes in lane_masks():
                lanes_low = lanes.astype(jnp.bfloat16)
                query = scr.query[:, columns] * lanes_low
                d_att = scr.d_att[:, columns] * lanes_low
                scores = against(query, keys[...]) * score_scale
                scores = jnp.where(scr.mask[...] > 0, scores, masked_score)
                expo = jnp.exp(scores - jnp.max(scores, axis=1, keepdims=True))
                probs = expo * (1.0 / jnp.sum(expo, axis=1, keepdims=True))
                d_probs = against(d_att, values[...])
                inner = jnp.sum(probs * d_probs, axis=1, keepdims=True)
                d_scores = (probs * (d_probs - inner)).astype(jnp.bfloat16)
                d_query = d_query + lanes * jnp.dot(
                    d_scores, keys[...], preferred_element_type=jnp.float32
                )
                keys_acc[...] += inner_rows(d_scores, query)
                values_acc[...] += inner_rows(probs.astype(jnp.bfloat16), d_att)
            every[4][pl.ds(0, tokens), columns] = unrotate(d_query * score_scale).astype(
                jnp.bfloat16
            )

    def finish_keys():
        lanes = lane_masks()
        d_key = jnp.zeros((tokens, LANES), jnp.float32)
        d_value = jnp.zeros((tokens, LANES), jnp.float32)
        for kv in range(kv_heads):
            for out in (0, 1):
                acc = (scr.keys_acc, scr.values_acc)[out][kv]
                acc = (acc + pltpu.roll(acc, HD, 1)) * lanes[kv]
                if out == 0:
                    d_key = d_key + acc
                else:
                    d_value = d_value + acc
        d_key = unrotate(d_key * score_scale)
        every[4][pl.ds(0, tokens), pl.ds(query_width, kv_width)] = d_key.astype(jnp.bfloat16)
        every[4][pl.ds(0, tokens), pl.ds(query_width + kv_width, kv_width)] = d_value.astype(
            jnp.bfloat16
        )

    def d_normed_one():
        for j in range(query_tiles + 1):
            for copy in query_weights(j):
                copy.wait()
            weights = query_buffer(j)
            grads = every[4][pl.ds(0, tokens), pl.ds(j * TILE, TILE)]

            @pl.loop(0, width // wide)
            def _(n):
                part = aligned(n * wide, wide)
                add = against(grads, weights[part, :])
                if j == 0:
                    scr.norm_acc[:, part] = add
                else:
                    scr.norm_acc[:, part] += add

            if j + 4 < query_tiles + 1:
                for copy in query_weights(j + 4):
                    copy.start()


    def mean_rows(value):
        return jnp.mean(value, axis=1, keepdims=True)

    def middle_back(row, full, other):
        grad = scr.norm_acc[full, :] + scr.x_came[0, row, :].astype(jnp.float32)
        middle = scr.middle[row, :]
        scale = lax.rsqrt(mean_rows(middle * middle) + norm_eps)
        normed = middle * scale
        scr.gain_part[0] += eight(grad * normed)
        scaled = grad * inp.mlp_gain[...]
        d_middle = scr.dy[full, :].astype(jnp.float32) + scale * (
            scaled - normed * mean_rows(scaled * normed)
        )
        scr.mlp_acc[other, :] = d_middle
        scr.one_full[full, :] = d_middle.astype(jnp.bfloat16)

    def finish_layer(row, full, other):
        mlp = scr.mlp_acc[full, :] + scr.x_came[1, row, :].astype(jnp.float32)
        scr.x_sent[1, row, :] = (scr.middle[row, :] + mlp).astype(jnp.bfloat16)

    def token_back(row, full, other):
        grad = scr.norm_acc[full, :] + scr.x_came[2, row, :].astype(jnp.float32)
        valid = scr.valid[full, :][:, :1]
        masked = scr.tok_full[full, :].astype(jnp.float32) * valid
        scale = lax.rsqrt(mean_rows(masked * masked) + norm_eps)
        normed = masked * scale
        scr.gain_part[1] += eight(grad * normed)
        scaled = grad * inp.attn_gain[...]
        out = scr.mlp_acc[other, :] + scale * (scaled - normed * mean_rows(scaled * normed))
        scr.x_sent[1, row, :] = (out * valid).astype(jnp.bfloat16)

    def gain_copy(i):
        src, dst = scr.gain_all.at[i], scr.gain_came.at[i]
        if i < bits + 2:
            return remote(src, dst, scr.gain_send.at[i], scr.gain_recv.at[i], 1 << i)
        return pltpu.make_async_remote_copy(
            src_ref=src,
            dst_ref=dst,
            send_sem=scr.gain_send.at[i],
            recv_sem=scr.gain_recv.at[i],
            device_id={"tensor": 1 - rank},
            device_id_type=MESH,
        )

    gain_steps = bits + 3

    def gain_next(i):
        gain_copy(i).wait_recv()
        scr.gain_all[i + 1] = scr.gain_all[i] + scr.gain_came[i]
        if i + 1 < gain_steps:
            gain_copy(i + 1).start()


    def prepare():
        ends = []
        for k in range(inp.lengths.shape[0]):
            ends.append(inp.lengths[k] + (ends[-1] if ends else 0))

        def segments(shape, axis):
            place = lax.broadcasted_iota(jnp.int32, shape, axis)
            return place, sum((place >= end).astype(jnp.int32) for end in ends)

        place, _ = segments((tokens, LANES), 0)
        start = jnp.zeros_like(place)
        for end in ends:
            start = jnp.maximum(start, jnp.where(place >= end, end, 0))
        scr.valid[...] = (place < ends[-1]).astype(jnp.float32)
        lane = lax.broadcasted_iota(jnp.int32, (tokens, LANES), 1)
        slow = lax.rem(lane, HD // 2).astype(jnp.float32)
        inverse = jnp.exp(slow * (-2.0 * math.log(10000.0) / HD))
        angles = (place - start).astype(jnp.float32) * inverse
        scr.cosine[...] = jnp.cos(angles)
        sine = jnp.sin(angles)
        scr.sine[...] = jnp.where(lax.rem(lane, HD) < HD // 2, sine, -sine)
        rows_at, row_segment = segments((tokens, tokens), 0)
        columns_at, column_segment = segments((tokens, tokens), 1)
        seen = (row_segment == column_segment) & (columns_at <= rows_at)
        scr.mask[...] = seen.astype(jnp.float32)


    def query_half(k):
        return every[2].at[pl.ds(0, width // 2), pl.ds(k * query_width, query_width)]

    def out_all():
        return every[1].at[pl.ds(0, query_width), pl.ds(0, width)]

    def forward_weights():
        dst = scr.gate_w.at[1]
        copies = [
            pltpu.make_async_copy(
                inp.w_query.at[pl.ds(k * width // 2, width // 2), :],
                query_half(k),
                scr.first_sem.at[k],
            )
            for k in range(2)
        ]
        for k, ref in ((0, inp.w_key), (1, inp.w_value)):
            copies.append(
                pltpu.make_async_copy(
                    ref, dst.at[:, pl.ds(k * kv_width, kv_width)], scr.first_sem.at[2 + k]
                )
            )
        copies.append(pltpu.make_async_copy(inp.w_out, out_all(), scr.first_sem.at[4]))
        return copies

    def all_rows(body):
        @pl.loop(0, tokens // ROWS)
        def _(i):
            body(aligned(i * ROWS, ROWS))

    def first_norm(row, full, other):
        one_rows(full)

    def first_norm_other(row, full, other):
        one_rows(other)

    def one_rows(full):
        masked = scr.tok_full[full, :].astype(jnp.float32) * scr.valid[full, :][:, :1]
        scale = lax.rsqrt(mean_rows(masked * masked) + norm_eps)
        scr.one_full[full, :] = (masked * scale * inp.attn_gain[...]).astype(jnp.bfloat16)

    def mask_cotangent(full):
        dy = scr.dy[full, :].astype(jnp.float32) * scr.valid[full, :][:, :1]
        scr.dy[full, :] = dy.astype(jnp.bfloat16)

    def rotated(value, row):
        lane = lax.broadcasted_iota(jnp.int32, value.shape, 1)
        other = jnp.where(
            lax.rem(lane, HD) < HD // 2,
            pltpu.roll(value, LANES - HD // 2, 1),
            pltpu.roll(value, HD // 2, 1),
        )
        return value * scr.cosine[row, :] - other * scr.sine[row, :]

    def projections(row):
        @pl.loop(0, query_tiles)
        def _(j):
            columns = aligned(j * TILE, TILE)
            out = jnp.dot(
                scr.one_full[row, : width // 2],
                query_half(0)[:, columns],
                preferred_element_type=jnp.float32,
            )
            out = out + jnp.dot(
                scr.one_full[row, width // 2 :],
                query_half(1)[:, columns],
                preferred_element_type=jnp.float32,
            )
            for k in range(TILE // LANES):
                part = rotated(out[:, k * LANES : (k + 1) * LANES], row)
                scr.query[row, aligned(j * TILE + k * LANES, LANES)] = part.astype(jnp.bfloat16)

        out = jnp.dot(scr.one_full[row, :], scr.gate_w[1], preferred_element_type=jnp.float32)
        lane = lax.broadcasted_iota(jnp.int32, (own, LANES), 1)
        for k, ref in ((0, scr.keys), (1, scr.values)):
            part = out[:, k * LANES : (k + 1) * LANES]
            part = rotated(part, row) if k == 0 else part
            part = part.astype(jnp.bfloat16).astype(jnp.float32)
            turned = pltpu.roll(part, HD, 1)
            ref[0, row, :] = jnp.where(lane < HD, part, turned).astype(jnp.bfloat16)
            ref[1, row, :] = jnp.where(lane < HD, turned, part).astype(jnp.bfloat16)

    def attend(row):
        for kv in range(kv_heads):

            @pl.loop(0, pairs)
            def _(p):
                columns = aligned((kv * pairs + p) * LANES, LANES)
                out = jnp.zeros((own, LANES), jnp.float32)
                for lanes in lane_masks():
                    query = scr.query[row, columns] * lanes.astype(jnp.bfloat16)
                    scores = against(query, scr.keys[kv]) * score_scale
                    scores = jnp.where(scr.mask[row, :] > 0, scores, masked_score)
                    expo = jnp.exp(scores - jnp.max(scores, axis=1, keepdims=True))
                    probs = expo * (1.0 / jnp.sum(expo, axis=1, keepdims=True))
                    out = out + lanes * jnp.dot(
                        probs.astype(jnp.bfloat16), scr.values[kv], preferred_element_type=jnp.float32
                    )
                every[3][row, columns] = out.astype(jnp.bfloat16)

    def out_rows(row, store):
        @pl.loop(0, width // wide)
        def _(n):
            part = aligned(n * wide, wide)
            store(
                part,
                jnp.dot(
                    every[3][row, :],
                    every[1][pl.ds(0, query_width), part],
                    preferred_element_type=jnp.float32,
                ),
            )

    def middle_forward(row, full, other):
        masked = scr.tok_full[full, :].astype(jnp.float32) * scr.valid[full, :][:, :1]
        middle = masked + (scr.norm_acc[row, :] + scr.x_came[0, row, :].astype(jnp.float32))
        scale = lax.rsqrt(mean_rows(middle * middle) + norm_eps)
        scr.middle[row, :] = middle
        scr.two_full[full, :] = (middle * scale * inp.mlp_gain[...]).astype(jnp.bfloat16)


    first_copies = [
        (x_copy(ref, full.at[mine, :], i), pltpu.make_async_copy(ref, full.at[mine, :], local_sem.at[i]))
        for i, (ref, full) in enumerate(((inp.tokens, scr.tok_full), (inp.cotangent, scr.dy)))
    ]
    for copy in first_copies[0]:
        copy.start()
    loads = forward_weights()
    for copy in loads:
        copy.start()
    first_copies[1][1].start()
    prepare()
    first_copies[0][1].wait()
    row_loop(first_norm)
    for copy in loads:
        copy.wait()
    projections(mine)
    theirs = aligned((1 - rank) * own, own)
    first_copies[0][0].wait_recv()
    first_copies[1][0].start()
    row_loop(first_norm_other)
    projections(theirs)
    turn(scr.one_full, 3)
    send_features(3)
    attend(theirs)

    def store_theirs(part, out):
        scr.x_sent[0, :, part] = out.astype(jnp.bfloat16)

    def store_mine(part, out):
        scr.norm_acc[pl.ds(0, own), part] = out

    out_rows(theirs, store_theirs)
    branch_copy = x_copy(scr.x_sent.at[0], scr.x_came.at[0], 2)
    branch_copy.start()
    first_copies[1][1].wait()
    first_copies[1][0].wait_recv()
    all_rows(mask_cotangent)
    turn(scr.dy, 0)
    send_features(0)
    attend(mine)
    for copy in hidden_weights(0):
        copy.start()
    out_rows(mine, store_mine)
    branch_copy.wait_recv()
    row_loop(middle_forward)
    two_copy = x_copy(scr.two_full.at[mine, :], scr.two_full.at[mine, :], 3)
    two_copy.start()
    scr.mlp_acc[...] = jnp.zeros_like(scr.mlp_acc)
    scr.norm_acc[...] = jnp.zeros_like(scr.norm_acc)
    scr.gain_part[...] = jnp.zeros_like(scr.gain_part)
    two_copy.wait_recv()
    norm_copy = x_copy(scr.x_sent.at[0], scr.x_came.at[0], 4)
    db_copy = x_copy(scr.one_full.at[mine, :], scr.one_full.at[mine, :], 5)
    mlp_copy = x_copy(scr.x_sent.at[1], scr.x_came.at[1], 6)
    one_copy = x_copy(scr.x_sent.at[0], scr.x_came.at[2], 7)
    layer_copy = pltpu.make_async_copy(scr.x_sent.at[1], layer_out, scr.last_sem.at[0])
    token_copy = pltpu.make_async_copy(scr.x_sent.at[1], token_grad, scr.last_sem.at[1])
    gains_copy = pltpu.make_async_copy(scr.gain_own, gains_out, local_sem.at[1])

    def send_norm():
        branch_copy.wait_send()
        send_partial(scr.norm_acc, 0)
        norm_copy.start()
        for i in range(2):
            out_weights(i).start()
        for j in range(4):
            for copy in query_weights(j):
                copy.start()

    def middle_grads():
        norm_copy.wait_recv()
        row_loop(middle_back)
        db_copy.start()

    def attended_grads():
        db_copy.wait_recv()
        mlp_copy.start()
        d_attended()

    def last_keys():
        attend_back(1)
        finish_keys()

    def layer_end():
        d_normed_one()
        norm_copy.wait_send()
        send_partial(scr.norm_acc, 0)
        one_copy.start()
        mlp_copy.wait_send()
        mlp_copy.wait_recv()
        row_loop(finish_layer)
        layer_copy.start()

    def token_end():
        layer_copy.wait()
        one_copy.wait_recv()
        row_loop(token_back)
        token_copy.start()
        gains = scr.gain_all.at[0]
        gains[...] = jnp.zeros_like(gains)
        for i in range(2):
            gains[pl.ds(i, 1), :] = jnp.sum(scr.gain_part[i], axis=0, keepdims=True)

    chain = {
        1: send_norm,
        2: lambda: send_partial(scr.mlp_acc, 1),
        3: middle_grads,
        4: attended_grads,
        5: lambda: attend_back(0),
        6: last_keys,
        7: layer_end,
        8: token_end,
    }

    def send(f):
        for j in feature_slots({1: 0, 2: 3}[f]):
            feature_copy({1: 0, 2: 3}[f], j).wait_send()
        turn({1: scr.two_full, 2: scr.one_full}[f], f)
        send_features(f)

    def gain(i):
        if i == 0:
            gain_copy(0).start()
        elif i < 5:
            gain_next(i - 1)
        else:
            for step in range(4, gain_steps):
                gain_next(step)
            gain_rows = width // (2 * (4 << bits))
            place = (2 * me + rank) * gain_rows
            block = scr.gain_all[gain_steps, :, aligned(lax.div(place, LANES) * LANES, LANES)]
            scr.gain_own[...] = pltpu.roll(block, lax.rem(LANES - lax.rem(place, LANES), LANES), 1)
            gains_copy.start()

    steps = {
        BEGIN: begin,
        PASS: pass_on,
        FIRST: first_product,
        SECOND: second,
        LAST: last,
        SEND: send,
        CHAIN: lambda i: chain[i](),
        GAIN: gain,
        PAIR: pass_pair,
        AGAIN: pass_again,
        ACROSS: send_across,
    }
    at = 0
    while at < len(ORDER):
        kind, number = ORDER[at] // 100 * 100, ORDER[at] % 100
        at += 1
        if kind == TILES:
            count = 1
            while at < len(ORDER) and ORDER[at] == number + count:
                count, at = count + 1, at + 1
            hidden_part(number, count)
        else:
            steps[kind](number)


    for copy, _ in first_copies:
        copy.wait_send()
    two_copy.wait_send()
    db_copy.wait_send()
    one_copy.wait_send()
    token_copy.wait()
    gains_copy.wait()
    for i in range(gain_steps):
        gain_copy(i).wait_send()
    for f in (1, 2):
        for j in (1, 2, 3):
            feature_copy(f, j).wait_send()
    for f in by_halves:
        for j in (2, 3):
            feature_across(f, j).wait_send()
    for t in range(len(plan)):
        for j in range(1, 8 if t < jobs.halved else 4):
            near(t, j).wait_send()
        if t < jobs.halved:
            pair_copy(t).wait_send()
        if t + ring_sent >= len(plan):
            for s in range(bits):
                far(t, s).wait_send()
        wait_outputs(t)


def layer_call(jobs, args, tokens, width):
    count = lax.axis_size("dp")
    bits = (count // 4).bit_length() - 1
    rows = width // 4
    block = width // count
    own = tokens // 2
    plan = jobs.plan
    vmem, any_space = pl.BlockSpec(memory_space=pltpu.VMEM), pl.BlockSpec(memory_space=pl.ANY)
    bf16, f32 = jnp.bfloat16, jnp.float32
    late_rows = rows // 2 - (rows // 2 >> (bits - 1))
    ring_total = max(4, bits + 1)
    kv_heads = jobs.outs[5] // HD
    dma = pltpu.SemaphoreType.DMA
    scratch = Scratch(
        tok_full=pltpu.VMEM((tokens, width), bf16),
        dy=pltpu.VMEM((tokens, width), bf16),
        one_full=pltpu.VMEM((tokens, width), bf16),
        middle=pltpu.VMEM((own, width), f32),
        query=pltpu.VMEM((tokens, jobs.outs[3]), bf16),
        keys=pltpu.VMEM((kv_heads, tokens, LANES), bf16),
        values=pltpu.VMEM((kv_heads, tokens, LANES), bf16),
        mask=pltpu.VMEM((tokens, tokens), f32),
        cosine=pltpu.VMEM((tokens, LANES), f32),
        sine=pltpu.VMEM((tokens, LANES), f32),
        valid=pltpu.VMEM((tokens, LANES), f32),
        source=pltpu.VMEM((2, 4, rows, tokens), bf16),
        sent=pltpu.VMEM((3, rows // 2, jobs.most), bf16),
        came=pltpu.VMEM((RING, rows // 2, jobs.most), bf16),
        sent_late=pltpu.VMEM((3, late_rows, jobs.most), bf16),
        came_late=pltpu.VMEM((RING, late_rows, jobs.most), bf16),
        total=pltpu.VMEM((ring_total, rows // 4, jobs.most), f32),
        turned=pltpu.VMEM((3, jobs.most, block), f32),
        gate_w=pltpu.VMEM((2, width, TILE), bf16),
        up_w=pltpu.VMEM((2, width, TILE), bf16),
        down_w=pltpu.VMEM((2, TILE, width), bf16),
        mlp_acc=pltpu.VMEM((tokens, width), f32),
        norm_acc=pltpu.VMEM((tokens, width), f32),
        two_full=pltpu.VMEM((tokens, width), bf16),
        x_came=pltpu.VMEM((3, own, width), bf16),
        x_sent=pltpu.VMEM((2, own, width), bf16),
        d_att=pltpu.VMEM((tokens, jobs.outs[3]), bf16),
        gain_part=pltpu.VMEM((2, 8, width), f32),
        gain_all=pltpu.VMEM((bits + 4, 8, width), f32),
        gain_came=pltpu.VMEM((bits + 3, 8, width), f32),
        gain_own=pltpu.VMEM((8, LANES), f32),
        pair_sent=pltpu.VMEM((jobs.halved, block, jobs.most_halved), bf16),
        pair_came=pltpu.VMEM((jobs.halved, block, jobs.most_halved), bf16),
        pair_send=dma((jobs.halved,)),
        pair_recv=dma((jobs.halved,)),
        keys_acc=pltpu.VMEM((kv_heads, tokens, LANES), f32),
        values_acc=pltpu.VMEM((kv_heads, tokens, LANES), f32),
        local_sem=dma((2,)),
        feat_send=dma((4, 8)),
        feat_recv=dma((4, 8)),
        across_send=dma((4, 4)),
        across_recv=dma((4, 4)),
        near_send=dma((len(plan), 8)),
        near_recv=dma((len(plan), 8)),
        far_send=dma((len(plan), bits)),
        far_recv=dma((len(plan), bits)),
        out_sem=dma((len(plan), jobs.pieces)),
        weight_sem=dma((6, 2)),
        x_send=dma((8,)),
        x_recv=dma((8,)),
        gain_send=dma((bits + 3,)),
        gain_recv=dma((bits + 3,)),
        last_sem=dma((3,)),
        first_sem=dma((5,)),
    )
    operands = [pltpu.VMEM((9 * tokens, jobs.widths[0] // 2), bf16)]
    operands += [pltpu.VMEM((4 * tokens, w), bf16) for w in jobs.widths[1:]]
    operands += [pltpu.VMEM((rows, 8 * tokens), bf16)] + [pltpu.VMEM((rows, 4 * tokens), bf16)] * 3
    return pl.pallas_call(
        functools.partial(layer_kernel, jobs, bits),
        out_shape=[
            jax.ShapeDtypeStruct((w, block) if i in (0, 3) else (block, w), f32)
            for i, w in enumerate(jobs.outs)
        ]
        + [
            jax.ShapeDtypeStruct((own, width), bf16),
            jax.ShapeDtypeStruct((own, width), bf16),
            jax.ShapeDtypeStruct((8, LANES), f32),
        ],
        in_specs=[pl.BlockSpec(memory_space=pltpu.SMEM), vmem, vmem] + [any_space] * (len(args) - 3),
        out_specs=[any_space] * (len(jobs.outs) + 3),
        scratch_shapes=operands + list(scratch),
        compiler_params=pltpu.CompilerParams(
            collective_id=0, has_side_effects=True, vmem_limit_bytes=63 * 1024 * 1024
        ),
    )(*args)


PIECES = 2


def hand_over_kernel(count, gain_rows, *refs):
    gains, refs = refs[0], refs[1:]
    inputs, outs = refs[:count], refs[count : 2 * count]
    attn_out, mlp_out = refs[2 * count : 2 * count + 2]
    held = refs[2 * count + 2 : 3 * count + 2]
    in_sem, out_sem = refs[3 * count + 2 :]
    pairs = []
    for i in range(count):
        rows = inputs[i].shape[0] // PIECES
        for piece in range(PIECES):
            at = pl.ds(piece * rows, rows)
            pairs.append(
                (
                    pltpu.make_async_copy(inputs[i].at[at], held[i].at[at], in_sem.at[i, piece]),
                    pltpu.make_async_copy(held[i].at[at], outs[i].at[at], out_sem.at[i, piece]),
                )
            )
    for copy, _ in pairs:
        copy.start()
    mlp_out[...] = gains[0:1, :gain_rows]
    attn_out[...] = gains[1:2, :gain_rows]
    for come, go in pairs:
        come.wait()
        go.start()
    for _, copy in pairs:
        copy.wait()


def hand_over(arrays, gains, gain_rows):
    any_space, vmem = pl.BlockSpec(memory_space=pl.ANY), pl.BlockSpec(memory_space=pltpu.VMEM)
    gain = jax.ShapeDtypeStruct((1, gain_rows), jnp.float32)
    return pl.pallas_call(
        functools.partial(hand_over_kernel, len(arrays), gain_rows),
        out_shape=[jax.ShapeDtypeStruct(x.shape, x.dtype) for x in arrays] + [gain, gain],
        in_specs=[vmem] + [any_space] * len(arrays),
        out_specs=[any_space] * len(arrays) + [vmem, vmem],
        scratch_shapes=[pltpu.VMEM(x.shape, x.dtype) for x in arrays]
        + [pltpu.SemaphoreType.DMA((len(arrays), PIECES))] * 2,
    )(gains, *arrays)


def on_device(
    tokens,
    frag_lengths,
    attn_gain,
    w_query,
    w_key,
    w_value,
    w_out,
    mlp_gain,
    w_gate,
    w_up,
    w_down,
    out_cotangent,
):
    tok_rows, model_width = tokens.shape
    pack_rows = tok_rows * lax.axis_size("tensor")
    rank = lax.axis_index("tensor")
    jobs = Jobs(w_gate.shape[1], w_query.shape[1], w_key.shape[1])
    args = Inputs(
        lengths=frag_lengths,
        attn_gain=attn_gain[None, :],
        mlp_gain=mlp_gain[None, :],
        tokens=tokens,
        cotangent=out_cotangent,
        w_query=w_query,
        w_key=w_key,
        w_value=w_value,
        w_out=w_out,
        w_gate=w_gate,
        w_up=w_up,
        w_down=w_down,
    )
    out = layer_call(jobs, args, pack_rows, model_width)
    gain_rows = model_width // (lax.axis_size("tensor") * lax.axis_size("dp"))
    out = hand_over(out[:-1], out[-1], gain_rows)
    g_down, g_gate, g_up, g_out, g_query, g_key, g_value, layer_out, token_grad = out[:9]
    return (
        layer_out,
        token_grad,
        out[9][0],
        g_query,
        g_key,
        g_value,
        g_out,
        out[10][0],
        g_gate,
        g_up,
        g_down,
    )


def solution(mesh):
    placed = (
        P(("dp", "tensor"), None),
        P("dp"),
        P(),
        P(None, "tensor"),
        P(None, "tensor"),
        P(None, "tensor"),
        P("tensor", None),
        P(),
        P(None, "tensor"),
        P(None, "tensor"),
        P("tensor", None),
        P(("dp", "tensor"), None),
    )
    return jax.shard_map(
        on_device,
        mesh=mesh,
        in_specs=placed,
        out_specs=(
            P(("dp", "tensor"), None),
            P(("dp", "tensor"), None),
            P(("dp", "tensor")),
            P("dp", "tensor"),
            P("dp", "tensor"),
            P("dp", "tensor"),
            P("tensor", "dp"),
            P(("dp", "tensor")),
            P("dp", "tensor"),
            P("dp", "tensor"),
            P("tensor", "dp"),
        ),
        check_vma=False,
    )
```
